32 devices in a mesh: grp: 2 (over x), xp: 8 (over z, y), yp: 2 (over core).
Axes of the slice: x: 2, y: 2, z: 4, core: 2. Of those that a mesh axis runs over, the one named last changes fastest.
Arguments:
- features: bfloat16 [64, 30, 512], P(('grp', 'xp', 'yp')), parts along dimension 0, may hold values from -6 to 6
- cotangent: bfloat16 [64, 30, 512], P(('grp', 'xp', 'yp')), parts along dimension 0, may hold values from -6 to 6
- w_first: bfloat16 [27, 84], replicated, may hold values from -0.4375 to 0.4375
- w_second: bfloat16 [27, 84], replicated, may hold values from -0.4375 to 0.4375
- neighbours: int32 [64, 27], P(('grp', 'xp', 'yp')), parts along dimension 0, may hold values from 0 to 18, as said below
- mirror: int32 [64, 3], P(('grp', 'xp', 'yp')), parts along dimension 0, may hold values from 0 to 1, as said below
Outputs:
- denoised: bfloat16 [64, 30, 512], P(('grp', 'xp', 'yp')), parts along dimension 0
- grad_first: float32 [54, 84], P('grp'), parts along dimension 0
- grad_second: float32 [54, 84], P('grp'), parts along dimension 0
The draws below stay inside these ranges and needn't reach their ends.
There are 2 independent parts, one for each index of `grp`. The reference program is written for one: setup_inputs(seed, part) draws one part's arguments, and reference() takes and returns one part's arrays. A program takes and returns all parts, laid end to end along the dimension named above; an argument that names none is the same for every part. Nothing has to cross between parts.
Inputs may be any that keep to these rules, and one draw needn't show every extreme that they name: Occupancy is symmetric under the three half-turns about the map's centre axes. neighbours[n, o] is the code of the brick at brick position + shift(o) as defined in the reference program, or 18 where that position is outside the map or empty. mirror[n, r] is the slot on the image pencil of the image of brick n under half-turn r.
All inputs are finite; a program needn't handle non-finite values.
Results may differ from the reference program's by a relative error of at most 0.0056.
Values may be sent and summed in bfloat16 or wider, within the bound.
No kernel may reach another device: no remote copies, remote signals or barrier semaphores. Data moves between devices by JAX's collectives and lax.ppermute only.
A program may use at most 192 MiB of HBM per device.

```python
import jax
import jax.numpy as jnp
from jax import lax

SCALARS = 8
COMPS = 30
VOXELS = 512
OFFSETS = 27
WCOLS = 84
BRICKS = 2
GX = 2
GY = 4
GZ = 2
NBRICK = 32
N_XP = 8
N_YP = 2


def brick_layout(key):
    key = jax.random.fold_in(key, 11)
    devices = N_XP * N_YP
    positions = GX * GY * GZ
    half_y = N_YP // 2
    representatives = N_XP // 2 * half_y
    keys = jax.random.split(key, representatives + devices)
    chosen = jax.vmap(lambda k: jax.random.permutation(k, positions)[:BRICKS])(keys[:representatives])
    orders = jax.vmap(lambda k: jax.random.permutation(k, BRICKS))(keys[representatives:])
    rep_x = jnp.arange(representatives) // half_y
    rep_y = jnp.arange(representatives) % half_y
    local_x = chosen // (GY * GZ)
    local_y = chosen // GZ % GY
    local_z = chosen % GZ
    occupancy = jnp.full((GX * N_XP, GY * N_YP, GZ), -1, jnp.int32)
    places = jnp.zeros((devices, BRICKS, 3), jnp.int32)
    for turn_x in (0, 1):
        for turn_y in (0, 1):
            owner_x = N_XP - 1 - rep_x if turn_x else rep_x
            owner_y = N_YP - 1 - rep_y if turn_y else rep_y
            owner = owner_x * N_YP + owner_y
            spot_x = GX - 1 - local_x if turn_x else local_x
            spot_y = GY - 1 - local_y if turn_y else local_y
            spot_z = GZ - 1 - local_z if turn_x != turn_y else local_z
            global_x = owner_x[:, None] * GX + spot_x
            global_y = owner_y[:, None] * GY + spot_y
            slots = orders[owner]
            occupancy = occupancy.at[global_x, global_y, spot_z].set(slots)
            places = places.at[owner[:, None], slots].set(jnp.stack([global_x, global_y, spot_z], axis=-1))
    return (occupancy, places)


def draw_neighbours(key, part):
    occupancy, places = brick_layout(key)
    devices = N_XP * N_YP
    device = jnp.arange(devices)
    pencil_x = (device // N_YP)[:, None]
    pencil_y = (device % N_YP)[:, None]
    codes = []
    for a in range(3):
        for b in range(3):
            for c in range(3):
                near_x = places[:, :, 0] + a - 1
                near_y = places[:, :, 1] + b - 1
                near_z = places[:, :, 2] + c - 1
                inside = (near_x >= 0) & (near_x < GX * N_XP) & (near_y >= 0) & (near_y < GY * N_YP) & (near_z >= 0) & (near_z < GZ)
                clip_x = jnp.clip(near_x, 0, GX * N_XP - 1)
                clip_y = jnp.clip(near_y, 0, GY * N_YP - 1)
                clip_z = jnp.clip(near_z, 0, GZ - 1)
                slots = occupancy[clip_x, clip_y, clip_z]
                owner = (clip_x // GX - pencil_x + 1) * 3 + (clip_y // GY - pencil_y + 1)
                codes.append(jnp.where(inside & (slots >= 0), owner * BRICKS + slots, 9 * BRICKS))
    return jnp.stack(codes, axis=-1).reshape(devices * BRICKS, 27).astype(jnp.int32)


def draw_mirror(key, part):
    occupancy, places = brick_layout(key)
    devices = N_XP * N_YP
    global_x = places[:, :, 0]
    global_y = places[:, :, 1]
    global_z = places[:, :, 2]
    far_x = GX * N_XP - 1 - global_x
    far_y = GY * N_YP - 1 - global_y
    far_z = GZ - 1 - global_z
    turn_first = occupancy[global_x, far_y, far_z]
    turn_second = occupancy[far_x, global_y, far_z]
    turn_third = occupancy[far_x, far_y, global_z]
    return jnp.stack([turn_first, turn_second, turn_third], axis=-1).reshape(devices * BRICKS, 3).astype(jnp.int32)


def steps_of(key, shape, shards, low, top_value):
    def one(dim, shards_of):
        steps = jax.random.uniform(jax.random.fold_in(jax.random.fold_in(key, 6), dim), (shards_of,), jnp.float32, low / len(shards), top_value / len(shards))
        return jnp.repeat(jnp.exp(steps), shape[dim] // shards_of).reshape((-1,) + (1,) * (len(shape) - dim - 1))

    loudness = one(*shards[0])
    for cut in shards[1:]:
        loudness = loudness * one(*cut)
    return loudness


def normal_values(stream_key, shape, deviation, bound, cuts=(), kind=jnp.bfloat16):
    values = jax.random.normal(stream_key, shape, jnp.float32) * deviation
    if len(cuts) > 0:
        values = steps_of(stream_key, shape, cuts, -0.22, 0.18) * values
    return jnp.clip(values, min=-bound, max=bound).astype(kind)


def setup_inputs(seed: int = 0, part: int = 0) -> dict:
    key_of = jax.random.split(jax.random.key(seed), 7)
    own_keys = jax.random.split(jax.random.fold_in(key_of[6], part), 7)
    features = normal_values(own_keys[0], (NBRICK, COMPS, VOXELS), 1.0, 6.0, ((0, 16),))
    cotangent = normal_values(own_keys[1], (NBRICK, COMPS, VOXELS), 1.0, 6.0, ((0, 16),))
    w_first = normal_values(key_of[2], (OFFSETS, WCOLS), (OFFSETS * SCALARS) ** -0.5, 0.4375)
    w_second = normal_values(key_of[3], (OFFSETS, WCOLS), (OFFSETS * SCALARS) ** -0.5, 0.4375)
    neighbours = draw_neighbours(jax.random.fold_in(jax.random.fold_in(key_of[6], part), 71), part)
    mirror = draw_mirror(jax.random.fold_in(jax.random.fold_in(key_of[6], part), 71), part)
    return {"features": features, "cotangent": cotangent, "w_first": w_first, "w_second": w_second, "neighbours": neighbours, "mirror": mirror}


flip_sets = ((3, 4), (2, 4), (2, 3))

def rim_slice(index_value):
    return (slice(7, 8), slice(0, 8), slice(0, 1))[index_value]

def assemble(brick_table, rows):
    planes = []
    for a in range(3):
        stripes = []
        for b in range(3):
            pieces = []
            for c in range(3):
                rim = brick_table[:, :, rim_slice(a), rim_slice(b), rim_slice(c)]
                pieces.append(jnp.take(rim, rows[:, a * 9 + b * 3 + c], axis=0))
            stripes.append(jnp.concatenate(pieces, axis=4))
        planes.append(jnp.concatenate(stripes, axis=3))
    return jnp.concatenate(planes, axis=2)

def shifted(padded, a, b, c):
    return padded[:, :, a:a + 8, b:b + 8, c:c + 8].reshape(padded.shape[0], 30, 512)

def split_weights(weights):
    scalar_w = weights[:, :64].reshape(27, 8, 8).astype(jnp.float32)
    vector_w = weights[:, 64:80].reshape(27, 4, 4).astype(jnp.float32)
    tensor_w = weights[:, 80:84].reshape(27, 2, 2).astype(jnp.float32) * 2.0
    return (scalar_w, vector_w, tensor_w)

def combine(parts, offset, source, transpose):
    scalar_w, vector_w, tensor_w = parts
    count = source.shape[0]
    values = source.astype(jnp.float32)
    flat_form = 'ji,njp->nip' if transpose else 'ij,njp->nip'
    comp_form = 'ji,nmjp->nmip' if transpose else 'ij,nmjp->nmip'
    scalar_out = jnp.einsum(flat_form, scalar_w[offset], values[:, :8])
    vector_out = jnp.einsum(comp_form, vector_w[offset], values[:, 8:20].reshape(count, 3, 4, 512))
    tensor_out = jnp.einsum(comp_form, tensor_w[offset], values[:, 20:].reshape(count, 5, 2, 512))
    return jnp.concatenate([scalar_out, vector_out.reshape(count, 12, 512), tensor_out.reshape(count, 10, 512)], axis=1)

def convolve(padded, parts, transpose):
    total = jnp.zeros((padded.shape[0], 30, 512), jnp.float32)
    for a in range(3):
        for b in range(3):
            for c in range(3):
                if transpose:
                    source = shifted(padded, 2 - a, 2 - b, 2 - c)
                else:
                    source = shifted(padded, a, b, c)
                total = total + combine(parts, a * 9 + b * 3 + c, source, transpose)
    return total

def weight_grad(grad, padded):
    count = grad.shape[0]
    values = grad.astype(jnp.float32)
    rows_out = []
    for a in range(3):
        for b in range(3):
            for c in range(3):
                source = shifted(padded, a, b, c).astype(jnp.float32)
                scalar_g = jnp.einsum('nip,njp->ij', values[:, :8], source[:, :8])
                vector_g = jnp.einsum('nmip,nmjp->ij', values[:, 8:20].reshape(count, 3, 4, 512), source[:, 8:20].reshape(count, 3, 4, 512))
                tensor_g = jnp.einsum('nmip,nmjp->ij', values[:, 20:].reshape(count, 5, 2, 512), source[:, 20:].reshape(count, 5, 2, 512)) * 2.0
                rows_out.append(jnp.concatenate([scalar_g.reshape(64), vector_g.reshape(16), tensor_g.reshape(4)]))
    return jnp.stack(rows_out)

def gate(pre):
    count = pre.shape[0]
    scalar_pre = pre[:, :8]
    sigmas = jax.nn.sigmoid(scalar_pre)
    vector_out = pre[:, 8:20].reshape(count, 3, 4, 512) * sigmas[:, None, :4]
    tensor_out = pre[:, 20:].reshape(count, 5, 2, 512) * sigmas[:, None, 4:6]
    return jnp.concatenate([jax.nn.silu(scalar_pre), vector_out.reshape(count, 12, 512), tensor_out.reshape(count, 10, 512)], axis=1)

def gate_backward(pre, grad):
    count = pre.shape[0]
    scalar_pre = pre[:, :8]
    sigmas = jax.nn.sigmoid(scalar_pre)
    vector_pre = pre[:, 8:20].reshape(count, 3, 4, 512)
    tensor_pre = pre[:, 20:].reshape(count, 5, 2, 512)
    vector_grad = grad[:, 8:20].reshape(count, 3, 4, 512)
    tensor_grad = grad[:, 20:].reshape(count, 5, 2, 512)
    slope = sigmas * (1.0 + scalar_pre * (1.0 - sigmas))
    bend = sigmas * (1.0 - sigmas)
    vector_gate = lax.optimization_barrier(jnp.sum(vector_grad * vector_pre, axis=1)) * bend[:, :4]
    tensor_gate = lax.optimization_barrier(jnp.sum(tensor_grad * tensor_pre, axis=1)) * bend[:, 4:6]
    extra = jnp.concatenate([vector_gate, tensor_gate, jnp.zeros((count, 2, 512), jnp.float32)], axis=1)
    scalar_grad = grad[:, :8] * slope + extra
    vector_out = vector_grad * sigmas[:, None, :4]
    tensor_out = tensor_grad * sigmas[:, None, 4:6]
    return jnp.concatenate([scalar_grad, vector_out.reshape(count, 12, 512), tensor_out.reshape(count, 10, 512)], axis=1)

def sign_table(which_turn):
    vector_signs = ((1.0, -1.0, -1.0), (-1.0, 1.0, -1.0), (-1.0, -1.0, 1.0))[which_turn]
    tensor_signs = ((-1.0, -1.0, 1.0, 1.0, 1.0), (-1.0, 1.0, -1.0, 1.0, 1.0), (1.0, -1.0, -1.0, 1.0, 1.0))[which_turn]
    values = [1.0] * 8 + [vector_signs[m] for m in range(3) for k in range(4)] + [tensor_signs[m] for m in range(5) for k in range(2)]
    return jnp.array(values, jnp.float32)

def rotate(source, rows, which_turn):
    moved = jnp.take(source, rows, axis=0).astype(jnp.float32).reshape(-1, 30, 8, 8, 8)
    moved = jnp.flip(moved, flip_sets[which_turn]) * sign_table(which_turn)[:, None, None, None]
    return moved.reshape(-1, 30, 512)

def symmetrize(source, partners):
    total = source.astype(jnp.float32)
    for which_turn in range(3):
        total = total + rotate(source, partners[:, which_turn], which_turn)
    return total * 0.25

def reference(features, cotangent, w_first, w_second, neighbours, mirror):
    count = features.shape[0]
    brick_ids = jnp.arange(count, dtype=jnp.int32)
    device = brick_ids // BRICKS
    pencil_x = (device // N_YP)[:, None]
    pencil_y = (device % N_YP)[:, None]
    empty = neighbours >= 9 * BRICKS
    direction = neighbours // BRICKS
    step_x = direction // 3 - 1
    step_y = direction % 3 - 1
    rows = ((pencil_x + step_x) * N_YP + (pencil_y + step_y)) * BRICKS + neighbours % BRICKS
    rows = jnp.where(empty, count, rows).astype(jnp.int32)
    px = device // N_YP
    py = device % N_YP
    partner_dev = jnp.stack([px * N_YP + (N_YP - 1 - py), (N_XP - 1 - px) * N_YP + py, (N_XP - 1 - px) * N_YP + (N_YP - 1 - py)], axis=1)
    partners = (partner_dev * BRICKS + mirror).astype(jnp.int32)
    zero_brick = jnp.zeros((1, 30, 8, 8, 8), jnp.bfloat16)

    def padded_of(field):
        brick_table = jnp.concatenate([field.reshape(count, 30, 8, 8, 8), zero_brick], axis=0)
        return assemble(brick_table, rows)
    first_parts = split_weights(w_first)
    second_parts = split_weights(w_second)
    padded_in = padded_of(features)
    pre = convolve(padded_in, first_parts, False)
    hidden = gate(pre).astype(jnp.bfloat16)
    padded_hidden = padded_of(hidden)
    second = convolve(padded_hidden, second_parts, False).astype(jnp.bfloat16)
    denoised = symmetrize(second, partners).astype(jnp.bfloat16)
    back = symmetrize(cotangent, partners).astype(jnp.bfloat16)
    back_hidden = convolve(padded_of(back), second_parts, True)
    back_pre = gate_backward(pre, back_hidden).astype(jnp.bfloat16)
    grad_second = weight_grad(back, padded_hidden) / count
    grad_first = weight_grad(back_pre, padded_in) / count
    return (denoised, grad_first, grad_second)
```

```python
import functools

import jax
import jax.numpy as jnp
import numpy as np
from jax import lax
from jax.experimental import pallas as pl
from jax.experimental.pallas import tpu as pltpu
from jax.sharding import PartitionSpec as P

BF = jnp.bfloat16
F32 = jnp.float32
CH = 32
LANES = 128
BOTH = ("xp", "yp")
HIGHEST = lax.Precision.HIGHEST


def component_tables():
    kind, comp, chan = np.full(CH, -1), np.full(CH, -1), np.full(CH, -1)
    for i in range(30):
        if i < 8:
            kind[i], comp[i], chan[i] = 0, 0, i
        elif i < 20:
            kind[i], comp[i], chan[i] = 1, (i - 8) // 4, (i - 8) % 4
        else:
            kind[i], comp[i], chan[i] = 2, (i - 20) // 2, (i - 20) % 2
    return kind, comp, chan


KIND, COMP, CHAN = component_tables()
WIDTH = (8, 4, 2)
START = (0, 64, 80)


def column(i, j):
    if KIND[i] < 0 or KIND[i] != KIND[j] or COMP[i] != COMP[j]:
        return None
    return START[KIND[i]] + CHAN[i] * WIDTH[KIND[i]] + CHAN[j]


def gate_of(i):
    if KIND[i] == 1:
        return CHAN[i]
    if KIND[i] == 2:
        return 4 + CHAN[i]
    return i


def expansions():
    direct = np.zeros((84, CH, CH), np.float32)
    gates = np.zeros((84, CH, CH), np.float32)
    turned = np.zeros((84, CH, CH), np.float32)
    for i in range(30):
        for j in range(30):
            c = column(i, j)
            if c is not None:
                value = 2.0 if KIND[i] == 2 else 1.0
                direct[c, i, j] = value
                turned[c, j, i] = value
            c = column(gate_of(i), j)
            if c is not None:
                gates[c, i, j] = 1.0
    return direct, gates, turned


def lane_of(y, z):
    return 10 * (y + 1) + z + 1


def spread_table():
    table = np.zeros((128, 256), np.float32)
    for p in range(2):
        for y in range(8):
            for z in range(8):
                table[p * 64 + y * 8 + z, p * 128 + lane_of(y, z)] = 1.0
    return table


def turns_table():
    table = np.zeros((4, 128, 128), np.float32)
    for p in range(2):
        for y in range(8):
            for z in range(8):
                to = p * 64 + y * 8 + z
                table[0, p * 64 + y * 8 + z, to] = 1.0
                table[1, p * 64 + (7 - y) * 8 + 7 - z, to] = 1.0
                table[2, (1 - p) * 64 + y * 8 + 7 - z, to] = 1.0
                table[3, (1 - p) * 64 + (7 - y) * 8 + z, to] = 1.0
    return table.reshape(512, 128)


def region_masks():
    masks = np.zeros((9, 128), np.float32)
    for row in range(10):
        for col in range(10):
            b = 0 if row == 0 else 2 if row == 9 else 1
            c = 0 if col == 0 else 2 if col == 9 else 1
            masks[b * 3 + c, 10 * row + col] = 1.0
    return masks


def turn_signs():
    signs = np.zeros((4, CH), np.float32)
    vector = ((1, 1, 1), (1, -1, -1), (-1, 1, -1), (-1, -1, 1))
    tensor = ((1, 1, 1, 1, 1), (-1, -1, 1, 1, 1), (-1, 1, -1, 1, 1), (1, -1, -1, 1, 1))
    for r in range(4):
        for i in range(30):
            signs[r, i] = 1.0 if KIND[i] == 0 else (vector[r] if KIND[i] == 1 else tensor[r])[COMP[i]]
    return signs


def gradient_tables():
    blocks = np.zeros((CH, CH), np.float32)
    place = np.zeros((CH, LANES), np.float32)
    keep = np.zeros((CH, LANES), np.float32)
    for i in range(30):
        for j in range(30):
            c = column(i, j)
            if c is not None:
                blocks[j, i] = 1.0
                place[i, c] = 2.0 if KIND[i] == 2 else 1.0
                keep[j, c] = 1.0
    return (
        np.tile(blocks, (9, 3)),
        np.kron(np.eye(3, dtype=np.float32), place),
        np.tile(keep, (9, 3)),
    )


def gather_rows():
    table = np.zeros((8, CH), np.float32)
    for i in range(30):
        table[gate_of(i), i] = 1.0
    return table


def dot(a, b, **kw):
    return jnp.dot(a, b, preferred_element_type=F32, **kw)


def stage_table(mid, low, high, own, part, near_low, far_low, near_high, far_high):
    zero = jnp.zeros((CH, LANES), BF)
    for s in range(2):
        for x in range(8):
            mid[s, x] = own(s, x)
            mid[2 + s, x] = part(s, x)
        low[s] = own(s, 7)
        low[2 + s] = part(s, 7)
        low[4 + s] = near_low(s)
        low[6 + s] = far_low(s)
        high[s] = own(s, 0)
        high[2 + s] = part(s, 0)
        high[4 + s] = near_high(s)
        high[6 + s] = far_high(s)
    for x in range(8):
        mid[4, x] = zero
    low[8] = zero
    high[8] = zero


def padded_brick(codes, n, mid, low, high, masks):
    def row(o, last):
        e = codes[n, o]
        d = lax.shift_right_logical(e, 1)
        s = lax.bitwise_and(e, 1)
        dx = lax.div(d, 3)
        other_y = jnp.where(d - 3 * dx == 1, 0, 2)
        other_x = jnp.where(dx == 1, 0, 4)
        return jnp.where(e >= 18, last, jnp.minimum(other_x + other_y + s, last))

    total = None
    for b in range(3):
        for c in range(3):
            o = 3 * b + c
            planes = jnp.concatenate(
                [low[row(o, 8)], mid[row(9 + o, 4)].reshape(8 * CH, LANES), high[row(18 + o, 8)]], axis=0
            )
            shift = ((b - 1) * 80 + (c - 1) * 8) % LANES
            if shift:
                planes = pltpu.roll(planes, shift, 1)
            planes = planes * masks[o : o + 1, :]
            total = planes if total is None else total + planes
    return total


def unfold(planes, columns, n):
    for o in range(9):
        shift = (11 - 10 * (o // 3) - o % 3) % LANES
        moved = pltpu.roll(planes, shift, 1) if shift else planes
        for p in range(10):
            columns[o * CH : (o + 1) * CH, (n * 10 + p) * LANES : (n * 10 + p + 1) * LANES] = moved[
                p * CH : (p + 1) * CH
            ]


def fold(stacked, row):
    return (
        stacked[row : row + CH, 0:1024]
        + stacked[row + CH : row + 2 * CH, LANES : LANES + 1024]
        + stacked[row + 2 * CH : row + 3 * CH, 2 * LANES : 2 * LANES + 1024]
    )


def columns_of(columns, n):
    return columns[:, n * 1280 : (n + 1) * 1280]


def symmetrized(sources, signs, slots, table, k, staged):
    parts = [staged[r, :, 128 * (k if r < 2 else 3 - k) : 128 * (k if r < 2 else 3 - k) + 128] for r in range(4)]
    return dot(jnp.concatenate(parts, axis=1), table[...]) * 0.25


def stage_turns(staged, sources, signs, mirror):
    own, across_y, across_x, across = sources
    for n in range(2):
        staged[0, n * CH : (n + 1) * CH, :] = own[n]
        for r, ref in ((1, across_y), (2, across_x), (3, across)):
            staged[r, n * CH : (n + 1) * CH, :] = ref[mirror[n, r - 1]] * signs[:, r : r + 1]


def spread_kernel(features, spread, fp, face_low, face_high, staged):
    staged[...] = jnp.zeros_like(staged)
    for n in range(2):
        staged[n * CH : n * CH + 30, :] = features[n]
    for k in range(4):
        planes = dot(staged[:, k * 128 : (k + 1) * 128], spread[...]).astype(BF)
        for p in range(2):
            for n in range(2):
                plane = planes[n * CH : (n + 1) * CH, p * 128 : (p + 1) * 128]
                fp[n, 2 * k + p] = plane
                if k == 0 and p == 0:
                    face_low[n] = plane
                if k == 3 and p == 1:
                    face_high[n] = plane


def first_kernel(
    codes, mirror, own, part, near_low, far_low, near_high, far_high, cot, cot_y, cot_x, cot_xy,
    w_first, spread, turns, masks, signs, pre, gate_in, columns, both, face_low, face_high,
    mid, low, high, staged,
):
    stage_table(
        mid, low, high,
        lambda s, x: own[s, x], lambda s, x: part[s, x],
        lambda s: near_low[s], lambda s: far_low[s], lambda s: near_high[s], lambda s: far_high[s],
    )
    inside = masks[4:5, :].astype(F32)
    inside8 = jnp.concatenate([inside] * 8, axis=1)
    for n in range(2):
        unfold(padded_brick(codes, n, mid, low, high, masks), columns, n)
    for n in range(2):
        stacked = dot(w_first[...], columns_of(columns, n))
        a = fold(stacked, 0)
        g = fold(stacked, 96)
        pre[n] = a
        gate_in[n] = g
        hidden = (a * jax.nn.sigmoid(g) * inside8).astype(BF)
        for x in range(8):
            plane = hidden[:, x * 128 : (x + 1) * 128]
            both[0, n, x] = plane
            if x == 0:
                face_low[0, n] = plane
            if x == 7:
                face_high[0, n] = plane
    zero2 = jnp.zeros((2, 512), BF)
    own_c, y_c, x_c, xy_c = cot, cot_y, cot_x, cot_xy
    for n in range(2):
        for r, ref in ((0, own_c), (1, y_c), (2, x_c), (3, xy_c)):
            value = ref[n] if r == 0 else ref[mirror[n, r - 1]]
            staged[r, n * CH : n * CH + 30, :] = value * signs[0:30, r : r + 1]
            staged[r, n * CH + 30 : (n + 1) * CH, :] = zero2
    for k in range(4):
        back = symmetrized(None, None, None, turns, k, staged).astype(BF)
        planes = dot(back, spread[...]).astype(BF)
        for p in range(2):
            for n in range(2):
                plane = planes[n * CH : (n + 1) * CH, p * 128 : (p + 1) * 128]
                both[1, n, 2 * k + p] = plane
                if k == 0 and p == 0:
                    face_low[1, n] = plane
                if k == 3 and p == 1:
                    face_high[1, n] = plane


def second_kernel(
    scale, codes, own, part, near_low, far_low, near_high, far_high, pre, gate_in, columns_in,
    w_second, w_turned, compact, masks, rows8, blocks, place, keep, second, grads,
    mid, low, high, columns_h, columns_b, placed_f, placed_s,
):
    inside = masks[4:5, :].astype(F32)
    inside8 = jnp.concatenate([inside] * 8, axis=1)
    for f, columns in ((0, columns_h), (1, columns_b)):
        stage_table(
            mid.at[f], low.at[f], high.at[f],
            lambda s, x: own[f, s, x], lambda s, x: part[f, s, x],
            lambda s: near_low[f, s], lambda s: far_low[f, s], lambda s: near_high[f, s], lambda s: far_high[f, s],
        )
        for n in range(2):
            unfold(padded_brick(codes, n, mid.at[f], low.at[f], high.at[f], masks), columns, n)
    zero = jnp.zeros((CH, LANES), BF)

    def place_planes(placed, n, planes):
        for a in range(3):
            for p in range(10):
                value = planes(p - a) if 0 <= p - a < 8 else zero
                placed[a * CH : (a + 1) * CH, (n * 10 + p) * LANES : (n * 10 + p + 1) * LANES] = value

    for n in range(2):
        result = fold(dot(w_second[...], columns_of(columns_h, n)), 0).astype(BF)
        for k in range(4):
            second[n * CH : (n + 1) * CH, k * 128 : (k + 1) * 128] = dot(
                result[:, k * 256 : (k + 1) * 256], compact[...]
            ).astype(BF)
        place_planes(placed_s, n, lambda x: own[1, n, x])
        grad = fold(dot(w_turned[...], columns_of(columns_b, n)), 0)
        a = pre[n]
        sig = jax.nn.sigmoid(gate_in[n])
        through = grad * sig
        extra = dot(rows8[...], grad * a, precision=HIGHEST)
        sig8 = sig[0:8]
        top = through[0:8] + sig8 * (1.0 - sig8) * extra
        back_pre = (jnp.concatenate([top, through[8:]], axis=0) * inside8).astype(BF)
        place_planes(placed_f, n, lambda x: back_pre[:, x * 128 : (x + 1) * 128])
    for base, columns, placed in ((0, columns_in, placed_f), (27, columns_h, placed_s)):
        raw = lax.dot_general(
            columns[...], placed[...], (((1,), (1,)), ((), ())), preferred_element_type=F32
        )
        spread_out = dot(raw * blocks[...], place[...], precision=HIGHEST) * keep[...]
        sums = jnp.sum(spread_out.reshape(9, CH, 384), axis=1) * scale[0]
        for a in range(3):
            grads[base + 9 * a : base + 9 * a + 9, :] = sums[:, a * LANES : (a + 1) * LANES]
    grads[54:56, :] = jnp.zeros((2, LANES), F32)


def turn_kernel(mirror, own, across_y, across_x, across, turns, signs, out, staged):
    for n in range(2):
        staged[0, n * CH : (n + 1) * CH, :] = own[n * CH : (n + 1) * CH, :]
        for r, ref in ((1, across_y), (2, across_x), (3, across)):
            at = pl.multiple_of(mirror[n, r - 1] * CH, CH)
            staged[r, n * CH : (n + 1) * CH, :] = ref[pl.ds(at, CH), :] * signs[:, r : r + 1]
    for k in range(4):
        result = symmetrized(None, None, None, turns, k, staged).astype(BF)
        for n in range(2):
            out[n, :, k * 128 : (k + 1) * 128] = result[n * CH : n * CH + 30]


SMEM = pl.BlockSpec(memory_space=pltpu.SMEM)
VMEM = pl.BlockSpec(memory_space=pltpu.VMEM)


def call(kernel, n_smem, n_vmem, outs, scratch):
    return pl.pallas_call(
        kernel,
        out_shape=tuple(jax.ShapeDtypeStruct(s, t) for s, t in outs),
        in_specs=[SMEM] * n_smem + [VMEM] * n_vmem,
        out_specs=tuple([VMEM] * len(outs)),
        scratch_shapes=scratch,
        compiler_params=pltpu.CompilerParams(vmem_limit_bytes=40 * 1024 * 1024),
    )


def swap_y(x):
    n = lax.axis_size("yp")
    return lax.ppermute(x, "yp", [(i, n - 1 - i) for i in range(n)])


def mirror_x(x):
    n = lax.axis_size("xp")
    return lax.ppermute(x, "xp", [(i, n - 1 - i) for i in range(n)])


def from_below(x):
    n = lax.axis_size("xp")
    return lax.ppermute(x, "xp", [(i, i + 1) for i in range(n - 1)])


def from_above(x):
    n = lax.axis_size("xp")
    return lax.ppermute(x, "xp", [(i + 1, i) for i in range(n - 1)])


def halo(planes, face_low, face_high):
    near_low = from_below(face_high)
    near_high = from_above(face_low)
    part = swap_y(planes)
    far_low = swap_y(near_low)
    far_high = swap_y(near_high)
    return part, near_low, far_low, near_high, far_high


def total_over_map(x):
    x = x + swap_y(x)
    n = lax.axis_size("xp")
    bit = 1
    while bit < n:
        x = x + lax.ppermute(x, "xp", [(i, i ^ bit) for i in range(n)])
        bit *= 2
    return x


def expanded(weights, table):
    m = table.shape[1]
    full = dot(weights, jnp.asarray(table.reshape(84, -1), BF)).astype(BF)
    full = full.reshape(3, 9, m, CH, CH)
    return full.transpose(2, 0, 3, 1, 4).reshape(m * 96, 288)


def on_device(features, cotangent, w_first, w_second, codes, mirror):
    direct, gates, turned = expansions()
    spread = jnp.asarray(spread_table(), BF)
    compact = jnp.asarray(spread_table().T, BF)
    turns = jnp.asarray(turns_table(), BF)
    masks = jnp.asarray(region_masks(), BF)
    signs = jnp.asarray(turn_signs().T, BF)
    blocks, place, keep = (jnp.asarray(t, F32) for t in gradient_tables())
    rows8 = jnp.asarray(gather_rows(), F32)

    cot_x = mirror_x(cotangent)
    cot_y = swap_y(cotangent)
    cot_xy = swap_y(cot_x)
    fp, face_low, face_high = call(
        spread_kernel, 0, 2,
        [((2, 8, CH, LANES), BF), ((2, CH, LANES), BF), ((2, CH, LANES), BF)],
        [pltpu.VMEM((64, 512), BF)],
    )(features, spread)
    w1 = expanded(w_first, np.stack([direct, gates], axis=1))
    w2 = expanded(w_second, direct[:, None])
    w2t = expanded(w_second[::-1], turned[:, None])
    tables = [pltpu.VMEM(s + (CH, LANES), BF) for s in ((5, 8), (9,), (9,))]
    tables2 = [pltpu.VMEM((2,) + s + (CH, LANES), BF) for s in ((5, 8), (9,), (9,))]
    part, near_low, far_low, near_high, far_high = halo(fp, face_low, face_high)
    pre, gate_in, columns, both, both_low, both_high = call(
        first_kernel, 2, 15,
        [
            ((2, CH, 1024), F32), ((2, CH, 1024), F32), ((288, 2560), BF), ((2, 2, 8, CH, LANES), BF),
            ((2, 2, CH, LANES), BF), ((2, 2, CH, LANES), BF),
        ],
        [*tables, pltpu.VMEM((4, 64, 512), BF)],
    )(
        codes, mirror, fp, part, near_low, far_low, near_high, far_high, cotangent, cot_y, cot_x, cot_xy,
        w1, spread, turns, masks, signs,
    )
    part, near_low, far_low, near_high, far_high = halo(both, both_low, both_high)
    n_bricks = features.shape[0] * lax.axis_size("xp") * lax.axis_size("yp")
    scale = jnp.full((1,), 1.0 / n_bricks, F32)
    second, grads = call(
        second_kernel, 2, 17,
        [((64, 512), BF), ((56, LANES), F32)],
        [*tables2, pltpu.VMEM((288, 2560), BF), pltpu.VMEM((288, 2560), BF), pltpu.VMEM((96, 2560), BF), pltpu.VMEM((96, 2560), BF)],
    )(
        scale, codes, both, part, near_low, far_low, near_high, far_high, pre, gate_in, columns,
        w2, w2t, compact, masks, rows8, blocks, place, keep,
    )
    total = total_over_map(grads)
    second_y = swap_y(second)
    second_x = mirror_x(second)
    second_xy = swap_y(second_x)
    (denoised,) = call(turn_kernel, 1, 6, [((2, 30, 512), BF)], [pltpu.VMEM((4, 64, 512), BF)])(
        mirror, second, second_y, second_x, second_xy, turns, signs
    )
    return denoised, total[0:27, 0:84], total[27:54, 0:84]


def solution(mesh):
    brick = P(("grp", "xp", "yp"))
    return jax.shard_map(
        on_device,
        mesh=mesh,
        in_specs=(brick, brick, P(), P(), brick, brick),
        out_specs=(brick, P("grp"), P("grp")),
        check_vma=False,
    )
```

```python
import functools

import jax
import jax.numpy as jnp
from jax import lax
from jax.experimental import pallas as pl
from jax.experimental.pallas import tpu as pltpu
from jax.sharding import PartitionSpec as P

BF = jnp.bfloat16
F32 = jnp.float32
CH = 32
LANES = 128
MID = 8 * LANES
HIGHEST = lax.Precision.HIGHEST
TURNS = (0, 63, 7 + 64, 56 + 64)


def iota(shape, dim):
    return lax.broadcasted_iota(jnp.int32, shape, dim)


def component_class(i):
    tensor = jnp.where(i < 30, 12 + ((i - 20) & 1), -1)
    return jnp.where(i < 8, i, jnp.where(i < 20, 8 + ((i - 8) & 3), tensor))


def component_index(i):
    return jnp.where(i < 8, 0, jnp.where(i < 20, (i - 8) >> 2, jnp.where(i < 30, (i - 20) >> 1, -1)))


def gate_class(i):
    tensor = jnp.where(i < 30, 4 + ((i - 20) & 1), -1)
    return jnp.where(i < 8, i, jnp.where(i < 20, (i - 8) & 3, tensor))


def out_class(c):
    tensor = jnp.where(c < 84, 12 + ((c - 80) >> 1), -2)
    return jnp.where(c < 64, c >> 3, jnp.where(c < 80, 8 + ((c - 64) >> 2), tensor))


def in_class(c):
    tensor = jnp.where(c < 84, 12 + ((c - 80) & 1), -2)
    return jnp.where(c < 64, c & 7, jnp.where(c < 80, 8 + ((c - 64) & 3), tensor))


def one(condition, kind=BF):
    return jnp.where(condition, 1.0, 0.0).astype(kind)


def plane_source(q):
    lane = q & 127
    row = (lane * 205) >> 11
    y, z = row - 1, lane - 10 * row - 1
    inside = (y >= 0) & (y < 8) & (z >= 0) & (z < 8)
    return jnp.where(inside, 64 * (q >> 7) + 8 * y + z, -1)


def spread_table():
    return one(plane_source(iota((128, 256), 1)) == iota((128, 256), 0))


def compact_table():
    return one(plane_source(iota((256, 128), 0)) == iota((256, 128), 1))


def turn_table(r):
    return one((iota((128, 128), 1) ^ TURNS[r]) == iota((128, 128), 0))


def turn_signs(r, shape):
    i = iota(shape, 0) & (CH - 1)
    m = component_index(i)
    vector = (i >= 8) & (i < 20) & (m != r - 1)
    tensor = (i >= 20) & (m < 3) & (m != 3 - r)
    return jnp.where(vector | tensor, -1.0, 1.0).astype(BF)


def region_masks():
    lane = iota((1, LANES), 1)
    row = (lane * 205) >> 11
    col = lane - 10 * row

    def part(v):
        return jnp.where(v == 0, 0, jnp.where(v == 9, 2, 1))

    region = jnp.where(row < 10, 3 * part(row) + part(col), -1)
    return [one(region == o) for o in range(9)]


def dot(a, b, **kw):
    return jnp.dot(a, b, preferred_element_type=F32, **kw)


def dot_t(a, b):
    return lax.dot_general(a, b, (((1,), (1,)), ((), ())), preferred_element_type=F32)


def is_odd():
    return (lax.axis_index("xp") & 1) == 1


def table_row(codes, n, o, last):
    e = codes[n, o]
    d = e >> 1
    dx = lax.div(d, 3)
    other = jnp.where(d - 3 * dx == 1, 0, 2) + jnp.where(dx == 1, 0, 4)
    return jnp.where(e >= 18, last, jnp.minimum(other + (e & 1), last))


def gathered(pieces_of, masks):
    total = None
    for b in range(3):
        for c in range(3):
            o = 3 * b + c
            planes = jnp.concatenate(pieces_of(o), axis=0)
            shift = ((b - 1) * 80 + (c - 1) * 8) % LANES
            if shift:
                planes = pltpu.roll(planes, shift, 1)
            planes = planes * masks[o]
            total = planes if total is None else total + planes
    return total


def unfold(planes, count, columns, start):
    for o in range(9):
        shift = (11 - 10 * (o // 3) - o % 3) % LANES
        moved = pltpu.roll(planes, shift, 1) if shift else planes
        for p in range(count):
            at = start + p * LANES
            columns[o * CH : (o + 1) * CH, at : at + LANES] = moved[p * CH : (p + 1) * CH]


def stage_mid(table, own, part):
    zero = jnp.zeros((CH, LANES), BF)
    for x in range(8):
        for s in range(2):
            table[s, x] = own(s, x)
            table[2 + s, x] = part(s, x)
        table[4, x] = zero


def mid_columns(codes, masks, table, columns):
    for n in range(2):
        planes = gathered(lambda o: [table[table_row(codes, n, 9 + o, 4)].reshape(8 * CH, LANES)], masks)
        unfold(planes, 8, columns, n * MID)


def stage_edge(low, high, own, part, received, far):
    odd = is_odd()
    zero = jnp.zeros((CH, LANES), BF)
    for s in range(2):
        low[s], high[s] = own(s, 7), own(s, 0)
        low[2 + s], high[2 + s] = part(s, 7), part(s, 0)
        for base, faces in ((4, received), (6, far)):
            first, second = faces(0, s), faces(1, s)
            low[base + s] = jnp.where(odd, first, second)
            high[base + s] = jnp.where(odd, second, first)
    low[8] = zero
    high[8] = zero


def edge_columns(codes, masks, low, high, columns):
    def pieces(o):
        found = []
        for n in range(2):
            found += [low[table_row(codes, n, o, 8)], high[table_row(codes, n, 18 + o, 8)]]
        return found

    unfold(gathered(pieces, masks), 4, columns, 0)


def fold_mid(stacked, row):
    zero = jnp.zeros((CH, LANES), F32)
    before = jnp.concatenate([zero, stacked[row : row + CH, : MID - LANES]], axis=1)
    after = jnp.concatenate([stacked[row + 2 * CH : row + 3 * CH, LANES:], zero], axis=1)
    return before + stacked[row + CH : row + 2 * CH] + after


def edge_term(stacked, row, n, side):
    at = (2 * n + side) * LANES
    first = row + 2 * CH * side
    return stacked[first : first + CH, at : at + LANES]


def write_faces(face_a, face_b, index, plane_low, plane_high):
    odd = is_odd()
    face_a[index] = jnp.where(odd, plane_low, plane_high)
    face_b[index] = jnp.where(odd, plane_high, plane_low)


def spread_kernel(features, *refs):
    small, (fp, face_a, face_b), copies, staged = refs[:4], refs[4:7], refs[7:11], refs[11]
    for source, copy in zip(small, copies):
        copy[...] = source[...]
    staged[...] = jnp.zeros_like(staged)
    for n in range(2):
        staged[n * CH : n * CH + 30, :] = features[n]
    spread = spread_table()
    outer = []
    for k in range(4):
        planes = dot(staged[:, k * 128 : (k + 1) * 128], spread).astype(BF)
        for p in range(2):
            for n in range(2):
                plane = planes[n * CH : (n + 1) * CH, p * 128 : (p + 1) * 128]
                fp[n, 2 * k + p] = plane
                if 2 * k + p in (0, 7):
                    outer.append(plane)
    for n in range(2):
        write_faces(face_a, face_b, n, outer[n], outer[2 + n])


def weights_kernel(w_first, w_second, one_out, two_out, turned_out, padded, left):
    shape = (CH, LANES)
    i, c = iota(shape, 0), iota(shape, 1)
    double = jnp.where(i >= 20, 2.0, 1.0)
    j = iota((LANES, LANES), 1) & (CH - 1)
    col = iota((LANES, LANES), 0)
    by_in = one(in_class(col) == component_class(j))
    by_out = one(out_class(col) == component_class(j))
    rows_out = jnp.where(component_class(i) == out_class(c), double, 0.0)
    rows_gate = one(gate_class(i) == out_class(c), F32)
    rows_in = jnp.where(component_class(i) == in_class(c), double, 0.0)
    same = component_index(i) == component_index(c & (CH - 1))
    quarter = c >> 5
    padded[...] = jnp.zeros_like(padded)
    padded[0, 0:27, 0:84] = w_first[...].astype(F32)
    padded[1, 0:27, 0:84] = w_second[...].astype(F32)
    for which, rows, columns, blocks, out, base, flip in (
        (0, rows_out, by_in, True, one_out, 0, False),
        (0, rows_gate, by_in, False, one_out, 96, False),
        (1, rows_out, by_in, True, two_out, 0, False),
        (1, rows_in, by_out, True, turned_out, 0, True),
    ):
        for a in range(3):
            for bc in range(9):
                o = 9 * a + bc
                o = 26 - o if flip else o
                left[bc * CH : (bc + 1) * CH, :] = (rows * padded[which, o : o + 1, :]).astype(BF)
            found = dot(left[...], columns)
            for g in range(3):
                tile = jnp.zeros(shape, F32)
                for q in range(min(4, 9 - 4 * g)):
                    bc = 4 * g + q
                    keep = (quarter == q) & same if blocks else quarter == q
                    tile = tile + jnp.where(keep, found[bc * CH : (bc + 1) * CH], 0.0)
                width = min(128, 288 - 128 * g)
                out[base + a * CH : base + (a + 1) * CH, g * 128 : g * 128 + width] = tile[:, :width].astype(BF)


def first_mid_kernel(codes, own, part, w_first, columns, pre, gate_in, hidden_mid, table):
    masks = region_masks()
    inside = masks[4].astype(F32)
    stage_mid(table, lambda s, x: own[s, x], lambda s, x: part[s, x])
    mid_columns(codes, masks, table, columns)
    for n in range(2):
        stacked = dot(w_first[...], columns[:, n * MID : (n + 1) * MID])
        a, g = fold_mid(stacked, 0), fold_mid(stacked, 96)
        pre[n] = a
        gate_in[n] = g
        for x in range(1, 7):
            at = slice(x * LANES, (x + 1) * LANES)
            hidden_mid[n, x - 1] = (a[:, at] * jax.nn.sigmoid(g[:, at]) * inside).astype(BF)


def turned_sum(staged, k):
    total = None
    for r in range(4):
        block = k if r < 2 else 3 - k
        term = dot(staged[r, :, 128 * block : 128 * block + 128], turn_table(r))
        total = term if total is None else total + term
    return total * 0.25


def back_kernel(mirror, own, across_y, across_x, across, back, staged):
    zero2 = jnp.zeros((2, 512), BF)
    for n in range(2):
        for r, ref in enumerate((own, across_y, across_x, across)):
            value = ref[n] if r == 0 else ref[mirror[n, r - 1]] * turn_signs(r, (30, 512))
            staged[r, n * CH : n * CH + 30, :] = value
            staged[r, n * CH + 30 : (n + 1) * CH, :] = zero2
    spread = spread_table()
    for k in range(4):
        planes = dot(turned_sum(staged, k).astype(BF), spread).astype(BF)
        for p in range(2):
            for n in range(2):
                back[n, 2 * k + p] = planes[n * CH : (n + 1) * CH, p * 128 : (p + 1) * 128]


def first_edge_kernel(
    codes, own, part, got_a, got_b, far_a, far_b, pre, gate_in, hidden_mid, back, w_first,
    columns, pre_edge, gate_edge, both, face_a, face_b, low, high,
):
    masks = region_masks()
    inside = masks[4].astype(F32)
    stage_edge(
        low, high, lambda s, x: own[s, x], lambda s, x: part[s, x],
        lambda which, s: (got_a, got_b)[which][s], lambda which, s: (far_a, far_b)[which][s],
    )
    edge_columns(codes, masks, low, high, columns)
    stacked = dot(w_first[...], columns[...])
    for n in range(2):
        outer = []
        for side in range(2):
            at = slice(7 * side * LANES, (7 * side + 1) * LANES)
            a = pre[n, :, at] + edge_term(stacked, 0, n, side)
            g = gate_in[n, :, at] + edge_term(stacked, 96, n, side)
            pre_edge[n, side] = a
            gate_edge[n, side] = g
            outer.append((a * jax.nn.sigmoid(g) * inside).astype(BF))
            both[0, n, 7 * side] = outer[side]
        write_faces(face_a, face_b, (0, n), *outer)
        for x in range(1, 7):
            both[0, n, x] = hidden_mid[n, x - 1]
        for x in range(8):
            both[1, n, x] = back[n, x]
        write_faces(face_a, face_b, (1, n), back[n, 0], back[n, 7])


def gate_back(grad, a, g, rows8, inside):
    sig = jax.nn.sigmoid(g)
    through = grad * sig
    extra = dot(rows8, grad * a, precision=HIGHEST)
    sig8 = sig[0:8]
    top = through[0:8] + sig8 * (1.0 - sig8) * extra
    return (jnp.concatenate([top, through[8:]], axis=0) * inside).astype(BF)


def gate_rows():
    return one(gate_class(iota((8, CH), 1)) == iota((8, CH), 0), F32)


def second_mid_kernel(
    codes, own, part, pre, gate_in, columns_f, w_second, w_turned, second, through_edge, raw,
    table, columns_h, columns_b, placed_f, placed_s,
):
    masks = region_masks()
    inside = jnp.concatenate([masks[4].astype(F32)] * 6, axis=1)
    for f, columns in ((0, columns_h), (1, columns_b)):
        stage_mid(table.at[f], lambda s, x: own[f, s, x], lambda s, x: part[f, s, x])
        mid_columns(codes, masks, table.at[f], columns)
    zero = jnp.zeros((CH, LANES), BF)
    rows8 = gate_rows()

    def place(placed, n, planes, first, last):
        for a in range(3):
            for q in range(8):
                x = q + 1 - a
                at = (8 * n + q) * LANES
                placed[a * CH : (a + 1) * CH, at : at + LANES] = planes(x) if first <= x <= last else zero

    for n in range(2):
        here = slice(n * MID, (n + 1) * MID)
        second[n] = fold_mid(dot(w_second[...], columns_h[:, here]), 0)
        place(placed_s, n, lambda x: own[1, n, x], 0, 7)
        grad = fold_mid(dot(w_turned[...], columns_b[:, here]), 0)
        through_edge[n, 0] = grad[:, :LANES]
        through_edge[n, 1] = grad[:, 7 * LANES :]
        inner = slice(LANES, 7 * LANES)
        back_pre = gate_back(grad[:, inner], pre[n, :, inner], gate_in[n, :, inner], rows8, inside)
        place(placed_f, n, lambda x: back_pre[:, (x - 1) * LANES : x * LANES], 1, 6)
    raw[0] = dot_t(columns_f[...], placed_f[...])
    raw[1] = dot_t(columns_h[...], placed_s[...])


def second_edge_kernel(
    scale, codes, own, part, got_a, got_b, far_a, far_b, pre_edge, gate_edge, second_in, through_edge,
    columns_f, columns_fe, raw, w_second, w_turned, second, grads,
    low, high, columns_h, columns_b, placed_f, placed_s, place, lifted,
):
    masks = region_masks()
    inside = masks[4].astype(F32)
    for f, columns in ((0, columns_h), (1, columns_b)):
        stage_edge(
            low.at[f], high.at[f], lambda s, x: own[f, s, x], lambda s, x: part[f, s, x],
            lambda which, s: (got_a, got_b)[which][f, s], lambda which, s: (far_a, far_b)[which][f, s],
        )
        edge_columns(codes, masks, low.at[f], high.at[f], columns)
    more = dot(w_second[...], columns_h[...])
    more_t = dot(w_turned[...], columns_b[...])
    rows8 = gate_rows()
    compact = compact_table()
    placed_f[...] = jnp.zeros_like(placed_f)
    placed_s[...] = jnp.zeros_like(placed_s)
    for n in range(2):
        for k in range(4):
            planes = second_in[n, :, k * 256 : (k + 1) * 256]
            zero = jnp.zeros((CH, LANES), F32)
            if k == 0:
                planes = planes + jnp.concatenate([edge_term(more, 0, n, 0), zero], axis=1)
            if k == 3:
                planes = planes + jnp.concatenate([zero, edge_term(more, 0, n, 1)], axis=1)
            second[n * CH : (n + 1) * CH, k * 128 : (k + 1) * 128] = dot(planes.astype(BF), compact).astype(BF)
        for side in range(2):
            grad = through_edge[n, side] + edge_term(more_t, 0, n, side)
            back_pre = gate_back(grad, pre_edge[n, side], gate_edge[n, side], rows8, inside)
            at = (2 * n + side) * LANES
            a = 2 * side
            placed_s[a * CH : (a + 1) * CH, at : at + LANES] = own[1, n, 7 * side]
            for a in range(3):
                at = (6 * n + 3 * side + a) * LANES
                placed_f[a * CH : (a + 1) * CH, at : at + LANES] = back_pre
    pieces = []
    for n in range(2):
        mid, edge = n * MID, 2 * n * LANES
        pieces += [
            columns_fe[:, edge : edge + LANES], columns_f[:, mid : mid + 2 * LANES],
            columns_f[:, mid + 6 * LANES : mid + MID], columns_fe[:, edge + LANES : edge + 2 * LANES],
        ]
    shape = (CH, LANES)
    i, c = iota(shape, 0), iota(shape, 1)
    lift = jnp.where(component_class(i) == out_class(c), jnp.where(i >= 20, 2.0, 1.0), 0.0)
    keep = one(component_class(i) == in_class(c), F32)
    same = one(component_index(i) == component_index(iota(shape, 1) & (CH - 1)), F32)[:, 0:96]
    place[...] = jnp.zeros_like(place)
    for a in range(3):
        place[a * CH : (a + 1) * CH, a * LANES : (a + 1) * LANES] = lift
    found = (
        raw[0] + dot_t(jnp.concatenate(pieces, axis=1), placed_f[...]),
        raw[1] + dot_t(columns_h[...], placed_s[...]),
    )
    for layer in range(2):
        masked = (found[layer].reshape(9, CH, 96) * same).reshape(9 * CH, 96)
        lifted[...] = dot(masked, place[...], precision=HIGHEST)
        for a in range(3):
            block = lifted[:, a * LANES : (a + 1) * LANES].reshape(9, CH, LANES) * keep
            first = 27 * layer + 9 * a
            grads[first : first + 9, :] = jnp.sum(block, axis=1) * scale
    grads[54:56, :] = jnp.zeros((2, LANES), F32)


def turn_kernel(mirror, own, across_y, across_x, across, out, staged):
    for n in range(2):
        staged[0, n * CH : (n + 1) * CH, :] = own[n * CH : (n + 1) * CH, :]
        for r, ref in ((1, across_y), (2, across_x), (3, across)):
            at = pl.multiple_of(mirror[n, r - 1] * CH, CH)
            staged[r, n * CH : (n + 1) * CH, :] = ref[pl.ds(at, CH), :] * turn_signs(r, (CH, 512))
    for k in range(4):
        result = turned_sum(staged, k).astype(BF)
        for n in range(2):
            out[n, :, k * 128 : (k + 1) * 128] = result[n * CH : n * CH + 30]


SMEM = pl.BlockSpec(memory_space=pltpu.SMEM)
VMEM = pl.BlockSpec(memory_space=pltpu.VMEM)


def call(kernel, us, n_smem, outs, scratch, *args):
    return pl.pallas_call(
        kernel,
        out_shape=tuple(jax.ShapeDtypeStruct(s, t) for s, t in outs),
        in_specs=[SMEM] * n_smem + [VMEM] * (len(args) - n_smem),
        out_specs=tuple([VMEM] * len(outs)),
        scratch_shapes=[pltpu.VMEM(s, t) for s, t in scratch],
        compiler_params=pltpu.CompilerParams(vmem_limit_bytes=24 * 1024 * 1024),
        cost_estimate=pl.CostEstimate(flops=0, transcendentals=0, bytes_accessed=int(us * 3_000_000)),
    )(*args)


def swap_y(x):
    n = lax.axis_size("yp")
    return lax.ppermute(x, "yp", [(i, n - 1 - i) for i in range(n)])


def mirror_x(x):
    n = lax.axis_size("xp")
    return lax.ppermute(x, "xp", [(i, n - 1 - i) for i in range(n)])


def pair_swap(x, first):
    n = lax.axis_size("xp")
    pairs = []
    for i in range(first, n - 1, 2):
        pairs += [(i, i + 1), (i + 1, i)]
    return lax.ppermute(x, "xp", pairs)


def exchange(face_a, face_b):
    got_b = pair_swap(face_b, 1)
    got_a = pair_swap(face_a, 0)
    return got_a, got_b


def after(arrays, *others):
    return lax.optimization_barrier((tuple(arrays), others))[0]


def on_device(features, cotangent, w_first, w_second, codes, mirror):
    plane = (CH, LANES)
    fp, face_a, face_b, codes, mirror, w_first, w_second = call(
        spread_kernel, 0.2, 0,
        [
            ((2, 8) + plane, BF), ((2,) + plane, BF), ((2,) + plane, BF),
            *((x.shape, x.dtype) for x in (codes, mirror, w_first, w_second)),
        ],
        [((64, 512), BF)], features, codes, mirror, w_first, w_second,
    )
    cot_x = mirror_x(cotangent)
    cot_y = swap_y(cotangent)
    got = exchange(face_a, face_b)
    part = swap_y(fp)
    w1, w2, w2t = call(
        weights_kernel, 0.5, 0, [((192, 288), BF), ((96, 288), BF), ((96, 288), BF)],
        [((2, CH, LANES), F32), ((288, LANES), BF)], w_first, w_second,
    )
    columns, pre, gate_in, hidden_mid = call(
        first_mid_kernel, 2, 1,
        [((288, 2 * MID), BF), ((2, CH, MID), F32), ((2, CH, MID), F32), ((2, 6) + plane, BF)],
        [((5, 8) + plane, BF)], codes, fp, part, w1,
    )
    *got, cot_x = after((*got, cot_x), hidden_mid)
    faces = (*got, swap_y(got[0]), swap_y(got[1]))
    cot_xy = swap_y(cot_x)
    (back,) = call(
        back_kernel, 1.5, 1, [((2, 8) + plane, BF)], [((4, 64, 512), BF)], mirror, cotangent, cot_y, cot_x, cot_xy
    )
    columns_e, pre_e, gate_e, both, face_a, face_b = call(
        first_edge_kernel, 1.2, 1,
        [
            ((288, 4 * LANES), BF), ((2, 2) + plane, F32), ((2, 2) + plane, F32), ((2, 2, 8) + plane, BF),
            ((2, 2) + plane, BF), ((2, 2) + plane, BF),
        ],
        [((9,) + plane, BF)] * 2, codes, fp, part, *faces, pre, gate_in, hidden_mid, back, w1,
    )
    got = exchange(face_a, face_b)
    part = swap_y(both)
    second_part, through_e, raw = call(
        second_mid_kernel, 3.5, 1, [((2, CH, MID), F32), ((2, 2) + plane, F32), ((2, 288, 96), F32)],
        [((2, 5, 8) + plane, BF), ((288, 2 * MID), BF), ((288, 2 * MID), BF), ((96, 2 * MID), BF), ((96, 2 * MID), BF)],
        codes, both, part, pre, gate_in, columns, w2, w2t,
    )
    got = after(got, raw)
    faces = (*got, swap_y(got[0]), swap_y(got[1]))
    n_bricks = features.shape[0] * lax.axis_size("xp") * lax.axis_size("yp")
    second, grads = call(
        functools.partial(second_edge_kernel, 1.0 / n_bricks), 2.8, 1, [((64, 512), BF), ((56, LANES), F32)],
        [((2, 9) + plane, BF)] * 2 + [((288, 4 * LANES), BF)] * 2
        + [((96, 12 * LANES), BF), ((96, 4 * LANES), BF), ((96, 3 * LANES), F32), ((288, 3 * LANES), F32)],
        codes, both, part, *faces, pre_e, gate_e, second_part, through_e, columns, columns_e, raw, w2, w2t,
    )
    total = grads + swap_y(grads)
    (second,) = after((second,), total)
    second_y = swap_y(second)
    second_x = mirror_x(second)
    second_xy = swap_y(second_x)
    (denoised,) = call(
        turn_kernel, 0.9, 1, [((2, 30, 512), BF)], [((4, 64, 512), BF)], mirror, second, second_y, second_x, second_xy
    )
    n = lax.axis_size("xp")
    bit = 1
    while bit < n:
        total = total + lax.ppermute(total, "xp", [(i, i ^ bit) for i in range(n)])
        bit *= 2
    return denoised, total[0:27, 0:84], total[27:54, 0:84]


def solution(mesh):
    brick = P(("grp", "xp", "yp"))
    return jax.shard_map(
        on_device,
        mesh=mesh,
        in_specs=(brick, brick, P(), P(), brick, brick),
        out_specs=(brick, P("grp"), P("grp")),
        check_vma=False,
    )
```

```python
import functools

import jax
import jax.numpy as jnp
from jax import lax
from jax.experimental import pallas as pl
from jax.experimental.pallas import tpu as pltpu
from jax.sharding import PartitionSpec as P

BF = jnp.bfloat16
F32 = jnp.float32
CH = 32
LANES = 128
MID = 8 * LANES
HIGHEST = lax.Precision.HIGHEST
TURNS = (0, 63, 7 + 64, 56 + 64)


def iota(shape, dim):
    return lax.broadcasted_iota(jnp.int32, shape, dim)


def component_class(i):
    tensor = jnp.where(i < 30, 12 + ((i - 20) & 1), -1)
    return jnp.where(i < 8, i, jnp.where(i < 20, 8 + ((i - 8) & 3), tensor))


def component_index(i):
    return jnp.where(i < 8, 0, jnp.where(i < 20, (i - 8) >> 2, jnp.where(i < 30, (i - 20) >> 1, -1)))


def gate_class(i):
    tensor = jnp.where(i < 30, 4 + ((i - 20) & 1), -1)
    return jnp.where(i < 8, i, jnp.where(i < 20, (i - 8) & 3, tensor))


def out_class(c):
    tensor = jnp.where(c < 84, 12 + ((c - 80) >> 1), -2)
    return jnp.where(c < 64, c >> 3, jnp.where(c < 80, 8 + ((c - 64) >> 2), tensor))


def in_class(c):
    tensor = jnp.where(c < 84, 12 + ((c - 80) & 1), -2)
    return jnp.where(c < 64, c & 7, jnp.where(c < 80, 8 + ((c - 64) & 3), tensor))


def one(condition, kind=BF):
    return jnp.where(condition, 1.0, 0.0).astype(kind)


def plane_source(q):
    lane = q & 127
    row = (lane * 205) >> 11
    y, z = row - 1, lane - 10 * row - 1
    inside = (y >= 0) & (y < 8) & (z >= 0) & (z < 8)
    return jnp.where(inside, 64 * (q >> 7) + 8 * y + z, -1)


def spread_table():
    return one(plane_source(iota((128, 256), 1)) == iota((128, 256), 0))


def compact_table():
    return one(plane_source(iota((256, 128), 0)) == iota((256, 128), 1))


def turn_table(r):
    return one((iota((128, 128), 1) ^ TURNS[r]) == iota((128, 128), 0))


def turns_table():
    return jnp.concatenate([turn_table(r) for r in range(4)], axis=0)


def turns_spread_table():
    source = plane_source(iota((128, 256), 1))
    return jnp.concatenate([one((source ^ TURNS[r]) == iota((128, 256), 0)) for r in range(4)], axis=0)


def turn_signs(r, shape):
    i = iota(shape, 0) & (CH - 1)
    m = component_index(i)
    vector = (i >= 8) & (i < 20) & (m != r - 1)
    tensor = (i >= 20) & (m < 3) & (m != 3 - r)
    return jnp.where(vector | tensor, -1.0, 1.0).astype(BF)


def region_masks():
    lane = iota((1, LANES), 1)
    row = (lane * 205) >> 11
    col = lane - 10 * row

    def part(v):
        return jnp.where(v == 0, 0, jnp.where(v == 9, 2, 1))

    region = jnp.where(row < 10, 3 * part(row) + part(col), -1)
    return [one(region == o) for o in range(9)]


def dot(a, b, **kw):
    return jnp.dot(a, b, preferred_element_type=F32, **kw)


def dot_t(a, b):
    return lax.dot_general(a, b, (((1,), (1,)), ((), ())), preferred_element_type=F32)


def is_odd():
    return (lax.axis_index("xp") & 1) == 1


def table_row(codes, n, o, last):
    e = codes[n, o]
    d = e >> 1
    dx = lax.div(d, 3)
    other = jnp.where(d - 3 * dx == 1, 0, 2) + jnp.where(dx == 1, 0, 4)
    return jnp.where(e >= 18, last, jnp.minimum(other + (e & 1), last))


def gathered(pieces_of, masks):
    total = None
    for b in range(3):
        for c in range(3):
            o = 3 * b + c
            planes = jnp.concatenate(pieces_of(o), axis=0)
            shift = ((b - 1) * 80 + (c - 1) * 8) % LANES
            if shift:
                planes = pltpu.roll(planes, shift, 1)
            planes = planes * masks[o]
            total = planes if total is None else total + planes
    return total


def unfold(planes, count, columns, start):
    for o in range(9):
        shift = (11 - 10 * (o // 3) - o % 3) % LANES
        moved = pltpu.roll(planes, shift, 1) if shift else planes
        for p in range(count):
            at = start + p * LANES
            columns[o * CH : (o + 1) * CH, at : at + LANES] = moved[p * CH : (p + 1) * CH]


def stage_mid(table, own, part):
    zero = jnp.zeros((CH, LANES), BF)
    for x in range(8):
        for s in range(2):
            table[s, x] = own(s, x)
            table[2 + s, x] = part(s, x)
        table[4, x] = zero


def mid_columns(codes, masks, table, columns):
    for n in range(2):
        planes = gathered(lambda o: [table[table_row(codes, n, 9 + o, 4)].reshape(8 * CH, LANES)], masks)
        unfold(planes, 8, columns, n * MID)


def stage_edge(low, high, own, part, received, far):
    odd = is_odd()
    zero = jnp.zeros((CH, LANES), BF)
    for s in range(2):
        low[s], high[s] = own(s, 7), own(s, 0)
        low[2 + s], high[2 + s] = part(s, 7), part(s, 0)
        for base, faces in ((4, received), (6, far)):
            first, second = faces(0, s), faces(1, s)
            low[base + s] = jnp.where(odd, first, second)
            high[base + s] = jnp.where(odd, second, first)
    low[8] = zero
    high[8] = zero


def edge_columns(codes, masks, low, high, columns):
    def pieces(o):
        found = []
        for n in range(2):
            found += [low[table_row(codes, n, o, 8)], high[table_row(codes, n, 18 + o, 8)]]
        return found

    unfold(gathered(pieces, masks), 4, columns, 0)


def fold_mid(stacked, row):
    zero = jnp.zeros((CH, LANES), F32)
    before = jnp.concatenate([zero, stacked[row : row + CH, : MID - LANES]], axis=1)
    after = jnp.concatenate([stacked[row + 2 * CH : row + 3 * CH, LANES:], zero], axis=1)
    return before + stacked[row + CH : row + 2 * CH] + after


def edge_terms(stacked, row):
    blocks = []
    for e in range(4):
        first = row + 2 * CH * (e & 1)
        blocks.append(stacked[first : first + CH, e * LANES : (e + 1) * LANES])
    return jnp.concatenate(blocks, axis=1)


def edge_planes(ref):
    return jnp.concatenate([ref[e >> 1, :, 7 * (e & 1) * LANES : (7 * (e & 1) + 1) * LANES] for e in range(4)], axis=1)


def write_faces(face_a, face_b, index, plane_low, plane_high):
    odd = is_odd()
    face_a[index] = jnp.where(odd, plane_low, plane_high)
    face_b[index] = jnp.where(odd, plane_high, plane_low)


def spread_kernel(features, fp, faces, staged):
    staged[...] = jnp.zeros_like(staged)
    for n in range(2):
        staged[n * CH : n * CH + 30, :] = features[n]
    rows = jnp.concatenate([staged[:, k * 128 : (k + 1) * 128] for k in range(4)], axis=0)
    planes = dot(rows, spread_table()).astype(BF)
    for n in range(2):
        for x in range(8):
            first = (x >> 1) * 2 * CH + n * CH
            fp[n, x] = planes[first : first + CH, (x & 1) * LANES : (x & 1) * LANES + LANES]
        write_faces(faces.at[0], faces.at[1], n, fp[n, 0], fp[n, 7])


def weights_kernel(packed, small, one_out, two_out, turned_out, codes_out, mirror_out, padded, left):
    shape = (CH, LANES)
    i, c = iota(shape, 0), iota(shape, 1)
    double = jnp.where(i >= 20, 2.0, 1.0)
    j = iota((LANES, LANES), 1) & (CH - 1)
    col = iota((LANES, LANES), 0)
    by_in = one(in_class(col) == component_class(j))
    by_out = one(out_class(col) == component_class(j))
    rows_out = jnp.where(component_class(i) == out_class(c), double, 0.0)
    rows_gate = one(gate_class(i) == out_class(c), F32)
    rows_in = jnp.where(component_class(i) == in_class(c), double, 0.0)
    same = component_index(i) == component_index(c & (CH - 1))
    quarter = c >> 5
    padded[...] = jnp.zeros_like(padded)
    for which in range(2):
        padded[which, 0:27, 0:84] = packed[0:27, which * LANES : which * LANES + 84].astype(F32)
    codes_out[...] = small[:, 0:27]
    mirror_out[...] = small[:, LANES : LANES + 3]
    for which, rows, columns, blocks, out, base, flip in (
        (0, rows_out, by_in, True, one_out, 0, False),
        (0, rows_gate, by_in, False, one_out, 96, False),
        (1, rows_out, by_in, True, two_out, 0, False),
        (1, rows_in, by_out, True, turned_out, 0, True),
    ):
        for a in range(3):
            for bc in range(9):
                o = 9 * a + bc
                o = 26 - o if flip else o
                left[bc * CH : (bc + 1) * CH, :] = (rows * padded[which, o : o + 1, :]).astype(BF)
            found = dot(left[...], columns)
            for g in range(3):
                tile = jnp.zeros(shape, F32)
                for q in range(min(4, 9 - 4 * g)):
                    bc = 4 * g + q
                    keep = (quarter == q) & same if blocks else quarter == q
                    tile = tile + jnp.where(keep, found[bc * CH : (bc + 1) * CH], 0.0)
                width = min(128, 288 - 128 * g)
                out[base + a * CH : base + (a + 1) * CH, g * 128 : g * 128 + width] = tile[:, :width].astype(BF)


def first_mid_kernel(codes, own, part, w_first, columns, pre, gate_in, hidden_mid, table):
    masks = region_masks()
    inside = masks[4].astype(F32)
    stage_mid(table, lambda s, x: own[s, x], lambda s, x: part[s, x])
    mid_columns(codes, masks, table, columns)
    for n in range(2):
        stacked = dot(w_first[...], columns[:, n * MID : (n + 1) * MID])
        a, g = fold_mid(stacked, 0), fold_mid(stacked, 96)
        pre[n] = a
        gate_in[n] = g
        for x in range(1, 7):
            at = slice(x * LANES, (x + 1) * LANES)
            hidden_mid[n, x - 1] = (a[:, at] * jax.nn.sigmoid(g[:, at]) * inside).astype(BF)


def turned_sum(staged, table):
    rows = []
    for k in range(4):
        blocks = (k, k, 3 - k, 3 - k)
        rows.append(jnp.concatenate([staged[r, :, 128 * b : 128 * b + 128] for r, b in enumerate(blocks)], axis=1))
    return dot(jnp.concatenate(rows, axis=0), table) * 0.25


def back_kernel(mirror, own, across_y, across_x, across, back, staged):
    zero2 = jnp.zeros((2, 512), BF)
    for n in range(2):
        for r in range(4):
            if r == 0:
                value = own[n]
            else:
                value = (across_y, across_x, across)[r - 1][mirror[n, r - 1]] * turn_signs(r, (30, 512))
            staged[r, n * CH : n * CH + 30, :] = value
            staged[r, n * CH + 30 : (n + 1) * CH, :] = zero2
    planes = turned_sum(staged, turns_spread_table()).astype(BF)
    for n in range(2):
        for x in range(8):
            first = (x >> 1) * 2 * CH + n * CH
            back[n, x] = planes[first : first + CH, (x & 1) * LANES : (x & 1) * LANES + LANES]


def first_edge_kernel(
    codes, own, part, got_a, got_b, pre, gate_in, hidden_mid, back, w_first,
    columns, pre_edge, gate_edge, both, face_a, face_b, low, high,
):
    masks = region_masks()
    inside = jnp.concatenate([masks[4].astype(F32)] * 4, axis=1)
    stage_edge(
        low, high, lambda s, x: own[s, x], lambda s, x: part[s, x],
        lambda which, s: (got_a, got_b)[which][s], lambda which, s: (got_a, got_b)[which][2 + s],
    )
    edge_columns(codes, masks, low, high, columns)
    stacked = dot(w_first[...], columns[...])
    a = edge_planes(pre) + edge_terms(stacked, 0)
    g = edge_planes(gate_in) + edge_terms(stacked, 96)
    pre_edge[...] = a
    gate_edge[...] = g
    hidden = (a * jax.nn.sigmoid(g) * inside).astype(BF)
    for n in range(2):
        outer = [hidden[:, e * LANES : (e + 1) * LANES] for e in (2 * n, 2 * n + 1)]
        both[0, n, 0], both[0, n, 7] = outer
        write_faces(face_a, face_b, (0, n), *outer)
        for x in range(1, 7):
            both[0, n, x] = hidden_mid[n, x - 1]
        for x in range(8):
            both[1, n, x] = back[n, x]
        write_faces(face_a, face_b, (1, n), back[n, 0], back[n, 7])


def gate_back(grad, a, g, rows8, inside):
    sig = jax.nn.sigmoid(g)
    through = grad * sig
    extra = dot(rows8, grad * a, precision=HIGHEST)
    sig8 = sig[0:8]
    top = through[0:8] + sig8 * (1.0 - sig8) * extra
    return (jnp.concatenate([top, through[8:]], axis=0) * inside).astype(BF)


def gate_rows():
    return one(gate_class(iota((8, CH), 1)) == iota((8, CH), 0), F32)


def second_mid_kernel(
    codes, own, part, pre, gate_in, columns_f, w_second, w_turned, second, through_edge, raw,
    table, columns_h, columns_b, placed_f, placed_s,
):
    masks = region_masks()
    inside = jnp.concatenate([masks[4].astype(F32)] * 6, axis=1)
    for f, columns in ((0, columns_h), (1, columns_b)):
        stage_mid(table.at[f], lambda s, x: own[f, s, x], lambda s, x: part[f, s, x])
        mid_columns(codes, masks, table.at[f], columns)
    zero = jnp.zeros((CH, LANES), BF)
    rows8 = gate_rows()
    for placed in (placed_f, placed_s):
        placed[3 * CH :, :] = jnp.zeros((CH, 2 * MID), BF)

    def place(placed, n, planes, first, last):
        for a in range(3):
            for q in range(8):
                x = q + 1 - a
                at = (8 * n + q) * LANES
                placed[a * CH : (a + 1) * CH, at : at + LANES] = planes(x) if first <= x <= last else zero

    for n in range(2):
        here = slice(n * MID, (n + 1) * MID)
        second[n] = fold_mid(dot(w_second[...], columns_h[:, here]), 0)
        place(placed_s, n, lambda x: own[1, n, x], 0, 7)
        grad = fold_mid(dot(w_turned[...], columns_b[:, here]), 0)
        through_edge[:, 2 * n * LANES : (2 * n + 1) * LANES] = grad[:, :LANES]
        through_edge[:, (2 * n + 1) * LANES : (2 * n + 2) * LANES] = grad[:, 7 * LANES :]
        inner = slice(LANES, 7 * LANES)
        back_pre = gate_back(grad[:, inner], pre[n, :, inner], gate_in[n, :, inner], rows8, inside)
        place(placed_f, n, lambda x: back_pre[:, (x - 1) * LANES : x * LANES], 1, 6)
    raw[0] = dot_t(columns_f[...], placed_f[...])
    raw[1] = dot_t(columns_h[...], placed_s[...])


def second_edge_kernel(
    scale, codes, own, part, got_a, got_b, far_a, far_b, pre_edge, gate_edge, second_in, through_edge,
    columns_f, columns_fe, raw, w_second, w_turned, second, grads,
    low, high, columns_h, columns_b, placed_f, placed_s, place,
):
    masks = region_masks()
    inside = jnp.concatenate([masks[4].astype(F32)] * 4, axis=1)
    for f, columns in ((0, columns_h), (1, columns_b)):
        stage_edge(
            low.at[f], high.at[f], lambda s, x: own[f, s, x], lambda s, x: part[f, s, x],
            lambda which, s: (got_a, got_b)[which][f, s], lambda which, s: (far_a, far_b)[which][f, s],
        )
        edge_columns(codes, masks, low.at[f], high.at[f], columns)
    more = edge_terms(dot(w_second[...], columns_h[...]), 0)
    more_t = edge_terms(dot(w_turned[...], columns_b[...]), 0)
    zero = jnp.zeros((CH, LANES), F32)
    rows = []
    for n in range(2):
        for k in range(4):
            planes = second_in[n, :, k * 256 : (k + 1) * 256]
            if k == 0:
                planes = planes + jnp.concatenate([more[:, 2 * n * LANES : (2 * n + 1) * LANES], zero], axis=1)
            if k == 3:
                planes = planes + jnp.concatenate([zero, more[:, (2 * n + 1) * LANES : (2 * n + 2) * LANES]], axis=1)
            rows.append(planes.astype(BF))
    packed = dot(jnp.concatenate(rows, axis=0), compact_table()).astype(BF)
    for n in range(2):
        for k in range(4):
            first = (4 * n + k) * CH
            second[n * CH : (n + 1) * CH, k * LANES : (k + 1) * LANES] = packed[first : first + CH]
    back_pre = gate_back(through_edge[...] + more_t, pre_edge[...], gate_edge[...], gate_rows(), inside)
    placed_f[...] = jnp.zeros_like(placed_f)
    placed_s[...] = jnp.zeros_like(placed_s)
    for n in range(2):
        for side in range(2):
            at = (2 * n + side) * LANES
            a = 2 * side
            placed_s[a * CH : (a + 1) * CH, at : at + LANES] = own[1, n, 7 * side]
            for a in range(3):
                to = (6 * n + 3 * side + a) * LANES
                placed_f[a * CH : (a + 1) * CH, to : to + LANES] = back_pre[:, at : at + LANES]
    pieces = []
    for n in range(2):
        mid, edge = n * MID, 2 * n * LANES
        pieces += [
            columns_fe[:, edge : edge + LANES], columns_f[:, mid : mid + 2 * LANES],
            columns_f[:, mid + 6 * LANES : mid + MID], columns_fe[:, edge + LANES : edge + 2 * LANES],
        ]
    shape = (CH, LANES)
    i, c = iota(shape, 0), iota(shape, 1)
    lift = jnp.where(component_class(i) == out_class(c), jnp.where(i >= 20, 2.0, 1.0), 0.0).astype(BF)
    keep = one(component_class(i) == in_class(c), F32)
    same = one(component_index(i) == component_index(c & (CH - 1)), F32)
    place[...] = jnp.zeros_like(place)
    for a in range(3):
        for half in (0, LANES):
            place[half + a * CH : half + (a + 1) * CH, a * LANES : (a + 1) * LANES] = lift
    found = (
        raw[0] + dot_t(jnp.concatenate(pieces, axis=1), placed_f[...]),
        raw[1] + dot_t(columns_h[...], placed_s[...]),
    )
    for layer in range(2):
        masked = (found[layer].reshape(9, CH, LANES) * same).reshape(9 * CH, LANES)
        top = masked.astype(BF)
        rest = (masked - top.astype(F32)).astype(BF)
        lifted = dot(jnp.concatenate([top, rest], axis=1), place[...])
        for a in range(3):
            block = lifted[:, a * LANES : (a + 1) * LANES].reshape(9, CH, LANES) * keep
            first = 27 * layer + 9 * a
            grads[first : first + 9, :] = jnp.sum(block, axis=1) * scale
    grads[54:56, :] = jnp.zeros((2, LANES), F32)


def turn_kernel(mirror, own, across_y, across_x, across, out, staged):
    for n in range(2):
        staged[0, n * CH : (n + 1) * CH, :] = own[n * CH : (n + 1) * CH, :]
        for r, ref in ((1, across_y), (2, across_x), (3, across)):
            at = pl.multiple_of(mirror[n, r - 1] * CH, CH)
            staged[r, n * CH : (n + 1) * CH, :] = ref[pl.ds(at, CH), :] * turn_signs(r, (CH, 512))
    result = turned_sum(staged, turns_table()).astype(BF)
    for k in range(4):
        for n in range(2):
            first = (2 * k + n) * CH
            out[:, n, k * 128 : (k + 1) * 128] = result[first : first + 30]


SMEM = pl.BlockSpec(memory_space=pltpu.SMEM)
VMEM = pl.BlockSpec(memory_space=pltpu.VMEM)


def call(kernel, us, n_smem, outs, scratch, *args):
    return pl.pallas_call(
        kernel,
        out_shape=tuple(jax.ShapeDtypeStruct(s, t) for s, t in outs),
        in_specs=[SMEM] * n_smem + [VMEM] * (len(args) - n_smem),
        out_specs=tuple([VMEM] * len(outs)),
        scratch_shapes=[pltpu.VMEM(s, t) for s, t in scratch],
        compiler_params=pltpu.CompilerParams(vmem_limit_bytes=24 * 1024 * 1024),
        cost_estimate=pl.CostEstimate(flops=0, transcendentals=0, bytes_accessed=int(us * 3_000_000)),
    )(*args)


def swap_y(x):
    n = lax.axis_size("yp")
    return lax.ppermute(x, "yp", [(i, n - 1 - i) for i in range(n)])


def mirror_x(x):
    n = lax.axis_size("xp")
    return lax.ppermute(x, "xp", [(i, n - 1 - i) for i in range(n)])


def pair_swap(x, first):
    n = lax.axis_size("xp")
    pairs = []
    for i in range(first, n - 1, 2):
        pairs += [(i, i + 1), (i + 1, i)]
    return lax.ppermute(x, "xp", pairs)


def exchange(face_a, face_b):
    got_b = pair_swap(face_b, 1)
    got_a = pair_swap(face_a, 0)
    return got_a, got_b


def after(arrays, *others):
    return lax.optimization_barrier((tuple(arrays), others))[0]


def side_by_side(arrays, rows):
    total = None
    for k, x in enumerate(arrays):
        x = jnp.pad(x, ((0, rows - x.shape[0]), (k * LANES, (len(arrays) - k) * LANES - LANES + LANES - x.shape[1])))
        total = x if total is None else total + x
    return lax.optimization_barrier(total)


def on_device(features, cotangent, w_first, w_second, codes, mirror):
    plane = (CH, LANES)
    cot_x = mirror_x(cotangent)
    cot_y = swap_y(cotangent)
    fp, faces = call(
        spread_kernel, 0.2, 0, [((2, 8) + plane, BF), ((2, 2) + plane, BF)], [((64, 512), BF)], features
    )
    faces = jnp.concatenate([faces, swap_y(faces)], axis=1)
    got = exchange(faces[0], faces[1])
    part = swap_y(fp)
    w_first, w_second, codes, mirror = after((w_first, w_second, codes, mirror), part)
    w1, w2, w2t, codes, mirror = call(
        weights_kernel, 1, 0,
        [((192, 288), BF), ((96, 288), BF), ((96, 288), BF), *((x.shape, x.dtype) for x in (codes, mirror))],
        [((2, CH, LANES), F32), ((288, LANES), BF)],
        side_by_side((w_first, w_second), CH), side_by_side((codes, mirror), 2),
    )
    columns, pre, gate_in, hidden_mid = call(
        first_mid_kernel, 2, 1,
        [((288, 2 * MID), BF), ((2, CH, MID), F32), ((2, CH, MID), F32), ((2, 6) + plane, BF)],
        [((5, 8) + plane, BF)], codes, fp, part, w1,
    )
    *got, cot_x = after((*got, cot_x), hidden_mid)
    (back,) = call(
        back_kernel, 0.8, 1, [((2, 8) + plane, BF)], [((4, 64, 512), BF)], mirror, cotangent, cot_y, cot_x, swap_y(cot_x)
    )
    columns_e, pre_e, gate_e, both, face_a, face_b = call(
        first_edge_kernel, 1.2, 1,
        [
            ((288, 4 * LANES), BF), ((CH, 4 * LANES), F32), ((CH, 4 * LANES), F32), ((2, 2, 8) + plane, BF),
            ((2, 2) + plane, BF), ((2, 2) + plane, BF),
        ],
        [((9,) + plane, BF)] * 2, codes, fp, part, *got, pre, gate_in, hidden_mid, back, w1,
    )
    got = exchange(face_a, face_b)
    part = swap_y(both)
    second_part, through_e, raw = call(
        second_mid_kernel, 3.5, 1, [((2, CH, MID), F32), ((CH, 4 * LANES), F32), ((2, 288, LANES), F32)],
        [((2, 5, 8) + plane, BF), ((288, 2 * MID), BF), ((288, 2 * MID), BF), ((128, 2 * MID), BF), ((128, 2 * MID), BF)],
        codes, both, part, pre, gate_in, columns, w2, w2t,
    )
    got = after(got, raw)
    faces = (*got, swap_y(got[0]), swap_y(got[1]))
    n_bricks = features.shape[0] * lax.axis_size("xp") * lax.axis_size("yp")
    second, grads = call(
        functools.partial(second_edge_kernel, 1.0 / n_bricks), 2.8, 1, [((64, 512), BF), ((56, LANES), F32)],
        [((2, 9) + plane, BF)] * 2 + [((288, 4 * LANES), BF)] * 2
        + [((128, 12 * LANES), BF), ((128, 4 * LANES), BF), ((256, 3 * LANES), BF)],
        codes, both, part, *faces, pre_e, gate_e, second_part, through_e, columns, columns_e, raw, w2, w2t,
    )
    total = grads + swap_y(grads)
    (second,) = after((second,), total)
    second_y = swap_y(second)
    second_x = mirror_x(second)
    second_xy = swap_y(second_x)
    (denoised,) = call(
        turn_kernel, 0.9, 1, [((30, 2, 512), BF)], [((4, 64, 512), BF)], mirror, second, second_y, second_x, second_xy
    )
    denoised = denoised.transpose(1, 0, 2)
    n = lax.axis_size("xp")
    bit = 1
    while bit < n:
        total = total + lax.ppermute(total, "xp", [(i, i ^ bit) for i in range(n)])
        bit *= 2
    return denoised, total[0:27, 0:84], total[27:54, 0:84]


def solution(mesh):
    brick = P(("grp", "xp", "yp"))
    return jax.shard_map(
        on_device,
        mesh=mesh,
        in_specs=(brick, brick, P(), P(), brick, brick),
        out_specs=(brick, P("grp"), P("grp")),
        check_vma=False,
    )
```

```python
import functools

import jax
import jax.numpy as jnp
from jax import lax
from jax.experimental import pallas as pl
from jax.experimental.pallas import tpu as pltpu
from jax.sharding import PartitionSpec as P

BF = jnp.bfloat16
F32 = jnp.float32
CH = 32
LANES = 128
MID = 8 * LANES
HIGHEST = lax.Precision.HIGHEST
TURNS = (0, 63, 7 + 64, 56 + 64)


def iota(shape, dim):
    return lax.broadcasted_iota(jnp.int32, shape, dim)


def component_class(i):
    tensor = jnp.where(i < 30, 12 + ((i - 20) & 1), -1)
    return jnp.where(i < 8, i, jnp.where(i < 20, 8 + ((i - 8) & 3), tensor))


def component_index(i):
    return jnp.where(i < 8, 0, jnp.where(i < 20, (i - 8) >> 2, jnp.where(i < 30, (i - 20) >> 1, -1)))


def gate_class(i):
    tensor = jnp.where(i < 30, 4 + ((i - 20) & 1), -1)
    return jnp.where(i < 8, i, jnp.where(i < 20, (i - 8) & 3, tensor))


def out_class(c):
    tensor = jnp.where(c < 84, 12 + ((c - 80) >> 1), -2)
    return jnp.where(c < 64, c >> 3, jnp.where(c < 80, 8 + ((c - 64) >> 2), tensor))


def in_class(c):
    tensor = jnp.where(c < 84, 12 + ((c - 80) & 1), -2)
    return jnp.where(c < 64, c & 7, jnp.where(c < 80, 8 + ((c - 64) & 3), tensor))


def one(condition, kind=BF):
    return jnp.where(condition, 1.0, 0.0).astype(kind)


def plane_source(q):
    lane = q & 127
    row = (lane * 205) >> 11
    y, z = row - 1, lane - 10 * row - 1
    inside = (y >= 0) & (y < 8) & (z >= 0) & (z < 8)
    return jnp.where(inside, 64 * (q >> 7) + 8 * y + z, -1)


def spread_table():
    return one(plane_source(iota((128, 256), 1)) == iota((128, 256), 0))


def compact_table():
    return one(plane_source(iota((256, 128), 0)) == iota((256, 128), 1))


def turn_table(r):
    return one((iota((128, 128), 1) ^ TURNS[r]) == iota((128, 128), 0))


def turns_table():
    return jnp.concatenate([turn_table(r) for r in range(4)], axis=0)


def turns_spread_table():
    source = plane_source(iota((128, 256), 1))
    return jnp.concatenate([one((source ^ TURNS[r]) == iota((128, 256), 0)) for r in range(4)], axis=0)


def turn_signs(r, shape):
    i = iota(shape, 0) & (CH - 1)
    m = component_index(i)
    vector = (i >= 8) & (i < 20) & (m != r - 1)
    tensor = (i >= 20) & (m < 3) & (m != 3 - r)
    return jnp.where(vector | tensor, -1.0, 1.0).astype(BF)


def region_masks():
    lane = iota((1, LANES), 1)
    row = (lane * 205) >> 11
    col = lane - 10 * row

    def part(v):
        return jnp.where(v == 0, 0, jnp.where(v == 9, 2, 1))

    region = jnp.where(row < 10, 3 * part(row) + part(col), -1)
    return [one(region == o) for o in range(9)]


def dot(a, b, **kw):
    return jnp.dot(a, b, preferred_element_type=F32, **kw)


def dot_t(a, b):
    return lax.dot_general(a, b, (((1,), (1,)), ((), ())), preferred_element_type=F32)


def is_odd():
    return (lax.axis_index("xp") & 1) == 1


def table_row(codes, n, o, last):
    e = codes[n, o]
    d = e >> 1
    dx = lax.div(d, 3)
    other = jnp.where(d - 3 * dx == 1, 0, 2) + jnp.where(dx == 1, 0, 4)
    return jnp.where(e >= 18, last, jnp.minimum(other + (e & 1), last))


def gathered(pieces_of, masks):
    total = None
    for b in range(3):
        for c in range(3):
            o = 3 * b + c
            planes = jnp.concatenate(pieces_of(o), axis=0)
            shift = ((b - 1) * 80 + (c - 1) * 8) % LANES
            if shift:
                planes = pltpu.roll(planes, shift, 1)
            planes = planes * masks[o]
            total = planes if total is None else total + planes
    return total


def unfold(planes, count, columns, start):
    for o in range(9):
        shift = (11 - 10 * (o // 3) - o % 3) % LANES
        moved = pltpu.roll(planes, shift, 1) if shift else planes
        for p in range(count):
            at = start + p * LANES
            columns[o * CH : (o + 1) * CH, at : at + LANES] = moved[p * CH : (p + 1) * CH]


def stage_mid(table, own, part):
    zero = jnp.zeros((CH, LANES), BF)
    for x in range(8):
        for s in range(2):
            table[s, x] = own(s, x)
            table[2 + s, x] = part(s, x)
        table[4, x] = zero


def mid_columns(codes, masks, table, columns):
    for n in range(2):
        planes = gathered(lambda o: [table[table_row(codes, n, 9 + o, 4)].reshape(8 * CH, LANES)], masks)
        unfold(planes, 8, columns, n * MID)


def stage_edge(low, high, own, part, received, far):
    odd = is_odd()
    zero = jnp.zeros((CH, LANES), BF)
    for s in range(2):
        low[s], high[s] = own(s, 7), own(s, 0)
        low[2 + s], high[2 + s] = part(s, 7), part(s, 0)
        for base, faces in ((4, received), (6, far)):
            first, second = faces(0, s), faces(1, s)
            low[base + s] = jnp.where(odd, first, second)
            high[base + s] = jnp.where(odd, second, first)
    low[8] = zero
    high[8] = zero


def edge_columns(codes, masks, low, high, columns):
    def pieces(o):
        found = []
        for n in range(2):
            found += [low[table_row(codes, n, o, 8)], high[table_row(codes, n, 18 + o, 8)]]
        return found

    unfold(gathered(pieces, masks), 4, columns, 0)


def fold_mid(stacked, row):
    zero = jnp.zeros((CH, LANES), F32)
    before = jnp.concatenate([zero, stacked[row : row + CH, : MID - LANES]], axis=1)
    after = jnp.concatenate([stacked[row + 2 * CH : row + 3 * CH, LANES:], zero], axis=1)
    return before + stacked[row + CH : row + 2 * CH] + after


def edge_terms(stacked, row):
    blocks = []
    for e in range(4):
        first = row + 2 * CH * (e & 1)
        blocks.append(stacked[first : first + CH, e * LANES : (e + 1) * LANES])
    return jnp.concatenate(blocks, axis=1)


def edge_planes(ref):
    return jnp.concatenate([ref[e >> 1, :, 7 * (e & 1) * LANES : (7 * (e & 1) + 1) * LANES] for e in range(4)], axis=1)


def write_faces(face_a, face_b, index, plane_low, plane_high):
    odd = is_odd()
    face_a[index] = jnp.where(odd, plane_low, plane_high)
    face_b[index] = jnp.where(odd, plane_high, plane_low)


def spread_kernel(features, fp, staged):
    staged[...] = jnp.zeros_like(staged)
    for n in range(2):
        staged[n * CH : n * CH + 30, :] = features[n]
    rows = jnp.concatenate([staged[:, k * 128 : (k + 1) * 128] for k in range(4)], axis=0)
    planes = dot(rows, spread_table()).astype(BF)
    for n in range(2):
        for x in range(8):
            first = (x >> 1) * 2 * CH + n * CH
            fp[n, x] = planes[first : first + CH, (x & 1) * LANES : (x & 1) * LANES + LANES]


def weights_kernel(packed, small, one_out, two_out, turned_out, codes_out, mirror_out, padded, left):
    shape = (CH, LANES)
    i, c = iota(shape, 0), iota(shape, 1)
    double = jnp.where(i >= 20, 2.0, 1.0)
    j = iota((LANES, LANES), 1) & (CH - 1)
    col = iota((LANES, LANES), 0)
    by_in = one(in_class(col) == component_class(j))
    by_out = one(out_class(col) == component_class(j))
    rows_out = jnp.where(component_class(i) == out_class(c), double, 0.0)
    rows_gate = one(gate_class(i) == out_class(c), F32)
    rows_in = jnp.where(component_class(i) == in_class(c), double, 0.0)
    same = component_index(i) == component_index(c & (CH - 1))
    quarter = c >> 5
    padded[...] = jnp.zeros_like(padded)
    for which in range(2):
        padded[which, 0:27, 0:84] = packed[0:27, which * LANES : which * LANES + 84].astype(F32)
    codes_out[...] = small[:, 0:27]
    mirror_out[...] = small[:, LANES : LANES + 3]
    for which, rows, columns, blocks, out, base, flip in (
        (0, rows_out, by_in, True, one_out, 0, False),
        (0, rows_gate, by_in, False, one_out, 96, False),
        (1, rows_out, by_in, True, two_out, 0, False),
        (1, rows_in, by_out, True, turned_out, 0, True),
    ):
        for a in range(3):
            for bc in range(9):
                o = 9 * a + bc
                o = 26 - o if flip else o
                left[bc * CH : (bc + 1) * CH, :] = (rows * padded[which, o : o + 1, :]).astype(BF)
            found = dot(left[...], columns)
            for g in range(3):
                tile = jnp.zeros(shape, F32)
                for q in range(min(4, 9 - 4 * g)):
                    bc = 4 * g + q
                    keep = (quarter == q) & same if blocks else quarter == q
                    tile = tile + jnp.where(keep, found[bc * CH : (bc + 1) * CH], 0.0)
                width = min(128, 288 - 128 * g)
                out[base + a * CH : base + (a + 1) * CH, g * 128 : g * 128 + width] = tile[:, :width].astype(BF)


def first_mid_kernel(codes, own, part, w_first, columns, pre, gate_in, hidden_mid, table):
    masks = region_masks()
    inside = masks[4].astype(F32)
    stage_mid(table, lambda s, x: own[s, x], lambda s, x: part[s, x])
    mid_columns(codes, masks, table, columns)
    for n in range(2):
        stacked = dot(w_first[...], columns[:, n * MID : (n + 1) * MID])
        a, g = fold_mid(stacked, 0), fold_mid(stacked, 96)
        pre[n] = a
        gate_in[n] = g
        for x in range(1, 7):
            at = slice(x * LANES, (x + 1) * LANES)
            hidden_mid[n, x - 1] = (a[:, at] * jax.nn.sigmoid(g[:, at]) * inside).astype(BF)


def turned_sum(staged, table):
    rows = []
    for k in range(4):
        blocks = (k, k, 3 - k, 3 - k)
        rows.append(jnp.concatenate([staged[r, :, 128 * b : 128 * b + 128] for r, b in enumerate(blocks)], axis=1))
    return dot(jnp.concatenate(rows, axis=0), table) * 0.25


def back_kernel(mirror, own, across_y, crossed, back, staged):
    zero2 = jnp.zeros((2, 512), BF)
    for n in range(2):
        for r in range(4):
            if r == 0:
                value = own[n]
            else:
                slot = mirror[n, r - 1]
                value = (across_y[slot] if r == 1 else crossed[2 * (r - 2) + slot]) * turn_signs(r, (30, 512))
            staged[r, n * CH : n * CH + 30, :] = value
            staged[r, n * CH + 30 : (n + 1) * CH, :] = zero2
    planes = turned_sum(staged, turns_spread_table()).astype(BF)
    for n in range(2):
        for x in range(8):
            first = (x >> 1) * 2 * CH + n * CH
            back[n, x] = planes[first : first + CH, (x & 1) * LANES : (x & 1) * LANES + LANES]


def first_edge_kernel(
    codes, own, part, got_a, got_b, pre, gate_in, hidden_mid, back, w_first,
    columns, pre_edge, gate_edge, both, face_a, face_b, low, high,
):
    masks = region_masks()
    inside = jnp.concatenate([masks[4].astype(F32)] * 4, axis=1)
    stage_edge(
        low, high, lambda s, x: own[s, x], lambda s, x: part[s, x],
        lambda which, s: (got_a, got_b)[which][s], lambda which, s: (got_a, got_b)[which][2 + s],
    )
    edge_columns(codes, masks, low, high, columns)
    stacked = dot(w_first[...], columns[...])
    a = edge_planes(pre) + edge_terms(stacked, 0)
    g = edge_planes(gate_in) + edge_terms(stacked, 96)
    pre_edge[...] = a
    gate_edge[...] = g
    hidden = (a * jax.nn.sigmoid(g) * inside).astype(BF)
    for n in range(2):
        outer = [hidden[:, e * LANES : (e + 1) * LANES] for e in (2 * n, 2 * n + 1)]
        both[0, n, 0], both[0, n, 7] = outer
        write_faces(face_a, face_b, (0, n), *outer)
        for x in range(1, 7):
            both[0, n, x] = hidden_mid[n, x - 1]
        for x in range(8):
            both[1, n, x] = back[n, x]
        write_faces(face_a, face_b, (1, n), back[n, 0], back[n, 7])


def gate_back(grad, a, g, rows8, inside):
    sig = jax.nn.sigmoid(g)
    through = grad * sig
    extra = dot(rows8, grad * a, precision=HIGHEST)
    sig8 = sig[0:8]
    top = through[0:8] + sig8 * (1.0 - sig8) * extra
    return (jnp.concatenate([top, through[8:]], axis=0) * inside).astype(BF)


def gate_rows():
    return one(gate_class(iota((8, CH), 1)) == iota((8, CH), 0), F32)


def second_mid_kernel(
    codes, own, part, pre, gate_in, columns_f, w_second, w_turned, second, through_edge, raw,
    table, columns_h, columns_b, placed_f, placed_s,
):
    masks = region_masks()
    inside = jnp.concatenate([masks[4].astype(F32)] * 6, axis=1)
    for f, columns in ((0, columns_h), (1, columns_b)):
        stage_mid(table.at[f], lambda s, x: own[f, s, x], lambda s, x: part[f, s, x])
        mid_columns(codes, masks, table.at[f], columns)
    zero = jnp.zeros((CH, LANES), BF)
    rows8 = gate_rows()
    for placed in (placed_f, placed_s):
        placed[3 * CH :, :] = jnp.zeros((CH, 2 * MID), BF)

    def place(placed, n, planes, first, last):
        for a in range(3):
            for q in range(8):
                x = q + 1 - a
                at = (8 * n + q) * LANES
                placed[a * CH : (a + 1) * CH, at : at + LANES] = planes(x) if first <= x <= last else zero

    for n in range(2):
        here = slice(n * MID, (n + 1) * MID)
        second[n] = fold_mid(dot(w_second[...], columns_h[:, here]), 0)
        place(placed_s, n, lambda x: own[1, n, x], 0, 7)
        grad = fold_mid(dot(w_turned[...], columns_b[:, here]), 0)
        through_edge[:, 2 * n * LANES : (2 * n + 1) * LANES] = grad[:, :LANES]
        through_edge[:, (2 * n + 1) * LANES : (2 * n + 2) * LANES] = grad[:, 7 * LANES :]
        inner = slice(LANES, 7 * LANES)
        back_pre = gate_back(grad[:, inner], pre[n, :, inner], gate_in[n, :, inner], rows8, inside)
        place(placed_f, n, lambda x: back_pre[:, (x - 1) * LANES : x * LANES], 1, 6)
    raw[0] = dot_t(columns_f[...], placed_f[...])
    raw[1] = dot_t(columns_h[...], placed_s[...])


def second_edge_kernel(
    scale, codes, own, part, got_a, got_b, far_a, far_b, pre_edge, gate_edge, second_in, through_edge,
    columns_f, columns_fe, raw, w_second, w_turned, second, grads,
    low, high, columns_h, columns_b, placed_f, placed_s, place,
):
    masks = region_masks()
    inside = jnp.concatenate([masks[4].astype(F32)] * 4, axis=1)
    for f, columns in ((0, columns_h), (1, columns_b)):
        stage_edge(
            low.at[f], high.at[f], lambda s, x: own[f, s, x], lambda s, x: part[f, s, x],
            lambda which, s: (got_a, got_b)[which][f, s], lambda which, s: (far_a, far_b)[which][f, s],
        )
        edge_columns(codes, masks, low.at[f], high.at[f], columns)
    more = edge_terms(dot(w_second[...], columns_h[...]), 0)
    more_t = edge_terms(dot(w_turned[...], columns_b[...]), 0)
    zero = jnp.zeros((CH, LANES), F32)
    rows = []
    for n in range(2):
        for k in range(4):
            planes = second_in[n, :, k * 256 : (k + 1) * 256]
            if k == 0:
                planes = planes + jnp.concatenate([more[:, 2 * n * LANES : (2 * n + 1) * LANES], zero], axis=1)
            if k == 3:
                planes = planes + jnp.concatenate([zero, more[:, (2 * n + 1) * LANES : (2 * n + 2) * LANES]], axis=1)
            rows.append(planes.astype(BF))
    packed = dot(jnp.concatenate(rows, axis=0), compact_table()).astype(BF)
    for n in range(2):
        for k in range(4):
            first = (4 * n + k) * CH
            second[n * CH : (n + 1) * CH, k * LANES : (k + 1) * LANES] = packed[first : first + CH]
    back_pre = gate_back(through_edge[...] + more_t, pre_edge[...], gate_edge[...], gate_rows(), inside)
    placed_f[...] = jnp.zeros_like(placed_f)
    placed_s[...] = jnp.zeros_like(placed_s)
    for n in range(2):
        for side in range(2):
            at = (2 * n + side) * LANES
            a = 2 * side
            placed_s[a * CH : (a + 1) * CH, at : at + LANES] = own[1, n, 7 * side]
            for a in range(3):
                to = (6 * n + 3 * side + a) * LANES
                placed_f[a * CH : (a + 1) * CH, to : to + LANES] = back_pre[:, at : at + LANES]
    pieces = []
    for n in range(2):
        mid, edge = n * MID, 2 * n * LANES
        pieces += [
            columns_fe[:, edge : edge + LANES], columns_f[:, mid : mid + 2 * LANES],
            columns_f[:, mid + 6 * LANES : mid + MID], columns_fe[:, edge + LANES : edge + 2 * LANES],
        ]
    shape = (CH, LANES)
    i, c = iota(shape, 0), iota(shape, 1)
    lift = jnp.where(component_class(i) == out_class(c), jnp.where(i >= 20, 2.0, 1.0), 0.0).astype(BF)
    keep = one(component_class(i) == in_class(c), F32)
    same = one(component_index(i) == component_index(c & (CH - 1)), F32)
    place[...] = jnp.zeros_like(place)
    for a in range(3):
        for half in (0, LANES):
            place[half + a * CH : half + (a + 1) * CH, a * LANES : (a + 1) * LANES] = lift
    found = (
        raw[0] + dot_t(jnp.concatenate(pieces, axis=1), placed_f[...]),
        raw[1] + dot_t(columns_h[...], placed_s[...]),
    )
    for layer in range(2):
        masked = (found[layer].reshape(9, CH, LANES) * same).reshape(9 * CH, LANES)
        top = masked.astype(BF)
        rest = (masked - top.astype(F32)).astype(BF)
        lifted = dot(jnp.concatenate([top, rest], axis=1), place[...])
        for a in range(3):
            block = lifted[:, a * LANES : (a + 1) * LANES].reshape(9, CH, LANES) * keep
            first = 27 * layer + 9 * a
            grads[first : first + 9, :] = jnp.sum(block, axis=1) * scale
    grads[54:56, :] = jnp.zeros((2, LANES), F32)


def turn_kernel(mirror, own, across_y, across_x, across, out, staged):
    for n in range(2):
        staged[0, n * CH : (n + 1) * CH, :] = own[n * CH : (n + 1) * CH, :]
        for r, ref in ((1, across_y), (2, across_x), (3, across)):
            at = pl.multiple_of(mirror[n, r - 1] * CH, CH)
            staged[r, n * CH : (n + 1) * CH, :] = ref[pl.ds(at, CH), :] * turn_signs(r, (CH, 512))
    result = turned_sum(staged, turns_table()).astype(BF)
    for k in range(4):
        for n in range(2):
            first = (2 * k + n) * CH
            out[:, n, k * 128 : (k + 1) * 128] = result[first : first + 30]


SMEM = pl.BlockSpec(memory_space=pltpu.SMEM)
VMEM = pl.BlockSpec(memory_space=pltpu.VMEM)


def call(kernel, us, n_smem, outs, scratch, *args):
    return pl.pallas_call(
        kernel,
        out_shape=tuple(jax.ShapeDtypeStruct(s, t) for s, t in outs),
        in_specs=[SMEM] * n_smem + [VMEM] * (len(args) - n_smem),
        out_specs=tuple([VMEM] * len(outs)),
        scratch_shapes=[pltpu.VMEM(s, t) for s, t in scratch],
        compiler_params=pltpu.CompilerParams(vmem_limit_bytes=24 * 1024 * 1024),
        cost_estimate=pl.CostEstimate(flops=0, transcendentals=0, bytes_accessed=int(us * 3_000_000)),
    )(*args)


def swap_y(x):
    n = lax.axis_size("yp")
    return lax.ppermute(x, "yp", [(i, n - 1 - i) for i in range(n)])


def mirror_x(x):
    n = lax.axis_size("xp")
    return lax.ppermute(x, "xp", [(i, n - 1 - i) for i in range(n)])


def pair_swap(x, first):
    n = lax.axis_size("xp")
    pairs = []
    for i in range(first, n - 1, 2):
        pairs += [(i, i + 1), (i + 1, i)]
    return lax.ppermute(x, "xp", pairs)


def exchange(face_a, face_b):
    got_b = pair_swap(face_b, 1)
    got_a = pair_swap(face_a, 0)
    return got_a, got_b


def after(arrays, *others):
    return lax.optimization_barrier((tuple(arrays), others))[0]


def side_by_side(arrays, rows):
    total = None
    for k, x in enumerate(arrays):
        x = jnp.pad(x, ((0, rows - x.shape[0]), (k * LANES, (len(arrays) - k) * LANES - LANES + LANES - x.shape[1])))
        total = x if total is None else total + x
    return lax.optimization_barrier(total)


def on_device(features, cotangent, w_first, w_second, codes, mirror):
    plane = (CH, LANES)
    cot_y = swap_y(cotangent)
    crossed = mirror_x(jnp.concatenate([cotangent, cot_y], axis=0))
    (fp,) = call(spread_kernel, 0.2, 0, [((2, 8) + plane, BF)], [((64, 512), BF)], features)
    part = swap_y(fp)
    low, high = (jnp.concatenate([fp[:, x], part[:, x]], axis=0) for x in (0, 7))
    odd = is_odd()
    got = exchange(jnp.where(odd, low, high), jnp.where(odd, high, low))
    w_first, w_second, codes, mirror = after((w_first, w_second, codes, mirror), part)
    w1, w2, w2t, codes, mirror = call(
        weights_kernel, 1, 0,
        [((192, 288), BF), ((96, 288), BF), ((96, 288), BF), *((x.shape, x.dtype) for x in (codes, mirror))],
        [((2, CH, LANES), F32), ((288, LANES), BF)],
        side_by_side((w_first, w_second), CH), side_by_side((codes, mirror), 2),
    )
    columns, pre, gate_in, hidden_mid = call(
        first_mid_kernel, 2, 1,
        [((288, 2 * MID), BF), ((2, CH, MID), F32), ((2, CH, MID), F32), ((2, 6) + plane, BF)],
        [((5, 8) + plane, BF)], codes, fp, part, w1,
    )
    *got, crossed = after((*got, crossed), hidden_mid)
    (back,) = call(
        back_kernel, 0.8, 1, [((2, 8) + plane, BF)], [((4, 64, 512), BF)], mirror, cotangent, cot_y, crossed
    )
    columns_e, pre_e, gate_e, both, face_a, face_b = call(
        first_edge_kernel, 1.2, 1,
        [
            ((288, 4 * LANES), BF), ((CH, 4 * LANES), F32), ((CH, 4 * LANES), F32), ((2, 2, 8) + plane, BF),
            ((2, 2) + plane, BF), ((2, 2) + plane, BF),
        ],
        [((9,) + plane, BF)] * 2, codes, fp, part, *got, pre, gate_in, hidden_mid, back, w1,
    )
    got = exchange(face_a, face_b)
    part = swap_y(both)
    second_part, through_e, raw = call(
        second_mid_kernel, 3.5, 1, [((2, CH, MID), F32), ((CH, 4 * LANES), F32), ((2, 288, LANES), F32)],
        [((2, 5, 8) + plane, BF), ((288, 2 * MID), BF), ((288, 2 * MID), BF), ((128, 2 * MID), BF), ((128, 2 * MID), BF)],
        codes, both, part, pre, gate_in, columns, w2, w2t,
    )
    got = after(got, raw)
    faces = (*got, swap_y(got[0]), swap_y(got[1]))
    n_bricks = features.shape[0] * lax.axis_size("xp") * lax.axis_size("yp")
    second, grads = call(
        functools.partial(second_edge_kernel, 1.0 / n_bricks), 2.8, 1, [((64, 512), BF), ((56, LANES), F32)],
        [((2, 9) + plane, BF)] * 2 + [((288, 4 * LANES), BF)] * 2
        + [((128, 12 * LANES), BF), ((128, 4 * LANES), BF), ((256, 3 * LANES), BF)],
        codes, both, part, *faces, pre_e, gate_e, second_part, through_e, columns, columns_e, raw, w2, w2t,
    )
    total = grads + swap_y(grads)
    (second,) = after((second,), total)
    second_y = swap_y(second)
    second_x = mirror_x(second)
    second_xy = swap_y(second_x)
    (denoised,) = call(
        turn_kernel, 0.9, 1, [((30, 2, 512), BF)], [((4, 64, 512), BF)], mirror, second, second_y, second_x, second_xy
    )
    denoised = denoised.transpose(1, 0, 2)
    n = lax.axis_size("xp")
    bit = 1
    while bit < n:
        total = total + lax.ppermute(total, "xp", [(i, i ^ bit) for i in range(n)])
        bit *= 2
    return denoised, total[0:27, 0:84], total[27:54, 0:84]


def solution(mesh):
    brick = P(("grp", "xp", "yp"))
    return jax.shard_map(
        on_device,
        mesh=mesh,
        in_specs=(brick, brick, P(), P(), brick, brick),
        out_specs=(brick, P("grp"), P("grp")),
        check_vma=False,
    )
```

```python
import functools

import jax
import jax.numpy as jnp
from jax import lax
from jax.experimental import pallas as pl
from jax.experimental.pallas import tpu as pltpu
from jax.sharding import PartitionSpec as P

BF = jnp.bfloat16
F32 = jnp.float32
CH = 32
LANES = 128
MID = 8 * LANES
HIGHEST = lax.Precision.HIGHEST
TURNS = (0, 63, 7 + 64, 56 + 64)


def iota(shape, dim):
    return lax.broadcasted_iota(jnp.int32, shape, dim)


def component_class(i):
    tensor = jnp.where(i < 30, 12 + ((i - 20) & 1), -1)
    return jnp.where(i < 8, i, jnp.where(i < 20, 8 + ((i - 8) & 3), tensor))


def component_index(i):
    return jnp.where(i < 8, 0, jnp.where(i < 20, (i - 8) >> 2, jnp.where(i < 30, (i - 20) >> 1, -1)))


def gate_class(i):
    tensor = jnp.where(i < 30, 4 + ((i - 20) & 1), -1)
    return jnp.where(i < 8, i, jnp.where(i < 20, (i - 8) & 3, tensor))


def out_class(c):
    tensor = jnp.where(c < 84, 12 + ((c - 80) >> 1), -2)
    return jnp.where(c < 64, c >> 3, jnp.where(c < 80, 8 + ((c - 64) >> 2), tensor))


def in_class(c):
    tensor = jnp.where(c < 84, 12 + ((c - 80) & 1), -2)
    return jnp.where(c < 64, c & 7, jnp.where(c < 80, 8 + ((c - 64) & 3), tensor))


def one(condition, kind=BF):
    return jnp.where(condition, 1.0, 0.0).astype(kind)


def plane_source(q):
    lane = q & 127
    row = (lane * 205) >> 11
    y, z = row - 1, lane - 10 * row - 1
    inside = (y >= 0) & (y < 8) & (z >= 0) & (z < 8)
    return jnp.where(inside, 64 * (q >> 7) + 8 * y + z, -1)


def spread_table():
    return one(plane_source(iota((128, 256), 1)) == iota((128, 256), 0))


def compact_table():
    return one(plane_source(iota((256, 128), 0)) == iota((256, 128), 1))


def turn_table(r):
    return one((iota((128, 128), 1) ^ TURNS[r]) == iota((128, 128), 0))


def turns_table():
    return jnp.concatenate([turn_table(r) for r in range(4)], axis=0)


def turns_spread_table():
    source = plane_source(iota((128, 256), 1))
    return jnp.concatenate([one((source ^ TURNS[r]) == iota((128, 256), 0)) for r in range(4)], axis=0)


def turn_signs(r, shape):
    i = iota(shape, 0) & (CH - 1)
    m = component_index(i)
    vector = (i >= 8) & (i < 20) & (m != r - 1)
    tensor = (i >= 20) & (m < 3) & (m != 3 - r)
    return jnp.where(vector | tensor, -1.0, 1.0).astype(BF)


def region_masks():
    lane = iota((1, LANES), 1)
    row = (lane * 205) >> 11
    col = lane - 10 * row

    def part(v):
        return jnp.where(v == 0, 0, jnp.where(v == 9, 2, 1))

    region = jnp.where(row < 10, 3 * part(row) + part(col), -1)
    return [one(region == o) for o in range(9)]


def dot(a, b, **kw):
    return jnp.dot(a, b, preferred_element_type=F32, **kw)


def dot_t(a, b):
    return lax.dot_general(a, b, (((1,), (1,)), ((), ())), preferred_element_type=F32)


def is_odd():
    return (lax.axis_index("xp") & 1) == 1


def table_row(codes, n, o, last):
    e = codes[n, o]
    d = e >> 1
    dx = lax.div(d, 3)
    other = jnp.where(d - 3 * dx == 1, 0, 2) + jnp.where(dx == 1, 0, 4)
    return jnp.where(e >= 18, last, jnp.minimum(other + (e & 1), last))


def gathered(pieces_of, masks):
    total = None
    for b in range(3):
        for c in range(3):
            o = 3 * b + c
            planes = jnp.concatenate(pieces_of(o), axis=0)
            shift = ((b - 1) * 80 + (c - 1) * 8) % LANES
            if shift:
                planes = pltpu.roll(planes, shift, 1)
            planes = planes * masks[o]
            total = planes if total is None else total + planes
    return total


def unfold(planes, count, columns, start):
    for o in range(9):
        shift = (11 - 10 * (o // 3) - o % 3) % LANES
        moved = pltpu.roll(planes, shift, 1) if shift else planes
        for p in range(count):
            at = start + p * LANES
            columns[o * CH : (o + 1) * CH, at : at + LANES] = moved[p * CH : (p + 1) * CH]


def stage_mid(table, own, part):
    zero = jnp.zeros((CH, LANES), BF)
    for x in range(8):
        for s in range(2):
            table[s, x] = own(s, x)
            table[2 + s, x] = part(s, x)
        table[4, x] = zero


def mid_columns(codes, masks, table, columns):
    for n in range(2):
        planes = gathered(lambda o: [table[table_row(codes, n, 9 + o, 4)].reshape(8 * CH, LANES)], masks)
        unfold(planes, 8, columns, n * MID)


def stage_edge(low, high, own, part, received, far):
    odd = is_odd()
    zero = jnp.zeros((CH, LANES), BF)
    for s in range(2):
        low[s], high[s] = own(s, 7), own(s, 0)
        low[2 + s], high[2 + s] = part(s, 7), part(s, 0)
        for base, faces in ((4, received), (6, far)):
            first, second = faces(0, s), faces(1, s)
            low[base + s] = jnp.where(odd, first, second)
            high[base + s] = jnp.where(odd, second, first)
    low[8] = zero
    high[8] = zero


def edge_columns(codes, masks, low, high, columns):
    def pieces(o):
        found = []
        for n in range(2):
            found += [low[table_row(codes, n, o, 8)], high[table_row(codes, n, 18 + o, 8)]]
        return found

    unfold(gathered(pieces, masks), 4, columns, 0)


def fold_mid(stacked, row):
    zero = jnp.zeros((CH, LANES), F32)
    before = jnp.concatenate([zero, stacked[row : row + CH, : MID - LANES]], axis=1)
    after = jnp.concatenate([stacked[row + 2 * CH : row + 3 * CH, LANES:], zero], axis=1)
    return before + stacked[row + CH : row + 2 * CH] + after


def edge_terms(stacked, row):
    blocks = []
    for e in range(4):
        first = row + 2 * CH * (e & 1)
        blocks.append(stacked[first : first + CH, e * LANES : (e + 1) * LANES])
    return jnp.concatenate(blocks, axis=1)


def edge_planes(ref):
    return jnp.concatenate([ref[e >> 1, :, 7 * (e & 1) * LANES : (7 * (e & 1) + 1) * LANES] for e in range(4)], axis=1)


def write_faces(face_a, face_b, index, plane_low, plane_high):
    odd = is_odd()
    face_a[index] = jnp.where(odd, plane_low, plane_high)
    face_b[index] = jnp.where(odd, plane_high, plane_low)


def spread_kernel(features, fp, staged):
    staged[...] = jnp.zeros_like(staged)
    for n in range(2):
        staged[n * CH : n * CH + 30, :] = features[n]
    rows = jnp.concatenate([staged[:, k * 128 : (k + 1) * 128] for k in range(4)], axis=0)
    planes = dot(rows, spread_table()).astype(BF)
    for n in range(2):
        for x in range(8):
            first = (x >> 1) * 2 * CH + n * CH
            fp[n, x] = planes[first : first + CH, (x & 1) * LANES : (x & 1) * LANES + LANES]


def weights_kernel(packed, small, one_out, two_out, turned_out, codes_out, mirror_out, padded, left):
    shape = (CH, LANES)
    i, c = iota(shape, 0), iota(shape, 1)
    double = jnp.where(i >= 20, 2.0, 1.0)
    j = iota((LANES, LANES), 1) & (CH - 1)
    col = iota((LANES, LANES), 0)
    by_in = one(in_class(col) == component_class(j))
    by_out = one(out_class(col) == component_class(j))
    rows_out = jnp.where(component_class(i) == out_class(c), double, 0.0)
    rows_gate = one(gate_class(i) == out_class(c), F32)
    rows_in = jnp.where(component_class(i) == in_class(c), double, 0.0)
    same = component_index(i) == component_index(c & (CH - 1))
    quarter = c >> 5
    padded[...] = jnp.zeros_like(padded)
    for which in range(2):
        padded[which, 0:27, 0:84] = packed[0:27, which * LANES : which * LANES + 84].astype(F32)
    codes_out[...] = small[:, 0:27]
    mirror_out[...] = small[:, LANES : LANES + 3]
    for which, rows, columns, blocks, out, base, flip in (
        (0, rows_out, by_in, True, one_out, 0, False),
        (0, rows_gate, by_in, False, one_out, 96, False),
        (1, rows_out, by_in, True, two_out, 0, False),
        (1, rows_in, by_out, True, turned_out, 0, True),
    ):
        for a in range(3):
            for bc in range(9):
                o = 9 * a + bc
                o = 26 - o if flip else o
                left[bc * CH : (bc + 1) * CH, :] = (rows * padded[which, o : o + 1, :]).astype(BF)
            found = dot(left[...], columns)
            for g in range(3):
                tile = jnp.zeros(shape, F32)
                for q in range(min(4, 9 - 4 * g)):
                    bc = 4 * g + q
                    keep = (quarter == q) & same if blocks else quarter == q
                    tile = tile + jnp.where(keep, found[bc * CH : (bc + 1) * CH], 0.0)
                width = min(128, 288 - 128 * g)
                out[base + a * CH : base + (a + 1) * CH, g * 128 : g * 128 + width] = tile[:, :width].astype(BF)


def first_mid_kernel(codes, own, part, w_first, columns, pre, gate_in, hidden_mid, table):
    masks = region_masks()
    inside = masks[4].astype(F32)
    stage_mid(table, lambda s, x: own[s, x], lambda s, x: part[s, x])
    mid_columns(codes, masks, table, columns)
    for n in range(2):
        stacked = dot(w_first[...], columns[:, n * MID : (n + 1) * MID])
        a, g = fold_mid(stacked, 0), fold_mid(stacked, 96)
        pre[n] = a
        gate_in[n] = g
        for x in range(1, 7):
            at = slice(x * LANES, (x + 1) * LANES)
            hidden_mid[n, x - 1] = (a[:, at] * jax.nn.sigmoid(g[:, at]) * inside).astype(BF)


def turned_sum(staged, table):
    rows = []
    for k in range(4):
        blocks = (k, k, 3 - k, 3 - k)
        rows.append(jnp.concatenate([staged[r, :, 128 * b : 128 * b + 128] for r, b in enumerate(blocks)], axis=1))
    return dot(jnp.concatenate(rows, axis=0), table) * 0.25


def back_kernel(mirror, own, across_y, crossed, back, staged):
    zero2 = jnp.zeros((2, 512), BF)
    for n in range(2):
        for r in range(4):
            if r == 0:
                value = own[n]
            else:
                slot = mirror[n, r - 1]
                value = (across_y[slot] if r == 1 else crossed[2 * (r - 2) + slot]) * turn_signs(r, (30, 512))
            staged[r, n * CH : n * CH + 30, :] = value
            staged[r, n * CH + 30 : (n + 1) * CH, :] = zero2
    planes = turned_sum(staged, turns_spread_table()).astype(BF)
    for n in range(2):
        for x in range(8):
            first = (x >> 1) * 2 * CH + n * CH
            back[n, x] = planes[first : first + CH, (x & 1) * LANES : (x & 1) * LANES + LANES]


def first_edge_kernel(
    codes, own, part, got_a, got_b, pre, gate_in, hidden_mid, back, w_first,
    columns, pre_edge, gate_edge, both, face_a, face_b, low, high,
):
    masks = region_masks()
    inside = jnp.concatenate([masks[4].astype(F32)] * 4, axis=1)
    stage_edge(
        low, high, lambda s, x: own[s, x], lambda s, x: part[s, x],
        lambda which, s: (got_a, got_b)[which][s], lambda which, s: (got_a, got_b)[which][2 + s],
    )
    edge_columns(codes, masks, low, high, columns)
    stacked = dot(w_first[...], columns[...])
    a = edge_planes(pre) + edge_terms(stacked, 0)
    g = edge_planes(gate_in) + edge_terms(stacked, 96)
    pre_edge[...] = a
    gate_edge[...] = g
    hidden = (a * jax.nn.sigmoid(g) * inside).astype(BF)
    for n in range(2):
        outer = [hidden[:, e * LANES : (e + 1) * LANES] for e in (2 * n, 2 * n + 1)]
        both[0, n, 0], both[0, n, 7] = outer
        write_faces(face_a, face_b, (0, n), *outer)
        for x in range(1, 7):
            both[0, n, x] = hidden_mid[n, x - 1]
        for x in range(8):
            both[1, n, x] = back[n, x]
        write_faces(face_a, face_b, (1, n), back[n, 0], back[n, 7])


def gate_back(grad, a, g, rows8, inside):
    sig = jax.nn.sigmoid(g)
    through = grad * sig
    extra = dot(rows8, grad * a, precision=HIGHEST)
    sig8 = sig[0:8]
    top = through[0:8] + sig8 * (1.0 - sig8) * extra
    return (jnp.concatenate([top, through[8:]], axis=0) * inside).astype(BF)


def gate_rows():
    return one(gate_class(iota((8, CH), 1)) == iota((8, CH), 0), F32)


def second_mid_kernel(
    codes, own, part, pre, gate_in, columns_f, w_second, w_turned, second, through_edge, raw,
    table, columns_h, columns_b, placed_f, placed_s,
):
    masks = region_masks()
    inside = jnp.concatenate([masks[4].astype(F32)] * 6, axis=1)
    for f, columns in ((0, columns_h), (1, columns_b)):
        stage_mid(table.at[f], lambda s, x: own[f, s, x], lambda s, x: part[f, s, x])
        mid_columns(codes, masks, table.at[f], columns)
    zero = jnp.zeros((CH, LANES), BF)
    rows8 = gate_rows()
    for placed in (placed_f, placed_s):
        placed[3 * CH :, :] = jnp.zeros((CH, 2 * MID), BF)

    def place(placed, n, planes, first, last):
        for a in range(3):
            for q in range(8):
                x = q + 1 - a
                at = (8 * n + q) * LANES
                placed[a * CH : (a + 1) * CH, at : at + LANES] = planes(x) if first <= x <= last else zero

    for n in range(2):
        here = slice(n * MID, (n + 1) * MID)
        second[n] = fold_mid(dot(w_second[...], columns_h[:, here]), 0)
        place(placed_s, n, lambda x: own[1, n, x], 0, 7)
        grad = fold_mid(dot(w_turned[...], columns_b[:, here]), 0)
        through_edge[:, 2 * n * LANES : (2 * n + 1) * LANES] = grad[:, :LANES]
        through_edge[:, (2 * n + 1) * LANES : (2 * n + 2) * LANES] = grad[:, 7 * LANES :]
        inner = slice(LANES, 7 * LANES)
        back_pre = gate_back(grad[:, inner], pre[n, :, inner], gate_in[n, :, inner], rows8, inside)
        place(placed_f, n, lambda x: back_pre[:, (x - 1) * LANES : x * LANES], 1, 6)
    raw[0] = dot_t(columns_f[...], placed_f[...])
    raw[1] = dot_t(columns_h[...], placed_s[...])


def second_edge_kernel(
    scale, codes, own, part, got_a, got_b, far_a, far_b, pre_edge, gate_edge, through_edge,
    columns_f, columns_fe, raw, w_second, w_turned, second_edge, grads,
    low, high, columns_h, columns_b, placed_f, placed_s, place,
):
    masks = region_masks()
    inside = jnp.concatenate([masks[4].astype(F32)] * 4, axis=1)
    for f, columns in ((0, columns_h), (1, columns_b)):
        stage_edge(
            low.at[f], high.at[f], lambda s, x: own[f, s, x], lambda s, x: part[f, s, x],
            lambda which, s: (got_a, got_b)[which][f, s], lambda which, s: (far_a, far_b)[which][f, s],
        )
        edge_columns(codes, masks, low.at[f], high.at[f], columns)
    second_edge[...] = edge_terms(dot(w_second[...], columns_h[...]), 0)
    more_t = edge_terms(dot(w_turned[...], columns_b[...]), 0)
    back_pre = gate_back(through_edge[...] + more_t, pre_edge[...], gate_edge[...], gate_rows(), inside)
    placed_f[...] = jnp.zeros_like(placed_f)
    placed_s[...] = jnp.zeros_like(placed_s)
    for n in range(2):
        for side in range(2):
            at = (2 * n + side) * LANES
            a = 2 * side
            placed_s[a * CH : (a + 1) * CH, at : at + LANES] = own[1, n, 7 * side]
            for a in range(3):
                to = (6 * n + 3 * side + a) * LANES
                placed_f[a * CH : (a + 1) * CH, to : to + LANES] = back_pre[:, at : at + LANES]
    pieces = []
    for n in range(2):
        mid, edge = n * MID, 2 * n * LANES
        pieces += [
            columns_fe[:, edge : edge + LANES], columns_f[:, mid : mid + 2 * LANES],
            columns_f[:, mid + 6 * LANES : mid + MID], columns_fe[:, edge + LANES : edge + 2 * LANES],
        ]
    shape = (CH, LANES)
    i, c = iota(shape, 0), iota(shape, 1)
    lift = jnp.where(component_class(i) == out_class(c), jnp.where(i >= 20, 2.0, 1.0), 0.0).astype(BF)
    keep = one(component_class(i) == in_class(c), F32)
    same = one(component_index(i) == component_index(c & (CH - 1)), F32)
    place[...] = jnp.zeros_like(place)
    for a in range(3):
        for half in (0, LANES):
            place[half + a * CH : half + (a + 1) * CH, a * LANES : (a + 1) * LANES] = lift
    found = (
        raw[0] + dot_t(jnp.concatenate(pieces, axis=1), placed_f[...]),
        raw[1] + dot_t(columns_h[...], placed_s[...]),
    )
    for layer in range(2):
        masked = (found[layer].reshape(9, CH, LANES) * same).reshape(9 * CH, LANES)
        top = masked.astype(BF)
        rest = (masked - top.astype(F32)).astype(BF)
        lifted = dot(jnp.concatenate([top, rest], axis=1), place[...])
        for a in range(3):
            block = lifted[:, a * LANES : (a + 1) * LANES].reshape(9, CH, LANES) * keep
            first = 27 * layer + 9 * a
            grads[first : first + 9, :] = jnp.sum(block, axis=1) * scale
    grads[54:56, :] = jnp.zeros((2, LANES), F32)


def compact_kernel(second_in, more, second):
    zero = jnp.zeros((CH, LANES), F32)
    rows = []
    for n in range(2):
        for k in range(4):
            planes = second_in[n, :, k * 256 : (k + 1) * 256]
            if k == 0:
                planes = planes + jnp.concatenate([more[:, 2 * n * LANES : (2 * n + 1) * LANES], zero], axis=1)
            if k == 3:
                planes = planes + jnp.concatenate([zero, more[:, (2 * n + 1) * LANES : (2 * n + 2) * LANES]], axis=1)
            rows.append(planes.astype(BF))
    packed = dot(jnp.concatenate(rows, axis=0), compact_table()).astype(BF)
    for n in range(2):
        for k in range(4):
            first = (4 * n + k) * CH
            second[n * CH : (n + 1) * CH, k * LANES : (k + 1) * LANES] = packed[first : first + CH]


def turn_kernel(mirror, own, across_y, across_x, across, out, staged):
    for n in range(2):
        staged[0, n * CH : (n + 1) * CH, :] = own[n * CH : (n + 1) * CH, :]
        for r, ref in ((1, across_y), (2, across_x), (3, across)):
            at = pl.multiple_of(mirror[n, r - 1] * CH, CH)
            staged[r, n * CH : (n + 1) * CH, :] = ref[pl.ds(at, CH), :] * turn_signs(r, (CH, 512))
    result = turned_sum(staged, turns_table()).astype(BF)
    for k in range(4):
        for n in range(2):
            first = (2 * k + n) * CH
            out[:, n, k * 128 : (k + 1) * 128] = result[first : first + 30]


SMEM = pl.BlockSpec(memory_space=pltpu.SMEM)
VMEM = pl.BlockSpec(memory_space=pltpu.VMEM)


def call(kernel, us, n_smem, outs, scratch, *args):
    return pl.pallas_call(
        kernel,
        out_shape=tuple(jax.ShapeDtypeStruct(s, t) for s, t in outs),
        in_specs=[SMEM] * n_smem + [VMEM] * (len(args) - n_smem),
        out_specs=tuple([VMEM] * len(outs)),
        scratch_shapes=[pltpu.VMEM(s, t) for s, t in scratch],
        compiler_params=pltpu.CompilerParams(vmem_limit_bytes=24 * 1024 * 1024),
        cost_estimate=pl.CostEstimate(flops=0, transcendentals=0, bytes_accessed=int(us * 3_000_000)),
    )(*args)


def swap_y(x):
    n = lax.axis_size("yp")
    return lax.ppermute(x, "yp", [(i, n - 1 - i) for i in range(n)])


def mirror_x(x):
    n = lax.axis_size("xp")
    return lax.ppermute(x, "xp", [(i, n - 1 - i) for i in range(n)])


def pair_swap(x, first):
    n = lax.axis_size("xp")
    pairs = []
    for i in range(first, n - 1, 2):
        pairs += [(i, i + 1), (i + 1, i)]
    return lax.ppermute(x, "xp", pairs)


def exchange(face_a, face_b):
    got_b = pair_swap(face_b, 1)
    got_a = pair_swap(face_a, 0)
    return got_a, got_b


def after(arrays, *others):
    return lax.optimization_barrier((tuple(arrays), others))[0]


def side_by_side(arrays, rows):
    total = None
    for k, x in enumerate(arrays):
        x = jnp.pad(x, ((0, rows - x.shape[0]), (k * LANES, (len(arrays) - k) * LANES - LANES + LANES - x.shape[1])))
        total = x if total is None else total + x
    return lax.optimization_barrier(total)


def on_device(features, cotangent, w_first, w_second, codes, mirror):
    plane = (CH, LANES)
    cot_y = swap_y(cotangent)
    crossed = mirror_x(jnp.concatenate([cotangent, cot_y], axis=0))
    (fp,) = call(spread_kernel, 0.2, 0, [((2, 8) + plane, BF)], [((64, 512), BF)], features)
    part = swap_y(fp)
    low, high = (jnp.concatenate([fp[:, x], part[:, x]], axis=0) for x in (0, 7))
    odd = is_odd()
    got = exchange(jnp.where(odd, low, high), jnp.where(odd, high, low))
    w_first, w_second, codes, mirror = after((w_first, w_second, codes, mirror), part)
    w1, w2, w2t, codes, mirror = call(
        weights_kernel, 1, 0,
        [((192, 288), BF), ((96, 288), BF), ((96, 288), BF), *((x.shape, x.dtype) for x in (codes, mirror))],
        [((2, CH, LANES), F32), ((288, LANES), BF)],
        side_by_side((w_first, w_second), CH), side_by_side((codes, mirror), 2),
    )
    columns, pre, gate_in, hidden_mid = call(
        first_mid_kernel, 2, 1,
        [((288, 2 * MID), BF), ((2, CH, MID), F32), ((2, CH, MID), F32), ((2, 6) + plane, BF)],
        [((5, 8) + plane, BF)], codes, fp, part, w1,
    )
    (crossed,) = after((crossed,), hidden_mid)
    (back,) = call(
        back_kernel, 0.8, 1, [((2, 8) + plane, BF)], [((4, 64, 512), BF)], mirror, cotangent, cot_y, crossed
    )
    got = after(got, hidden_mid, back)
    columns_e, pre_e, gate_e, both, face_a, face_b = call(
        first_edge_kernel, 1.2, 1,
        [
            ((288, 4 * LANES), BF), ((CH, 4 * LANES), F32), ((CH, 4 * LANES), F32), ((2, 2, 8) + plane, BF),
            ((2, 2) + plane, BF), ((2, 2) + plane, BF),
        ],
        [((9,) + plane, BF)] * 2, codes, fp, part, *got, pre, gate_in, hidden_mid, back, w1,
    )
    got = exchange(face_a, face_b)
    part = swap_y(both)
    second_part, through_e, raw = call(
        second_mid_kernel, 3.5, 1, [((2, CH, MID), F32), ((CH, 4 * LANES), F32), ((2, 288, LANES), F32)],
        [((2, 5, 8) + plane, BF), ((288, 2 * MID), BF), ((288, 2 * MID), BF), ((128, 2 * MID), BF), ((128, 2 * MID), BF)],
        codes, both, part, pre, gate_in, columns, w2, w2t,
    )
    got = after(got, raw)
    faces = (*got, swap_y(got[0]), swap_y(got[1]))
    n_bricks = features.shape[0] * lax.axis_size("xp") * lax.axis_size("yp")
    second_e, grads = call(
        functools.partial(second_edge_kernel, 1.0 / n_bricks), 2, 1, [((CH, 4 * LANES), F32), ((56, LANES), F32)],
        [((2, 9) + plane, BF)] * 2 + [((288, 4 * LANES), BF)] * 2
        + [((128, 12 * LANES), BF), ((128, 4 * LANES), BF), ((256, 3 * LANES), BF)],
        codes, both, part, *faces, pre_e, gate_e, through_e, columns, columns_e, raw, w2, w2t,
    )
    total = grads + swap_y(grads)
    second_part, second_e = after((second_part, second_e), total)
    (second,) = call(compact_kernel, 0.5, 0, [((64, 512), BF)], [], second_part, second_e)
    second_y = swap_y(second)
    second_x = mirror_x(second)
    second_xy = swap_y(second_x)
    (denoised,) = call(
        turn_kernel, 0.9, 1, [((30, 2, 512), BF)], [((4, 64, 512), BF)], mirror, second, second_y, second_x, second_xy
    )
    denoised = denoised.transpose(1, 0, 2)
    n = lax.axis_size("xp")
    bit = 1
    while bit < n:
        total = total + lax.ppermute(total, "xp", [(i, i ^ bit) for i in range(n)])
        bit *= 2
    return denoised, total[0:27, 0:84], total[27:54, 0:84]


def solution(mesh):
    brick = P(("grp", "xp", "yp"))
    return jax.shard_map(
        on_device,
        mesh=mesh,
        in_specs=(brick, brick, P(), P(), brick, brick),
        out_specs=(brick, P("grp"), P("grp")),
        check_vma=False,
    )
```

```python
import functools

import jax
import jax.numpy as jnp
from jax import lax
from jax.experimental import pallas as pl
from jax.experimental.pallas import tpu as pltpu
from jax.sharding import PartitionSpec as P

BF = jnp.bfloat16
F32 = jnp.float32
CH = 32
LANES = 128
HALF = 16
MID = 8 * LANES
HIGHEST = lax.Precision.HIGHEST
TURNS = (0, 63, 7 + 64, 56 + 64)


def iota(shape, dim):
    return lax.broadcasted_iota(jnp.int32, shape, dim)


def component_class(i):
    tensor = jnp.where(i < 30, 12 + ((i - 20) & 1), -1)
    return jnp.where(i < 8, i, jnp.where(i < 20, 8 + ((i - 8) & 3), tensor))


def component_index(i):
    return jnp.where(i < 8, 0, jnp.where(i < 20, (i - 8) >> 2, jnp.where(i < 30, (i - 20) >> 1, -1)))


def gate_class(i):
    tensor = jnp.where(i < 30, 4 + ((i - 20) & 1), -1)
    return jnp.where(i < 8, i, jnp.where(i < 20, (i - 8) & 3, tensor))


def out_class(c):
    tensor = jnp.where(c < 84, 12 + ((c - 80) >> 1), -2)
    return jnp.where(c < 64, c >> 3, jnp.where(c < 80, 8 + ((c - 64) >> 2), tensor))


def in_class(c):
    tensor = jnp.where(c < 84, 12 + ((c - 80) & 1), -2)
    return jnp.where(c < 64, c & 7, jnp.where(c < 80, 8 + ((c - 64) & 3), tensor))


def one(condition, kind=BF):
    return jnp.where(condition, 1.0, 0.0).astype(kind)


def plane_source(q):
    lane = q & 127
    row = (lane * 205) >> 11
    y, z = row - 1, lane - 10 * row - 1
    inside = (y >= 0) & (y < 8) & (z >= 0) & (z < 8)
    return jnp.where(inside, 64 * (q >> 7) + 8 * y + z, -1)


def spread_table():
    return one(plane_source(iota((128, 256), 1)) == iota((128, 256), 0))


def compact_table():
    return one(plane_source(iota((256, 128), 0)) == iota((256, 128), 1))


def turn_table(r):
    return one((iota((128, 128), 1) ^ TURNS[r]) == iota((128, 128), 0))


def turns_table():
    return jnp.concatenate([turn_table(r) for r in range(4)], axis=0)


def turns_spread_table():
    source = plane_source(iota((128, 256), 1))
    return jnp.concatenate([one((source ^ TURNS[r]) == iota((128, 256), 0)) for r in range(4)], axis=0)


def turn_signs(r, shape):
    i = iota(shape, 0) & (CH - 1)
    m = component_index(i)
    vector = (i >= 8) & (i < 20) & (m != r - 1)
    tensor = (i >= 20) & (m < 3) & (m != 3 - r)
    return jnp.where(vector | tensor, -1.0, 1.0).astype(BF)


def region_masks():
    lane = iota((1, LANES), 1)
    row = (lane * 205) >> 11
    col = lane - 10 * row

    def part(v):
        return jnp.where(v == 0, 0, jnp.where(v == 9, 2, 1))

    region = jnp.where(row < 10, 3 * part(row) + part(col), -1)
    return [one(region == o) for o in range(9)]


def dot(a, b, **kw):
    return jnp.dot(a, b, preferred_element_type=F32, **kw)


def dot_t(a, b):
    return lax.dot_general(a, b, (((1,), (1,)), ((), ())), preferred_element_type=F32)


def is_odd():
    return (lax.axis_index("xp") & 1) == 1


def table_row(codes, n, o, last):
    e = codes[n, o]
    d = e >> 1
    dx = lax.div(d, 3)
    other = jnp.where(d - 3 * dx == 1, 0, 2) + jnp.where(dx == 1, 0, 4)
    return jnp.where(e >= 18, last, jnp.minimum(other + (e & 1), last))


def gathered(pieces_of, masks):
    total = None
    for b in range(3):
        for c in range(3):
            o = 3 * b + c
            planes = jnp.concatenate(pieces_of(o), axis=0)
            shift = ((b - 1) * 80 + (c - 1) * 8) % LANES
            if shift:
                planes = pltpu.roll(planes, shift, 1)
            planes = planes * masks[o]
            total = planes if total is None else total + planes
    return total


def unfold(planes, count, columns, start):
    for o in range(9):
        shift = (11 - 10 * (o // 3) - o % 3) % LANES
        moved = pltpu.roll(planes, shift, 1) if shift else planes
        for p in range(count):
            at = start + p * LANES
            columns[o * CH : (o + 1) * CH, at : at + LANES] = moved[p * CH : (p + 1) * CH]


def stage_mid(table, own, part):
    zero = jnp.zeros((CH, LANES), BF)
    for x in range(8):
        for s in range(2):
            table[s, x] = own(s, x)
            table[2 + s, x] = part(s, x)
        table[4, x] = zero


def mid_columns(codes, masks, table, columns):
    for n in range(2):
        planes = gathered(lambda o: [table[table_row(codes, n, 9 + o, 4)].reshape(8 * CH, LANES)], masks)
        unfold(planes, 8, columns, n * MID)


def edge_planes_of(own, part, received, far):
    odd = is_odd()
    low = [f(s, 7) for f in (own, part) for s in range(2)]
    high = [f(s, 0) for f in (own, part) for s in range(2)]
    for faces in (received, far):
        for s in range(2):
            first, second = faces(0, s), faces(1, s)
            low.append(jnp.where(odd, first, second))
            high.append(jnp.where(odd, second, first))
    return [[plane.reshape(2, HALF, LANES) for plane in side] for side in (low, high)]


def edge_columns(choose, masks, candidates, columns):
    def pieces(o):
        found = []
        for e in range(4):
            total = None
            for r, plane in enumerate(candidates[e & 1]):
                term = plane * choose[8 * (9 * e + o) + r]
                total = term if total is None else total + term
            found.append(total.reshape(CH, LANES))
        return found

    unfold(gathered(pieces, masks), 4, columns, 0)


def write_choices(codes, mirror, choose, turn_choice):
    d = codes >> 1
    dx = (d * 11) >> 5
    other = jnp.where(d - 3 * dx == 1, 0, 2) + jnp.where(dx == 1, 0, 4)
    row = jnp.where(codes >= 18, -1, other + (codes & 1))
    shape = (HALF, LANES)
    for e in range(4):
        n = e >> 1
        for o in range(9):
            at = o + 18 * (e & 1)
            wide = jnp.broadcast_to(row[n : n + 1, at : at + 1], shape)
            for r in range(8):
                choose[8 * (9 * e + o) + r] = one(wide == r)
    for n in range(2):
        for r in range(3):
            wide = jnp.broadcast_to(mirror[n : n + 1, r : r + 1], shape)
            turn_choice[3 * n + r] = wide.astype(F32).astype(BF)


def chosen(turn_choice, n, r, first, second):
    tile = jnp.concatenate([turn_choice[3 * n + r - 1]] * 4, axis=1)
    slot = jnp.concatenate([tile, tile], axis=0)[: first.shape[0]]
    return second * slot + first * (1.0 - slot).astype(BF)


def fold_mid(stacked, row):
    zero = jnp.zeros((CH, LANES), F32)
    before = jnp.concatenate([zero, stacked[row : row + CH, : MID - LANES]], axis=1)
    after = jnp.concatenate([stacked[row + 2 * CH : row + 3 * CH, LANES:], zero], axis=1)
    return before + stacked[row + CH : row + 2 * CH] + after


def edge_terms(stacked, row):
    blocks = []
    for e in range(4):
        first = row + 2 * CH * (e & 1)
        blocks.append(stacked[first : first + CH, e * LANES : (e + 1) * LANES])
    return jnp.concatenate(blocks, axis=1)


def edge_planes(ref):
    return jnp.concatenate([ref[e >> 1, :, 7 * (e & 1) * LANES : (7 * (e & 1) + 1) * LANES] for e in range(4)], axis=1)


def write_faces(face_a, face_b, index, plane_low, plane_high):
    odd = is_odd()
    face_a[index] = jnp.where(odd, plane_low, plane_high)
    face_b[index] = jnp.where(odd, plane_high, plane_low)


def spread_kernel(features, fp, staged):
    staged[...] = jnp.zeros_like(staged)
    for n in range(2):
        staged[n * CH : n * CH + 30, :] = features[n]
    rows = jnp.concatenate([staged[:, k * 128 : (k + 1) * 128] for k in range(4)], axis=0)
    planes = dot(rows, spread_table()).astype(BF)
    for n in range(2):
        for x in range(8):
            first = (x >> 1) * 2 * CH + n * CH
            fp[n, x] = planes[first : first + CH, (x & 1) * LANES : (x & 1) * LANES + LANES]


def weights_kernel(packed, small, one_out, two_out, turned_out, codes_out, choose, turn_choice, padded, left):
    shape = (CH, LANES)
    i, c = iota(shape, 0), iota(shape, 1)
    double = jnp.where(i >= 20, 2.0, 1.0)
    j = iota((LANES, LANES), 1) & (CH - 1)
    col = iota((LANES, LANES), 0)
    by_in = one(in_class(col) == component_class(j))
    by_out = one(out_class(col) == component_class(j))
    rows_out = jnp.where(component_class(i) == out_class(c), double, 0.0)
    rows_gate = one(gate_class(i) == out_class(c), F32)
    rows_in = jnp.where(component_class(i) == in_class(c), double, 0.0)
    same = component_index(i) == component_index(c & (CH - 1))
    quarter = c >> 5
    padded[...] = jnp.zeros_like(padded)
    for which in range(2):
        padded[which, 0:27, 0:84] = packed[0:27, which * LANES : which * LANES + 84].astype(F32)
    codes_out[...] = small[:, 0:27]
    write_choices(small[:, 0:LANES], small[:, LANES : 2 * LANES], choose, turn_choice)
    for which, rows, columns, blocks, out, base, flip in (
        (0, rows_out, by_in, True, one_out, 0, False),
        (0, rows_gate, by_in, False, one_out, 96, False),
        (1, rows_out, by_in, True, two_out, 0, False),
        (1, rows_in, by_out, True, turned_out, 0, True),
    ):
        for a in range(3):
            for bc in range(9):
                o = 9 * a + bc
                o = 26 - o if flip else o
                left[bc * CH : (bc + 1) * CH, :] = (rows * padded[which, o : o + 1, :]).astype(BF)
            found = dot(left[...], columns)
            for g in range(3):
                tile = jnp.zeros(shape, F32)
                for q in range(min(4, 9 - 4 * g)):
                    bc = 4 * g + q
                    keep = (quarter == q) & same if blocks else quarter == q
                    tile = tile + jnp.where(keep, found[bc * CH : (bc + 1) * CH], 0.0)
                width = min(128, 288 - 128 * g)
                out[base + a * CH : base + (a + 1) * CH, g * 128 : g * 128 + width] = tile[:, :width].astype(BF)


def first_mid_kernel(codes, own, part, w_first, columns, pre, gate_in, hidden_mid, table):
    masks = region_masks()
    inside = masks[4].astype(F32)
    stage_mid(table, lambda s, x: own[s, x], lambda s, x: part[s, x])
    mid_columns(codes, masks, table, columns)
    for n in range(2):
        stacked = dot(w_first[...], columns[:, n * MID : (n + 1) * MID])
        a, g = fold_mid(stacked, 0), fold_mid(stacked, 96)
        pre[n] = a
        gate_in[n] = g
        for x in range(1, 7):
            at = slice(x * LANES, (x + 1) * LANES)
            hidden_mid[n, x - 1] = (a[:, at] * jax.nn.sigmoid(g[:, at]) * inside).astype(BF)


def turned_sum(staged, table):
    rows = []
    for k in range(4):
        blocks = (k, k, 3 - k, 3 - k)
        rows.append(jnp.concatenate([staged[r, :, 128 * b : 128 * b + 128] for r, b in enumerate(blocks)], axis=1))
    return dot(jnp.concatenate(rows, axis=0), table) * 0.25


def back_kernel(turn_choice, own, across_y, crossed, back, staged):
    zero2 = jnp.zeros((2, 512), BF)
    for n in range(2):
        for r in range(4):
            if r == 0:
                value = own[n]
            else:
                first, second = (across_y[0], across_y[1]) if r == 1 else (crossed[2 * r - 4], crossed[2 * r - 3])
                value = chosen(turn_choice, n, r, first, second) * turn_signs(r, (30, 512))
            staged[r, n * CH : n * CH + 30, :] = value
            staged[r, n * CH + 30 : (n + 1) * CH, :] = zero2
    planes = turned_sum(staged, turns_spread_table()).astype(BF)
    for n in range(2):
        for x in range(8):
            first = (x >> 1) * 2 * CH + n * CH
            back[n, x] = planes[first : first + CH, (x & 1) * LANES : (x & 1) * LANES + LANES]


def first_edge_kernel(
    choose, own, part, got_a, got_b, pre, gate_in, hidden_mid, back, w_first,
    columns, pre_edge, gate_edge, both, face_a, face_b,
):
    masks = region_masks()
    inside = jnp.concatenate([masks[4].astype(F32)] * 4, axis=1)
    candidates = edge_planes_of(
        lambda s, x: own[s, x], lambda s, x: part[s, x],
        lambda which, s: (got_a, got_b)[which][s], lambda which, s: (got_a, got_b)[which][2 + s],
    )
    edge_columns(choose, masks, candidates, columns)
    stacked = dot(w_first[...], columns[...])
    a = edge_planes(pre) + edge_terms(stacked, 0)
    g = edge_planes(gate_in) + edge_terms(stacked, 96)
    pre_edge[...] = a
    gate_edge[...] = g
    hidden = (a * jax.nn.sigmoid(g) * inside).astype(BF)
    for n in range(2):
        outer = [hidden[:, e * LANES : (e + 1) * LANES] for e in (2 * n, 2 * n + 1)]
        both[0, n, 0], both[0, n, 7] = outer
        write_faces(face_a, face_b, (0, n), *outer)
        for x in range(1, 7):
            both[0, n, x] = hidden_mid[n, x - 1]
        for x in range(8):
            both[1, n, x] = back[n, x]
        write_faces(face_a, face_b, (1, n), back[n, 0], back[n, 7])


def gate_back(grad, a, g, rows8, inside):
    sig = jax.nn.sigmoid(g)
    through = grad * sig
    extra = dot(rows8, grad * a, precision=HIGHEST)
    sig8 = sig[0:8]
    top = through[0:8] + sig8 * (1.0 - sig8) * extra
    return (jnp.concatenate([top, through[8:]], axis=0) * inside).astype(BF)


def gate_rows():
    return one(gate_class(iota((8, CH), 1)) == iota((8, CH), 0), F32)


def second_mid_kernel(
    codes, own, part, pre, gate_in, columns_f, w_second, w_turned, second, through_edge, raw,
    table, columns_h, columns_b, placed_f, placed_s,
):
    masks = region_masks()
    inside = jnp.concatenate([masks[4].astype(F32)] * 6, axis=1)
    for f, columns in ((0, columns_h), (1, columns_b)):
        stage_mid(table.at[f], lambda s, x: own[f, s, x], lambda s, x: part[f, s, x])
        mid_columns(codes, masks, table.at[f], columns)
    zero = jnp.zeros((CH, LANES), BF)
    rows8 = gate_rows()
    for placed in (placed_f, placed_s):
        placed[3 * CH :, :] = jnp.zeros((CH, 2 * MID), BF)

    def place(placed, n, planes, first, last):
        for a in range(3):
            for q in range(8):
                x = q + 1 - a
                at = (8 * n + q) * LANES
                placed[a * CH : (a + 1) * CH, at : at + LANES] = planes(x) if first <= x <= last else zero

    for n in range(2):
        here = slice(n * MID, (n + 1) * MID)
        second[n] = fold_mid(dot(w_second[...], columns_h[:, here]), 0)
        place(placed_s, n, lambda x: own[1, n, x], 0, 7)
        grad = fold_mid(dot(w_turned[...], columns_b[:, here]), 0)
        through_edge[:, 2 * n * LANES : (2 * n + 1) * LANES] = grad[:, :LANES]
        through_edge[:, (2 * n + 1) * LANES : (2 * n + 2) * LANES] = grad[:, 7 * LANES :]
        inner = slice(LANES, 7 * LANES)
        back_pre = gate_back(grad[:, inner], pre[n, :, inner], gate_in[n, :, inner], rows8, inside)
        place(placed_f, n, lambda x: back_pre[:, (x - 1) * LANES : x * LANES], 1, 6)
    raw[0] = dot_t(columns_f[...], placed_f[...])
    raw[1] = dot_t(columns_h[...], placed_s[...])


def second_edge_kernel(
    scale, choose, own, part, got_a, got_b, far_a, far_b, pre_edge, gate_edge, through_edge,
    columns_f, columns_fe, raw, w_second, w_turned, second_edge, grads,
    columns_h, columns_b, placed_f, placed_s, place,
):
    masks = region_masks()
    inside = jnp.concatenate([masks[4].astype(F32)] * 4, axis=1)
    for f, columns in ((0, columns_h), (1, columns_b)):
        candidates = edge_planes_of(
            lambda s, x: own[f, s, x], lambda s, x: part[f, s, x],
            lambda which, s: (got_a, got_b)[which][f, s], lambda which, s: (far_a, far_b)[which][f, s],
        )
        edge_columns(choose, masks, candidates, columns)
    second_edge[...] = edge_terms(dot(w_second[...], columns_h[...]), 0)
    more_t = edge_terms(dot(w_turned[...], columns_b[...]), 0)
    back_pre = gate_back(through_edge[...] + more_t, pre_edge[...], gate_edge[...], gate_rows(), inside)
    placed_f[...] = jnp.zeros_like(placed_f)
    placed_s[...] = jnp.zeros_like(placed_s)
    for n in range(2):
        for side in range(2):
            at = (2 * n + side) * LANES
            a = 2 * side
            placed_s[a * CH : (a + 1) * CH, at : at + LANES] = own[1, n, 7 * side]
            for a in range(3):
                to = (6 * n + 3 * side + a) * LANES
                placed_f[a * CH : (a + 1) * CH, to : to + LANES] = back_pre[:, at : at + LANES]
    pieces = []
    for n in range(2):
        mid, edge = n * MID, 2 * n * LANES
        pieces += [
            columns_fe[:, edge : edge + LANES], columns_f[:, mid : mid + 2 * LANES],
            columns_f[:, mid + 6 * LANES : mid + MID], columns_fe[:, edge + LANES : edge + 2 * LANES],
        ]
    shape = (CH, LANES)
    i, c = iota(shape, 0), iota(shape, 1)
    lift = jnp.where(component_class(i) == out_class(c), jnp.where(i >= 20, 2.0, 1.0), 0.0).astype(BF)
    keep = one(component_class(i) == in_class(c), F32)
    same = one(component_index(i) == component_index(c & (CH - 1)), F32)
    place[...] = jnp.zeros_like(place)
    for a in range(3):
        for half in (0, LANES):
            place[half + a * CH : half + (a + 1) * CH, a * LANES : (a + 1) * LANES] = lift
    found = (
        raw[0] + dot_t(jnp.concatenate(pieces, axis=1), placed_f[...]),
        raw[1] + dot_t(columns_h[...], placed_s[...]),
    )
    for layer in range(2):
        masked = (found[layer].reshape(9, CH, LANES) * same).reshape(9 * CH, LANES)
        top = masked.astype(BF)
        rest = (masked - top.astype(F32)).astype(BF)
        lifted = dot(jnp.concatenate([top, rest], axis=1), place[...])
        for a in range(3):
            block = lifted[:, a * LANES : (a + 1) * LANES].reshape(9, CH, LANES) * keep
            first = 27 * layer + 9 * a
            grads[first : first + 9, :] = jnp.sum(block, axis=1) * scale
    grads[54:56, :] = jnp.zeros((2, LANES), F32)


def compact_kernel(second_in, more, second):
    zero = jnp.zeros((CH, LANES), F32)
    rows = []
    for n in range(2):
        for k in range(4):
            planes = second_in[n, :, k * 256 : (k + 1) * 256]
            if k == 0:
                planes = planes + jnp.concatenate([more[:, 2 * n * LANES : (2 * n + 1) * LANES], zero], axis=1)
            if k == 3:
                planes = planes + jnp.concatenate([zero, more[:, (2 * n + 1) * LANES : (2 * n + 2) * LANES]], axis=1)
            rows.append(planes.astype(BF))
    packed = dot(jnp.concatenate(rows, axis=0), compact_table()).astype(BF)
    for n in range(2):
        for k in range(4):
            first = (4 * n + k) * CH
            second[n * CH : (n + 1) * CH, k * LANES : (k + 1) * LANES] = packed[first : first + CH]


def turn_kernel(turn_choice, own, across_y, across_x, across, out, staged):
    for n in range(2):
        staged[0, n * CH : (n + 1) * CH, :] = own[n * CH : (n + 1) * CH, :]
        for r, ref in ((1, across_y), (2, across_x), (3, across)):
            value = chosen(turn_choice, n, r, ref[0:CH, :], ref[CH : 2 * CH, :])
            staged[r, n * CH : (n + 1) * CH, :] = value * turn_signs(r, (CH, 512))
    result = turned_sum(staged, turns_table()).astype(BF)
    for k in range(4):
        for n in range(2):
            first = (2 * k + n) * CH
            out[:, n, k * 128 : (k + 1) * 128] = result[first : first + 30]


SMEM = pl.BlockSpec(memory_space=pltpu.SMEM)
VMEM = pl.BlockSpec(memory_space=pltpu.VMEM)


def call(kernel, us, n_smem, outs, scratch, *args):
    return pl.pallas_call(
        kernel,
        out_shape=tuple(jax.ShapeDtypeStruct(s, t) for s, t in outs),
        in_specs=[SMEM] * n_smem + [VMEM] * (len(args) - n_smem),
        out_specs=tuple([VMEM] * len(outs)),
        scratch_shapes=[pltpu.VMEM(s, t) for s, t in scratch],
        compiler_params=pltpu.CompilerParams(vmem_limit_bytes=24 * 1024 * 1024),
        cost_estimate=pl.CostEstimate(flops=0, transcendentals=0, bytes_accessed=int(us * 3_000_000)),
    )(*args)


def swap_y(x):
    n = lax.axis_size("yp")
    return lax.ppermute(x, "yp", [(i, n - 1 - i) for i in range(n)])


def mirror_x(x):
    n = lax.axis_size("xp")
    return lax.ppermute(x, "xp", [(i, n - 1 - i) for i in range(n)])


def pair_swap(x, first):
    n = lax.axis_size("xp")
    pairs = []
    for i in range(first, n - 1, 2):
        pairs += [(i, i + 1), (i + 1, i)]
    return lax.ppermute(x, "xp", pairs)


def exchange(face_a, face_b):
    got_b = pair_swap(face_b, 1)
    got_a = pair_swap(face_a, 0)
    return got_a, got_b


def after(arrays, *others):
    return lax.optimization_barrier((tuple(arrays), others))[0]


def side_by_side(arrays, rows):
    total = None
    for k, x in enumerate(arrays):
        x = jnp.pad(x, ((0, rows - x.shape[0]), (k * LANES, (len(arrays) - k) * LANES - LANES + LANES - x.shape[1])))
        total = x if total is None else total + x
    return lax.optimization_barrier(total)


def on_device(features, cotangent, w_first, w_second, codes, mirror):
    plane = (CH, LANES)
    cot_y = swap_y(cotangent)
    crossed = mirror_x(jnp.concatenate([cotangent, cot_y], axis=0))
    (fp,) = call(spread_kernel, 0.2, 0, [((2, 8) + plane, BF)], [((64, 512), BF)], features)
    part = swap_y(fp)
    low, high = (jnp.concatenate([fp[:, x], part[:, x]], axis=0) for x in (0, 7))
    odd = is_odd()
    got = exchange(jnp.where(odd, low, high), jnp.where(odd, high, low))
    w_first, w_second, codes, mirror = after((w_first, w_second, codes, mirror), part)
    w1, w2, w2t, codes, choose, turn_choice = call(
        weights_kernel, 1, 0,
        [
            ((192, 288), BF), ((96, 288), BF), ((96, 288), BF), (codes.shape, codes.dtype),
            ((288, HALF, LANES), BF), ((6, HALF, LANES), BF),
        ],
        [((2, CH, LANES), F32), ((288, LANES), BF)],
        side_by_side((w_first, w_second), CH), side_by_side((codes, mirror), 2),
    )
    columns, pre, gate_in, hidden_mid = call(
        first_mid_kernel, 2, 1,
        [((288, 2 * MID), BF), ((2, CH, MID), F32), ((2, CH, MID), F32), ((2, 6) + plane, BF)],
        [((5, 8) + plane, BF)], codes, fp, part, w1,
    )
    (crossed,) = after((crossed,), hidden_mid)
    (back,) = call(
        back_kernel, 0.8, 0, [((2, 8) + plane, BF)], [((4, 64, 512), BF)], turn_choice, cotangent, cot_y, crossed
    )
    got = after(got, hidden_mid, back)
    columns_e, pre_e, gate_e, both, face_a, face_b = call(
        first_edge_kernel, 1, 0,
        [
            ((288, 4 * LANES), BF), ((CH, 4 * LANES), F32), ((CH, 4 * LANES), F32), ((2, 2, 8) + plane, BF),
            ((2, 2) + plane, BF), ((2, 2) + plane, BF),
        ],
        [], choose, fp, part, *got, pre, gate_in, hidden_mid, back, w1,
    )
    got = exchange(face_a, face_b)
    part = swap_y(both)
    second_part, through_e, raw = call(
        second_mid_kernel, 3.5, 1, [((2, CH, MID), F32), ((CH, 4 * LANES), F32), ((2, 288, LANES), F32)],
        [((2, 5, 8) + plane, BF), ((288, 2 * MID), BF), ((288, 2 * MID), BF), ((128, 2 * MID), BF), ((128, 2 * MID), BF)],
        codes, both, part, pre, gate_in, columns, w2, w2t,
    )
    got = after(got, raw)
    faces = (*got, swap_y(got[0]), swap_y(got[1]))
    n_bricks = features.shape[0] * lax.axis_size("xp") * lax.axis_size("yp")
    second_e, grads = call(
        functools.partial(second_edge_kernel, 1.0 / n_bricks), 2, 0, [((CH, 4 * LANES), F32), ((56, LANES), F32)],
        [((288, 4 * LANES), BF)] * 2
        + [((128, 12 * LANES), BF), ((128, 4 * LANES), BF), ((256, 3 * LANES), BF)],
        choose, both, part, *faces, pre_e, gate_e, through_e, columns, columns_e, raw, w2, w2t,
    )
    total = grads + swap_y(grads)
    second_part, second_e = after((second_part, second_e), total)
    (second,) = call(compact_kernel, 0.5, 0, [((64, 512), BF)], [], second_part, second_e)
    second_y = swap_y(second)
    second_x = mirror_x(second)
    second_xy = swap_y(second_x)
    (denoised,) = call(
        turn_kernel, 0.9, 0, [((30, 2, 512), BF)], [((4, 64, 512), BF)], turn_choice, second, second_y, second_x, second_xy
    )
    denoised = denoised.transpose(1, 0, 2)
    n = lax.axis_size("xp")
    bit = 1
    while bit < n:
        total = total + lax.ppermute(total, "xp", [(i, i ^ bit) for i in range(n)])
        bit *= 2
    return denoised, total[0:27, 0:84], total[27:54, 0:84]


def solution(mesh):
    brick = P(("grp", "xp", "yp"))
    return jax.shard_map(
        on_device,
        mesh=mesh,
        in_specs=(brick, brick, P(), P(), brick, brick),
        out_specs=(brick, P("grp"), P("grp")),
        check_vma=False,
    )
```

```python
import functools

import jax
import jax.numpy as jnp
from jax import lax
from jax.experimental import pallas as pl
from jax.experimental.pallas import tpu as pltpu
from jax.sharding import PartitionSpec as P

BF = jnp.bfloat16
F32 = jnp.float32
CH = 32
LANES = 128
HALF = 16
MID = 8 * LANES
TURNS = (0, 63, 7 + 64, 56 + 64)


def iota(shape, dim):
    return lax.broadcasted_iota(jnp.int32, shape, dim)


def component_class(i):
    tensor = jnp.where(i < 30, 12 + ((i - 20) & 1), -1)
    return jnp.where(i < 8, i, jnp.where(i < 20, 8 + ((i - 8) & 3), tensor))


def component_index(i):
    return jnp.where(i < 8, 0, jnp.where(i < 20, (i - 8) >> 2, jnp.where(i < 30, (i - 20) >> 1, -1)))


def gate_class(i):
    tensor = jnp.where(i < 30, 4 + ((i - 20) & 1), -1)
    return jnp.where(i < 8, i, jnp.where(i < 20, (i - 8) & 3, tensor))


def out_class(c):
    tensor = jnp.where(c < 84, 12 + ((c - 80) >> 1), -2)
    return jnp.where(c < 64, c >> 3, jnp.where(c < 80, 8 + ((c - 64) >> 2), tensor))


def in_class(c):
    tensor = jnp.where(c < 84, 12 + ((c - 80) & 1), -2)
    return jnp.where(c < 64, c & 7, jnp.where(c < 80, 8 + ((c - 64) & 3), tensor))


def one(condition, kind=BF):
    return jnp.where(condition, 1.0, 0.0).astype(kind)


def plane_source(q):
    lane = q & 127
    row = (lane * 205) >> 11
    y, z = row - 1, lane - 10 * row - 1
    inside = (y >= 0) & (y < 8) & (z >= 0) & (z < 8)
    return jnp.where(inside, 64 * (q >> 7) + 8 * y + z, -1)


def spread_table():
    return one(plane_source(iota((128, 256), 1)) == iota((128, 256), 0))


def compact_table():
    return one(plane_source(iota((256, 128), 0)) == iota((256, 128), 1))


def turn_table(r):
    return one((iota((128, 128), 1) ^ TURNS[r]) == iota((128, 128), 0))


def turns_table():
    return jnp.concatenate([turn_table(r) for r in range(4)], axis=0)


def turns_spread_table():
    source = plane_source(iota((128, 256), 1))
    return jnp.concatenate([one((source ^ TURNS[r]) == iota((128, 256), 0)) for r in range(4)], axis=0)


def turn_signs(r, shape):
    i = iota(shape, 0) & (CH - 1)
    m = component_index(i)
    vector = (i >= 8) & (i < 20) & (m != r - 1)
    tensor = (i >= 20) & (m < 3) & (m != 3 - r)
    return jnp.where(vector | tensor, -1.0, 1.0).astype(BF)


def region_masks():
    lane = iota((1, LANES), 1)
    row = (lane * 205) >> 11
    col = lane - 10 * row

    def part(v):
        return jnp.where(v == 0, 0, jnp.where(v == 9, 2, 1))

    region = jnp.where(row < 10, 3 * part(row) + part(col), -1)
    return [one(region == o) for o in range(9)]


def dot(a, b, **kw):
    return jnp.dot(a, b, preferred_element_type=F32, **kw)


def dot_t(a, b):
    return lax.dot_general(a, b, (((1,), (1,)), ((), ())), preferred_element_type=F32)


def is_odd():
    return (lax.axis_index("xp") & 1) == 1


def table_row(codes, n, o, last):
    e = codes[n, o]
    d = e >> 1
    dx = lax.div(d, 3)
    other = jnp.where(d - 3 * dx == 1, 0, 2) + jnp.where(dx == 1, 0, 4)
    return jnp.where(e >= 18, last, jnp.minimum(other + (e & 1), last))


def gathered(pieces_of, masks):
    total = None
    for b in range(3):
        for c in range(3):
            o = 3 * b + c
            planes = jnp.concatenate(pieces_of(o), axis=0)
            shift = ((b - 1) * 80 + (c - 1) * 8) % LANES
            if shift:
                planes = pltpu.roll(planes, shift, 1)
            planes = planes * masks[o]
            total = planes if total is None else total + planes
    return total


def unfold(planes, count, columns, start):
    for o in range(9):
        shift = (11 - 10 * (o // 3) - o % 3) % LANES
        moved = pltpu.roll(planes, shift, 1) if shift else planes
        for p in range(count):
            at = start + p * LANES
            columns[o * CH : (o + 1) * CH, at : at + LANES] = moved[p * CH : (p + 1) * CH]


def stage_mid(table, own, part):
    zero = jnp.zeros((CH, LANES), BF)
    for x in range(8):
        for s in range(2):
            table[s, x] = own(s, x)
            table[2 + s, x] = part(s, x)
        table[4, x] = zero


def mid_columns(codes, masks, table, columns):
    for n in range(2):
        planes = gathered(lambda o: [table[table_row(codes, n, 9 + o, 4)].reshape(8 * CH, LANES)], masks)
        unfold(planes, 8, columns, n * MID)


def edge_planes_of(own, part, received, far):
    odd = is_odd()
    low = [f(s, 7) for f in (own, part) for s in range(2)]
    high = [f(s, 0) for f in (own, part) for s in range(2)]
    for faces in (received, far):
        for s in range(2):
            first, second = faces(0, s), faces(1, s)
            low.append(jnp.where(odd, first, second))
            high.append(jnp.where(odd, second, first))
    return [[plane.reshape(2, HALF, LANES) for plane in side] for side in (low, high)]


def edge_columns(choose, masks, candidates, columns):
    def pieces(o):
        found = []
        for e in range(4):
            total = None
            for r, plane in enumerate(candidates[e & 1]):
                term = plane * choose[8 * (9 * e + o) + r]
                total = term if total is None else total + term
            found.append(total.reshape(CH, LANES))
        return found

    unfold(gathered(pieces, masks), 4, columns, 0)


def write_choices(codes, mirror, choose, turn_choice):
    d = codes >> 1
    dx = (d * 11) >> 5
    other = jnp.where(d - 3 * dx == 1, 0, 2) + jnp.where(dx == 1, 0, 4)
    row = jnp.where(codes >= 18, -1, other + (codes & 1))
    shape = (HALF, LANES)
    for e in range(4):
        n = e >> 1
        for o in range(9):
            at = o + 18 * (e & 1)
            wide = jnp.broadcast_to(row[n : n + 1, at : at + 1], shape)
            for r in range(8):
                choose[8 * (9 * e + o) + r] = one(wide == r)
    for n in range(2):
        for r in range(3):
            wide = jnp.broadcast_to(mirror[n : n + 1, r : r + 1], shape)
            turn_choice[3 * n + r] = wide.astype(F32).astype(BF)


def chosen(turn_choice, n, r, first, second):
    tile = jnp.concatenate([turn_choice[3 * n + r - 1]] * 4, axis=1)
    slot = jnp.concatenate([tile, tile], axis=0)[: first.shape[0]]
    return second * slot + first * (1.0 - slot).astype(BF)


def fold_mid(stacked, row):
    zero = jnp.zeros((CH, LANES), F32)
    before = jnp.concatenate([zero, stacked[row : row + CH, : MID - LANES]], axis=1)
    after = jnp.concatenate([stacked[row + 2 * CH : row + 3 * CH, LANES:], zero], axis=1)
    return before + stacked[row + CH : row + 2 * CH] + after


def edge_terms(stacked, row):
    blocks = []
    for e in range(4):
        first = row + 2 * CH * (e & 1)
        blocks.append(stacked[first : first + CH, e * LANES : (e + 1) * LANES])
    return jnp.concatenate(blocks, axis=1)


def edge_planes(ref):
    return jnp.concatenate([ref[e >> 1, :, 7 * (e & 1) * LANES : (7 * (e & 1) + 1) * LANES] for e in range(4)], axis=1)


def write_faces(face_a, face_b, index, plane_low, plane_high):
    odd = is_odd()
    face_a[index] = jnp.where(odd, plane_low, plane_high)
    face_b[index] = jnp.where(odd, plane_high, plane_low)


def spread_kernel(features, fp, staged):
    staged[...] = jnp.zeros_like(staged)
    for n in range(2):
        staged[n * CH : n * CH + 30, :] = features[n]
    rows = jnp.concatenate([staged[:, k * 128 : (k + 1) * 128] for k in range(4)], axis=0)
    planes = dot(rows, spread_table()).astype(BF)
    for n in range(2):
        for x in range(8):
            first = (x >> 1) * 2 * CH + n * CH
            fp[n, x] = planes[first : first + CH, (x & 1) * LANES : (x & 1) * LANES + LANES]


def weights_kernel(packed, small, one_out, two_out, turned_out, codes_out, choose, turn_choice, padded, left):
    shape = (CH, LANES)
    i, c = iota(shape, 0), iota(shape, 1)
    double = jnp.where(i >= 20, 2.0, 1.0)
    j = iota((LANES, LANES), 1) & (CH - 1)
    col = iota((LANES, LANES), 0)
    by_in = one(in_class(col) == component_class(j))
    by_out = one(out_class(col) == component_class(j))
    rows_out = jnp.where(component_class(i) == out_class(c), double, 0.0)
    rows_gate = one(gate_class(i) == out_class(c), F32)
    rows_in = jnp.where(component_class(i) == in_class(c), double, 0.0)
    same = component_index(i) == component_index(c & (CH - 1))
    quarter = c >> 5
    padded[...] = jnp.zeros_like(padded)
    for which in range(2):
        padded[which, 0:27, 0:84] = packed[0:27, which * LANES : which * LANES + 84].astype(F32)
    codes_out[...] = small[:, 0:27]
    write_choices(small[:, 0:LANES], small[:, LANES : 2 * LANES], choose, turn_choice)
    for which, rows, columns, blocks, out, base, flip in (
        (0, rows_out, by_in, True, one_out, 0, False),
        (0, rows_gate, by_in, False, one_out, 96, False),
        (1, rows_out, by_in, True, two_out, 0, False),
        (1, rows_in, by_out, True, turned_out, 0, True),
    ):
        for a in range(3):
            for bc in range(9):
                o = 9 * a + bc
                o = 26 - o if flip else o
                left[bc * CH : (bc + 1) * CH, :] = (rows * padded[which, o : o + 1, :]).astype(BF)
            found = dot(left[...], columns)
            for g in range(3):
                tile = jnp.zeros(shape, F32)
                for q in range(min(4, 9 - 4 * g)):
                    bc = 4 * g + q
                    keep = (quarter == q) & same if blocks else quarter == q
                    tile = tile + jnp.where(keep, found[bc * CH : (bc + 1) * CH], 0.0)
                width = min(128, 288 - 128 * g)
                out[base + a * CH : base + (a + 1) * CH, g * 128 : g * 128 + width] = tile[:, :width].astype(BF)


def first_mid_kernel(codes, own, part, w_first, columns, pre, gate_in, hidden_mid, table):
    masks = region_masks()
    inside = masks[4].astype(F32)
    stage_mid(table, lambda s, x: own[s, x], lambda s, x: part[s, x])
    mid_columns(codes, masks, table, columns)
    for n in range(2):
        stacked = dot(w_first[...], columns[:, n * MID : (n + 1) * MID])
        a, g = fold_mid(stacked, 0), fold_mid(stacked, 96)
        pre[n] = a
        gate_in[n] = g
        for x in range(1, 7):
            at = slice(x * LANES, (x + 1) * LANES)
            hidden_mid[n, x - 1] = (a[:, at] * jax.nn.sigmoid(g[:, at]) * inside).astype(BF)


def turned_sum(staged, table):
    rows = []
    for k in range(4):
        blocks = (k, k, 3 - k, 3 - k)
        rows.append(jnp.concatenate([staged[r, :, 128 * b : 128 * b + 128] for r, b in enumerate(blocks)], axis=1))
    return dot(jnp.concatenate(rows, axis=0), table) * 0.25


def back_kernel(turn_choice, own, across_y, crossed, back, staged):
    zero2 = jnp.zeros((2, 512), BF)
    for n in range(2):
        for r in range(4):
            if r == 0:
                value = own[n]
            else:
                first, second = (across_y[0], across_y[1]) if r == 1 else (crossed[2 * r - 4], crossed[2 * r - 3])
                value = chosen(turn_choice, n, r, first, second) * turn_signs(r, (30, 512))
            staged[r, n * CH : n * CH + 30, :] = value
            staged[r, n * CH + 30 : (n + 1) * CH, :] = zero2
    planes = turned_sum(staged, turns_spread_table()).astype(BF)
    for n in range(2):
        for x in range(8):
            first = (x >> 1) * 2 * CH + n * CH
            back[n, x] = planes[first : first + CH, (x & 1) * LANES : (x & 1) * LANES + LANES]


def first_edge_kernel(
    choose, own, part, got_a, got_b, pre, gate_in, hidden_mid, back, w_first,
    columns, pre_edge, gate_edge, both, face_a, face_b,
):
    masks = region_masks()
    inside = jnp.concatenate([masks[4].astype(F32)] * 4, axis=1)
    candidates = edge_planes_of(
        lambda s, x: own[s, x], lambda s, x: part[s, x],
        lambda which, s: (got_a, got_b)[which][s], lambda which, s: (got_a, got_b)[which][2 + s],
    )
    edge_columns(choose, masks, candidates, columns)
    stacked = dot(w_first[...], columns[...])
    a = edge_planes(pre) + edge_terms(stacked, 0)
    g = edge_planes(gate_in) + edge_terms(stacked, 96)
    pre_edge[...] = a
    gate_edge[...] = g
    hidden = (a * jax.nn.sigmoid(g) * inside).astype(BF)
    for n in range(2):
        outer = [hidden[:, e * LANES : (e + 1) * LANES] for e in (2 * n, 2 * n + 1)]
        both[0, n, 0], both[0, n, 7] = outer
        write_faces(face_a, face_b, (0, n), *outer)
        for x in range(1, 7):
            both[0, n, x] = hidden_mid[n, x - 1]
        for x in range(8):
            both[1, n, x] = back[n, x]
        write_faces(face_a, face_b, (1, n), back[n, 0], back[n, 7])


def gate_back(grad, a, g, rows8, inside):
    sig = jax.nn.sigmoid(g)
    through = grad * sig
    left, parts = grad * a, []
    for _ in range(3):
        parts.append(left.astype(BF))
        left = left - parts[-1].astype(F32)
    extra = dot(jnp.concatenate([rows8] * 3, axis=1), jnp.concatenate(parts, axis=0))
    sig8 = sig[0:8]
    top = through[0:8] + sig8 * (1.0 - sig8) * extra
    return (jnp.concatenate([top, through[8:]], axis=0) * inside).astype(BF)


def gate_rows():
    return one(gate_class(iota((8, CH), 1)) == iota((8, CH), 0))


def second_mid_kernel(
    codes, own, part, pre, gate_in, w_second, w_turned, second, through_edge, columns_h, placed_f, placed_s,
    table, columns_b,
):
    masks = region_masks()
    inside = jnp.concatenate([masks[4].astype(F32)] * 6, axis=1)
    for f, columns in ((0, columns_h), (1, columns_b)):
        stage_mid(table.at[f], lambda s, x: own[f, s, x], lambda s, x: part[f, s, x])
        mid_columns(codes, masks, table.at[f], columns)
    zero = jnp.zeros((CH, LANES), BF)
    rows8 = gate_rows()
    for placed in (placed_f, placed_s):
        placed[3 * CH :, :] = jnp.zeros((CH, 2 * MID), BF)

    def place(placed, n, planes, first, last):
        for a in range(3):
            for q in range(8):
                x = q + 1 - a
                at = (8 * n + q) * LANES
                placed[a * CH : (a + 1) * CH, at : at + LANES] = planes(x) if first <= x <= last else zero

    for n in range(2):
        here = slice(n * MID, (n + 1) * MID)
        second[n] = fold_mid(dot(w_second[...], columns_h[:, here]), 0)
        place(placed_s, n, lambda x: own[1, n, x], 0, 7)
        grad = fold_mid(dot(w_turned[...], columns_b[:, here]), 0)
        through_edge[:, 2 * n * LANES : (2 * n + 1) * LANES] = grad[:, :LANES]
        through_edge[:, (2 * n + 1) * LANES : (2 * n + 2) * LANES] = grad[:, 7 * LANES :]
        inner = slice(LANES, 7 * LANES)
        back_pre = gate_back(grad[:, inner], pre[n, :, inner], gate_in[n, :, inner], rows8, inside)
        place(placed_f, n, lambda x: back_pre[:, (x - 1) * LANES : x * LANES], 1, 6)


def gradient_kernel(columns_f, columns_h, placed_f, placed_s, raw):
    raw[0] = dot_t(columns_f[...], placed_f[...])
    raw[1] = dot_t(columns_h[...], placed_s[...])


def second_edge_kernel(
    scale, choose, own, part, got_a, got_b, far, pre_edge, gate_edge, through_edge,
    columns_f, columns_fe, raw, w_second, w_turned, second_edge, grads,
    columns_h, columns_b, placed_f, placed_s, place,
):
    masks = region_masks()
    inside = jnp.concatenate([masks[4].astype(F32)] * 4, axis=1)
    for f, columns in ((0, columns_h), (1, columns_b)):
        candidates = edge_planes_of(
            lambda s, x: own[f, s, x], lambda s, x: part[f, s, x],
            lambda which, s: (got_a, got_b)[which][f, s], lambda which, s: far[which, f, s],
        )
        edge_columns(choose, masks, candidates, columns)
    second_edge[...] = edge_terms(dot(w_second[...], columns_h[...]), 0)
    more_t = edge_terms(dot(w_turned[...], columns_b[...]), 0)
    back_pre = gate_back(through_edge[...] + more_t, pre_edge[...], gate_edge[...], gate_rows(), inside)
    placed_f[...] = jnp.zeros_like(placed_f)
    placed_s[...] = jnp.zeros_like(placed_s)
    for n in range(2):
        for side in range(2):
            at = (2 * n + side) * LANES
            a = 2 * side
            placed_s[a * CH : (a + 1) * CH, at : at + LANES] = own[1, n, 7 * side]
            for a in range(3):
                to = (6 * n + 3 * side + a) * LANES
                placed_f[a * CH : (a + 1) * CH, to : to + LANES] = back_pre[:, at : at + LANES]
    pieces = []
    for n in range(2):
        mid, edge = n * MID, 2 * n * LANES
        pieces += [
            columns_fe[:, edge : edge + LANES], columns_f[:, mid : mid + 2 * LANES],
            columns_f[:, mid + 6 * LANES : mid + MID], columns_fe[:, edge + LANES : edge + 2 * LANES],
        ]
    shape = (CH, LANES)
    i, c = iota(shape, 0), iota(shape, 1)
    lift = jnp.where(component_class(i) == out_class(c), jnp.where(i >= 20, 2.0, 1.0), 0.0).astype(BF)
    keep = one(component_class(i) == in_class(c), F32)
    same = one(component_index(i) == component_index(c & (CH - 1)), F32)
    place[...] = jnp.zeros_like(place)
    for a in range(3):
        for half in (0, LANES):
            place[half + a * CH : half + (a + 1) * CH, a * LANES : (a + 1) * LANES] = lift
    found = (
        raw[0] + dot_t(jnp.concatenate(pieces, axis=1), placed_f[...]),
        raw[1] + dot_t(columns_h[...], placed_s[...]),
    )
    for layer in range(2):
        masked = (found[layer].reshape(9, CH, LANES) * same).reshape(9 * CH, LANES)
        top = masked.astype(BF)
        rest = (masked - top.astype(F32)).astype(BF)
        lifted = dot(jnp.concatenate([top, rest], axis=1), place[...])
        for a in range(3):
            block = lifted[:, a * LANES : (a + 1) * LANES].reshape(9, CH, LANES) * keep
            first = 27 * layer + 9 * a
            grads[first : first + 9, :] = jnp.sum(block, axis=1) * scale
    grads[54:56, :] = jnp.zeros((2, LANES), F32)


def compact_kernel(second_in, more, second):
    zero = jnp.zeros((CH, LANES), F32)
    rows = []
    for n in range(2):
        for k in range(4):
            planes = second_in[n, :, k * 256 : (k + 1) * 256]
            if k == 0:
                planes = planes + jnp.concatenate([more[:, 2 * n * LANES : (2 * n + 1) * LANES], zero], axis=1)
            if k == 3:
                planes = planes + jnp.concatenate([zero, more[:, (2 * n + 1) * LANES : (2 * n + 2) * LANES]], axis=1)
            rows.append(planes.astype(BF))
    packed = dot(jnp.concatenate(rows, axis=0), compact_table()).astype(BF)
    for n in range(2):
        for k in range(4):
            first = (4 * n + k) * CH
            second[n * CH : (n + 1) * CH, k * LANES : (k + 1) * LANES] = packed[first : first + CH]


def turn_kernel(turn_choice, own, across_y, across_x, across, out, staged):
    for n in range(2):
        staged[0, n * CH : (n + 1) * CH, :] = own[n * CH : (n + 1) * CH, :]
        for r, ref in ((1, across_y), (2, across_x), (3, across)):
            value = chosen(turn_choice, n, r, ref[0:CH, :], ref[CH : 2 * CH, :])
            staged[r, n * CH : (n + 1) * CH, :] = value * turn_signs(r, (CH, 512))
    result = turned_sum(staged, turns_table()).astype(BF)
    for k in range(4):
        for n in range(2):
            first = (2 * k + n) * CH
            out[:, n, k * 128 : (k + 1) * 128] = result[first : first + 30]


SMEM = pl.BlockSpec(memory_space=pltpu.SMEM)
VMEM = pl.BlockSpec(memory_space=pltpu.VMEM)


def call(kernel, us, n_smem, outs, scratch, *args):
    return pl.pallas_call(
        kernel,
        out_shape=tuple(jax.ShapeDtypeStruct(s, t) for s, t in outs),
        in_specs=[SMEM] * n_smem + [VMEM] * (len(args) - n_smem),
        out_specs=tuple([VMEM] * len(outs)),
        scratch_shapes=[pltpu.VMEM(s, t) for s, t in scratch],
        compiler_params=pltpu.CompilerParams(vmem_limit_bytes=24 * 1024 * 1024),
        cost_estimate=pl.CostEstimate(flops=0, transcendentals=0, bytes_accessed=int(us * 3_000_000)),
    )(*args)


def swap_y(x):
    n = lax.axis_size("yp")
    return lax.ppermute(x, "yp", [(i, n - 1 - i) for i in range(n)])


def mirror_x(x):
    n = lax.axis_size("xp")
    return lax.ppermute(x, "xp", [(i, n - 1 - i) for i in range(n)])


def pair_swap(x, first):
    n = lax.axis_size("xp")
    pairs = []
    for i in range(first, n - 1, 2):
        pairs += [(i, i + 1), (i + 1, i)]
    return lax.ppermute(x, "xp", pairs)


def exchange(face_a, face_b):
    got_b = pair_swap(face_b, 1)
    got_a = pair_swap(face_a, 0)
    return got_a, got_b


def after(arrays, *others):
    return lax.optimization_barrier((tuple(arrays), others))[0]


def side_by_side(arrays, rows):
    total = None
    for k, x in enumerate(arrays):
        x = jnp.pad(x, ((0, rows - x.shape[0]), (k * LANES, (len(arrays) - k) * LANES - LANES + LANES - x.shape[1])))
        total = x if total is None else total + x
    return lax.optimization_barrier(total)


def on_device(features, cotangent, w_first, w_second, codes, mirror):
    plane = (CH, LANES)
    cot_y = swap_y(cotangent)
    crossed = mirror_x(jnp.concatenate([cotangent, cot_y], axis=0))
    (fp,) = call(spread_kernel, 0.2, 0, [((2, 8) + plane, BF)], [((64, 512), BF)], features)
    part = swap_y(fp)
    low, high = (jnp.concatenate([fp[:, x], part[:, x]], axis=0) for x in (0, 7))
    odd = is_odd()
    got = exchange(jnp.where(odd, low, high), jnp.where(odd, high, low))
    w_first, w_second, codes, mirror = after((w_first, w_second, codes, mirror), part)
    w1, w2, w2t, codes, choose, turn_choice = call(
        weights_kernel, 1, 0,
        [
            ((192, 288), BF), ((96, 288), BF), ((96, 288), BF), (codes.shape, codes.dtype),
            ((288, HALF, LANES), BF), ((6, HALF, LANES), BF),
        ],
        [((2, CH, LANES), F32), ((288, LANES), BF)],
        side_by_side((w_first, w_second), CH), side_by_side((codes, mirror), 2),
    )
    columns, pre, gate_in, hidden_mid = call(
        first_mid_kernel, 2, 1,
        [((288, 2 * MID), BF), ((2, CH, MID), F32), ((2, CH, MID), F32), ((2, 6) + plane, BF)],
        [((5, 8) + plane, BF)], codes, fp, part, w1,
    )
    (crossed,) = after((crossed,), hidden_mid)
    (back,) = call(
        back_kernel, 0.8, 0, [((2, 8) + plane, BF)], [((4, 64, 512), BF)], turn_choice, cotangent, cot_y, crossed
    )
    got = after(got, hidden_mid, back)
    columns_e, pre_e, gate_e, both, face_a, face_b = call(
        first_edge_kernel, 1, 0,
        [
            ((288, 4 * LANES), BF), ((CH, 4 * LANES), F32), ((CH, 4 * LANES), F32), ((2, 2, 8) + plane, BF),
            ((2, 2) + plane, BF), ((2, 2) + plane, BF),
        ],
        [], choose, fp, part, *got, pre, gate_in, hidden_mid, back, w1,
    )
    got = exchange(face_a, face_b)
    part = swap_y(both)
    second_part, through_e, columns_h, placed_f, placed_s = call(
        second_mid_kernel, 2.5, 1,
        [((2, CH, MID), F32), ((CH, 4 * LANES), F32), ((288, 2 * MID), BF), *[((128, 2 * MID), BF)] * 2],
        [((2, 5, 8) + plane, BF), ((288, 2 * MID), BF)],
        codes, both, part, pre, gate_in, w2, w2t,
    )
    got = after(got, second_part)
    far = swap_y(jnp.stack(got))
    columns_h, placed_f, placed_s = after((columns_h, placed_f, placed_s), *got)
    (raw,) = call(gradient_kernel, 1, 0, [((2, 288, LANES), F32)], [], columns, columns_h, placed_f, placed_s)
    n_bricks = features.shape[0] * lax.axis_size("xp") * lax.axis_size("yp")
    second_e, grads = call(
        functools.partial(second_edge_kernel, 1.0 / n_bricks), 2, 0, [((CH, 4 * LANES), F32), ((56, LANES), F32)],
        [((288, 4 * LANES), BF)] * 2
        + [((128, 12 * LANES), BF), ((128, 4 * LANES), BF), ((256, 3 * LANES), BF)],
        choose, both, part, *got, far, pre_e, gate_e, through_e, columns, columns_e, raw, w2, w2t,
    )
    total = grads + swap_y(grads)
    second_part, second_e = after((second_part, second_e), total)
    (second,) = call(compact_kernel, 0.5, 0, [((64, 512), BF)], [], second_part, second_e)
    second_y = swap_y(second)
    second_x = mirror_x(second)
    second_xy = swap_y(second_x)
    (denoised,) = call(
        turn_kernel, 0.9, 0, [((30, 2, 512), BF)], [((4, 64, 512), BF)], turn_choice, second, second_y, second_x, second_xy
    )
    denoised = denoised.transpose(1, 0, 2)
    n = lax.axis_size("xp")
    bit = 1
    while bit < n:
        total = total + lax.ppermute(total, "xp", [(i, i ^ bit) for i in range(n)])
        bit *= 2
    return denoised, total[0:27, 0:84], total[27:54, 0:84]


def solution(mesh):
    brick = P(("grp", "xp", "yp"))
    return jax.shard_map(
        on_device,
        mesh=mesh,
        in_specs=(brick, brick, P(), P(), brick, brick),
        out_specs=(brick, P("grp"), P("grp")),
        check_vma=False,
    )
```

```python
import functools

import jax
import jax.numpy as jnp
from jax import lax
from jax.experimental import pallas as pl
from jax.experimental.pallas import tpu as pltpu
from jax.sharding import PartitionSpec as P

BF = jnp.bfloat16
F32 = jnp.float32
CH = 32
LANES = 128
HALF = 16
OFFSETS = 27
MID = 8 * LANES
TURNS = (0, 63, 7 + 64, 56 + 64)


def iota(shape, dim):
    return lax.broadcasted_iota(jnp.int32, shape, dim)


def component_class(i):
    tensor = jnp.where(i < 30, 12 + ((i - 20) & 1), -1)
    return jnp.where(i < 8, i, jnp.where(i < 20, 8 + ((i - 8) & 3), tensor))


def component_index(i):
    return jnp.where(i < 8, 0, jnp.where(i < 20, (i - 8) >> 2, jnp.where(i < 30, (i - 20) >> 1, -1)))


def gate_class(i):
    tensor = jnp.where(i < 30, 4 + ((i - 20) & 1), -1)
    return jnp.where(i < 8, i, jnp.where(i < 20, (i - 8) & 3, tensor))


def out_class(c):
    tensor = jnp.where(c < 84, 12 + ((c - 80) >> 1), -2)
    return jnp.where(c < 64, c >> 3, jnp.where(c < 80, 8 + ((c - 64) >> 2), tensor))


def in_class(c):
    tensor = jnp.where(c < 84, 12 + ((c - 80) & 1), -2)
    return jnp.where(c < 64, c & 7, jnp.where(c < 80, 8 + ((c - 64) & 3), tensor))


def one(condition, kind=BF):
    return jnp.where(condition, 1.0, 0.0).astype(kind)


def plane_source(q):
    lane = q & 127
    row = (lane * 205) >> 11
    y, z = row - 1, lane - 10 * row - 1
    inside = (y >= 0) & (y < 8) & (z >= 0) & (z < 8)
    return jnp.where(inside, 64 * (q >> 7) + 8 * y + z, -1)


def spread_table():
    return one(plane_source(iota((128, 256), 1)) == iota((128, 256), 0))


def compact_table():
    return one(plane_source(iota((256, 128), 0)) == iota((256, 128), 1))


def turn_table(r):
    return one((iota((128, 128), 1) ^ TURNS[r]) == iota((128, 128), 0))


def turns_table():
    return jnp.concatenate([turn_table(r) for r in range(4)], axis=0)


def turns_spread_table():
    source = plane_source(iota((128, 256), 1))
    return jnp.concatenate([one((source ^ TURNS[r]) == iota((128, 256), 0)) for r in range(4)], axis=0)


def turn_signs(r, shape):
    i = iota(shape, 0) & (CH - 1)
    m = component_index(i)
    vector = (i >= 8) & (i < 20) & (m != r - 1)
    tensor = (i >= 20) & (m < 3) & (m != 3 - r)
    return jnp.where(vector | tensor, -1.0, 1.0).astype(BF)


def region_masks():
    lane = iota((1, LANES), 1)
    row = (lane * 205) >> 11
    col = lane - 10 * row

    def part(v):
        return jnp.where(v == 0, 0, jnp.where(v == 9, 2, 1))

    region = jnp.where(row < 10, 3 * part(row) + part(col), -1)
    return [one(region == o) for o in range(9)]


def dot(a, b, **kw):
    return jnp.dot(a, b, preferred_element_type=F32, **kw)


def dot_t(a, b):
    return lax.dot_general(a, b, (((1,), (1,)), ((), ())), preferred_element_type=F32)


def is_odd():
    return (lax.axis_index("xp") & 1) == 1


def table_row(codes, n, o, last):
    e = codes[n, o]
    d = e >> 1
    dx = lax.div(d, 3)
    other = jnp.where(d - 3 * dx == 1, 0, 2) + jnp.where(dx == 1, 0, 4)
    return jnp.where(e >= 18, last, jnp.minimum(other + (e & 1), last))


def gathered(pieces_of, masks):
    total = None
    for b in range(3):
        for c in range(3):
            o = 3 * b + c
            planes = jnp.concatenate(pieces_of(o), axis=0)
            shift = ((b - 1) * 80 + (c - 1) * 8) % LANES
            if shift:
                planes = pltpu.roll(planes, shift, 1)
            planes = planes * masks[o]
            total = planes if total is None else total + planes
    return total


def unfold(planes, count, columns, start):
    for o in range(9):
        shift = (11 - 10 * (o // 3) - o % 3) % LANES
        moved = pltpu.roll(planes, shift, 1) if shift else planes
        for p in range(count):
            at = start + p * LANES
            columns[o * CH : (o + 1) * CH, at : at + LANES] = moved[p * CH : (p + 1) * CH]


def stage_mid(table, own, part):
    zero = jnp.zeros((CH, LANES), BF)
    for x in range(8):
        for s in range(2):
            table[s, x] = own(s, x)
            table[2 + s, x] = part(s, x)
        table[4, x] = zero


def mid_columns(codes, masks, table, columns):
    for n in range(2):
        planes = gathered(lambda o: [table[table_row(codes, n, 9 + o, 4)].reshape(8 * CH, LANES)], masks)
        unfold(planes, 8, columns, n * MID)


def edge_planes_of(own, part, received, far):
    odd = is_odd()
    low = [f(s, 7) for f in (own, part) for s in range(2)]
    high = [f(s, 0) for f in (own, part) for s in range(2)]
    for faces in (received, far):
        for s in range(2):
            first, second = faces(0, s), faces(1, s)
            low.append(jnp.where(odd, first, second))
            high.append(jnp.where(odd, second, first))
    return [[plane.reshape(2, HALF, LANES) for plane in side] for side in (low, high)]


OTHER_X, OTHER_Y, SLOTS, N_CHOICES = 0, 8, 16, 88


def edge_columns(choose, masks, candidates, columns):
    def pick(row, here, there):
        return [p * choose[row + 4] + q * choose[row] for p, q in zip(here, there)]

    found = []
    for e in range(4):
        own, part, near, far = (candidates[e & 1][2 * k : 2 * k + 2] for k in range(4))
        same_y = pick(OTHER_X + e, own, near)
        other_y = pick(OTHER_X + e, part, far)
        rows = [pick(OTHER_Y + 2 * (e >> 1) + k, same_y, other_y) for k in range(2)]
        found.append((rows[0], same_y, rows[1]))

    def pieces(o):
        planes = []
        for e in range(4):
            first, second = found[e][o // 3]
            at = SLOTS + 2 * (9 * e + o)
            planes.append((first * choose[at] + second * choose[at + 1]).reshape(CH, LANES))
        return planes

    unfold(gathered(pieces, masks), 4, columns, 0)


def write_choices(codes, mirror, choose, turn_choice):
    lane = iota(codes.shape, 1)
    a = (lane * 57) >> 9
    b = ((lane * 171) >> 9) - 3 * a
    d = codes >> 1
    dx = (d * 11) >> 5
    dy = d - 3 * dx
    there = (codes < 18) & (lane < OFFSETS)
    slot = jnp.where(there, codes & 1, -1)
    shape = (HALF, LANES)

    def flag(condition):
        return jnp.max(jnp.where(there & condition, 1.0, 0.0), axis=1, keepdims=True)

    for k in range(2):
        for base, found in ((OTHER_X, flag((a == 2 * k) & (dx != 1))), (OTHER_Y, flag((b == 2 * k) & (dy != 1)))):
            for n in range(2):
                wide = jnp.broadcast_to(found[n : n + 1], shape)
                choose[base + 2 * n + k] = wide.astype(BF)
                choose[base + 4 + 2 * n + k] = (1.0 - wide).astype(BF)
    for e in range(4):
        n = e >> 1
        for o in range(9):
            at = o + 18 * (e & 1)
            wide = jnp.broadcast_to(slot[n : n + 1, at : at + 1], shape)
            for s in range(2):
                choose[SLOTS + 2 * (9 * e + o) + s] = one(wide == s)
    for n in range(2):
        for r in range(3):
            wide = jnp.broadcast_to(mirror[n : n + 1, r : r + 1], shape)
            turn_choice[3 * n + r] = wide.astype(F32).astype(BF)


def chosen(turn_choice, n, r, first, second):
    tile = jnp.concatenate([turn_choice[3 * n + r - 1]] * 4, axis=1)
    slot = jnp.concatenate([tile, tile], axis=0)[: first.shape[0]]
    return second * slot + first * (1.0 - slot).astype(BF)


def fold_mid(stacked, row):
    zero = jnp.zeros((CH, LANES), F32)
    before = jnp.concatenate([zero, stacked[row : row + CH, : MID - LANES]], axis=1)
    after = jnp.concatenate([stacked[row + 2 * CH : row + 3 * CH, LANES:], zero], axis=1)
    return before + stacked[row + CH : row + 2 * CH] + after


def edge_terms(stacked, row):
    blocks = []
    for e in range(4):
        first = row + 2 * CH * (e & 1)
        blocks.append(stacked[first : first + CH, e * LANES : (e + 1) * LANES])
    return jnp.concatenate(blocks, axis=1)


def edge_planes(ref):
    return jnp.concatenate([ref[e >> 1, :, 7 * (e & 1) * LANES : (7 * (e & 1) + 1) * LANES] for e in range(4)], axis=1)


def write_faces(face_a, face_b, index, plane_low, plane_high):
    odd = is_odd()
    face_a[index] = jnp.where(odd, plane_low, plane_high)
    face_b[index] = jnp.where(odd, plane_high, plane_low)


def spread_kernel(features, fp, staged):
    staged[...] = jnp.zeros_like(staged)
    for n in range(2):
        staged[n * CH : n * CH + 30, :] = features[n]
    rows = jnp.concatenate([staged[:, k * 128 : (k + 1) * 128] for k in range(4)], axis=0)
    planes = dot(rows, spread_table()).astype(BF)
    for n in range(2):
        for x in range(8):
            first = (x >> 1) * 2 * CH + n * CH
            fp[n, x] = planes[first : first + CH, (x & 1) * LANES : (x & 1) * LANES + LANES]


def weights_kernel(packed, small, one_out, two_out, turned_out, codes_out, choose, turn_choice, padded, left):
    shape = (CH, LANES)
    i, c = iota(shape, 0), iota(shape, 1)
    double = jnp.where(i >= 20, 2.0, 1.0)
    j = iota((LANES, LANES), 1) & (CH - 1)
    col = iota((LANES, LANES), 0)
    by_in = one(in_class(col) == component_class(j))
    by_out = one(out_class(col) == component_class(j))
    rows_out = jnp.where(component_class(i) == out_class(c), double, 0.0)
    rows_gate = one(gate_class(i) == out_class(c), F32)
    rows_in = jnp.where(component_class(i) == in_class(c), double, 0.0)
    same = component_index(i) == component_index(c & (CH - 1))
    quarter = c >> 5
    padded[...] = jnp.zeros_like(padded)
    for which in range(2):
        padded[which, 0:27, 0:84] = packed[0:27, which * LANES : which * LANES + 84].astype(F32)
    codes_out[...] = small[:, 0:27]
    write_choices(small[:, 0:LANES], small[:, LANES : 2 * LANES], choose, turn_choice)
    for which, rows, columns, blocks, out, base, flip in (
        (0, rows_out, by_in, True, one_out, 0, False),
        (0, rows_gate, by_in, False, one_out, 96, False),
        (1, rows_out, by_in, True, two_out, 0, False),
        (1, rows_in, by_out, True, turned_out, 0, True),
    ):
        for a in range(3):
            for bc in range(9):
                o = 9 * a + bc
                o = 26 - o if flip else o
                left[bc * CH : (bc + 1) * CH, :] = (rows * padded[which, o : o + 1, :]).astype(BF)
            found = dot(left[...], columns)
            for g in range(3):
                tile = jnp.zeros(shape, F32)
                for q in range(min(4, 9 - 4 * g)):
                    bc = 4 * g + q
                    keep = (quarter == q) & same if blocks else quarter == q
                    tile = tile + jnp.where(keep, found[bc * CH : (bc + 1) * CH], 0.0)
                width = min(128, 288 - 128 * g)
                out[base + a * CH : base + (a + 1) * CH, g * 128 : g * 128 + width] = tile[:, :width].astype(BF)


def first_mid_kernel(codes, own, part, w_first, columns, pre, gate_in, hidden_mid, table):
    masks = region_masks()
    inside = masks[4].astype(F32)
    stage_mid(table, lambda s, x: own[s, x], lambda s, x: part[s, x])
    mid_columns(codes, masks, table, columns)
    for n in range(2):
        stacked = dot(w_first[...], columns[:, n * MID : (n + 1) * MID])
        a, g = fold_mid(stacked, 0), fold_mid(stacked, 96)
        pre[n] = a
        gate_in[n] = g
        for x in range(1, 7):
            at = slice(x * LANES, (x + 1) * LANES)
            hidden_mid[n, x - 1] = (a[:, at] * jax.nn.sigmoid(g[:, at]) * inside).astype(BF)


def turned_sum(staged, table):
    rows = []
    for k in range(4):
        blocks = (k, k, 3 - k, 3 - k)
        rows.append(jnp.concatenate([staged[r, :, 128 * b : 128 * b + 128] for r, b in enumerate(blocks)], axis=1))
    return dot(jnp.concatenate(rows, axis=0), table) * 0.25


def back_kernel(turn_choice, own, across_y, crossed, back, staged):
    zero2 = jnp.zeros((2, 512), BF)
    for n in range(2):
        for r in range(4):
            if r == 0:
                value = own[n]
            else:
                first, second = (across_y[0], across_y[1]) if r == 1 else (crossed[2 * r - 4], crossed[2 * r - 3])
                value = chosen(turn_choice, n, r, first, second) * turn_signs(r, (30, 512))
            staged[r, n * CH : n * CH + 30, :] = value
            staged[r, n * CH + 30 : (n + 1) * CH, :] = zero2
    planes = turned_sum(staged, turns_spread_table()).astype(BF)
    for n in range(2):
        for x in range(8):
            first = (x >> 1) * 2 * CH + n * CH
            back[n, x] = planes[first : first + CH, (x & 1) * LANES : (x & 1) * LANES + LANES]


def first_edge_kernel(
    choose, own, part, got_a, got_b, pre, gate_in, hidden_mid, back, w_first,
    columns, pre_edge, gate_edge, both, face_a, face_b,
):
    masks = region_masks()
    inside = jnp.concatenate([masks[4].astype(F32)] * 4, axis=1)
    candidates = edge_planes_of(
        lambda s, x: own[s, x], lambda s, x: part[s, x],
        lambda which, s: (got_a, got_b)[which][s], lambda which, s: (got_a, got_b)[which][2 + s],
    )
    edge_columns(choose, masks, candidates, columns)
    stacked = dot(w_first[...], columns[...])
    a = edge_planes(pre) + edge_terms(stacked, 0)
    g = edge_planes(gate_in) + edge_terms(stacked, 96)
    pre_edge[...] = a
    gate_edge[...] = g
    hidden = (a * jax.nn.sigmoid(g) * inside).astype(BF)
    for n in range(2):
        outer = [hidden[:, e * LANES : (e + 1) * LANES] for e in (2 * n, 2 * n + 1)]
        both[0, n, 0], both[0, n, 7] = outer
        write_faces(face_a, face_b, (0, n), *outer)
        for x in range(1, 7):
            both[0, n, x] = hidden_mid[n, x - 1]
        for x in range(8):
            both[1, n, x] = back[n, x]
        write_faces(face_a, face_b, (1, n), back[n, 0], back[n, 7])


def gate_back(grad, a, g, rows8, inside):
    sig = jax.nn.sigmoid(g)
    through = grad * sig
    left, parts = grad * a, []
    for _ in range(3):
        parts.append(left.astype(BF))
        left = left - parts[-1].astype(F32)
    extra = dot(jnp.concatenate([rows8] * 3, axis=1), jnp.concatenate(parts, axis=0))
    sig8 = sig[0:8]
    top = through[0:8] + sig8 * (1.0 - sig8) * extra
    return (jnp.concatenate([top, through[8:]], axis=0) * inside).astype(BF)


def gate_rows():
    return one(gate_class(iota((8, CH), 1)) == iota((8, CH), 0))


def second_mid_kernel(
    codes, own, part, pre, gate_in, w_second, w_turned, second, through_edge, columns_h, placed_f, placed_s,
    table, columns_b,
):
    masks = region_masks()
    inside = jnp.concatenate([masks[4].astype(F32)] * 6, axis=1)
    for f, columns in ((0, columns_h), (1, columns_b)):
        stage_mid(table.at[f], lambda s, x: own[f, s, x], lambda s, x: part[f, s, x])
        mid_columns(codes, masks, table.at[f], columns)
    zero = jnp.zeros((CH, LANES), BF)
    rows8 = gate_rows()
    for placed in (placed_f, placed_s):
        placed[3 * CH :, :] = jnp.zeros((CH, 2 * MID), BF)

    def place(placed, n, planes, first, last):
        for a in range(3):
            for q in range(8):
                x = q + 1 - a
                at = (8 * n + q) * LANES
                placed[a * CH : (a + 1) * CH, at : at + LANES] = planes(x) if first <= x <= last else zero

    for n in range(2):
        here = slice(n * MID, (n + 1) * MID)
        second[n] = fold_mid(dot(w_second[...], columns_h[:, here]), 0)
        place(placed_s, n, lambda x: own[1, n, x], 0, 7)
        grad = fold_mid(dot(w_turned[...], columns_b[:, here]), 0)
        through_edge[:, 2 * n * LANES : (2 * n + 1) * LANES] = grad[:, :LANES]
        through_edge[:, (2 * n + 1) * LANES : (2 * n + 2) * LANES] = grad[:, 7 * LANES :]
        inner = slice(LANES, 7 * LANES)
        back_pre = gate_back(grad[:, inner], pre[n, :, inner], gate_in[n, :, inner], rows8, inside)
        place(placed_f, n, lambda x: back_pre[:, (x - 1) * LANES : x * LANES], 1, 6)


def gradient_kernel(columns_f, columns_h, placed_f, placed_s, raw):
    raw[0] = dot_t(columns_f[...], placed_f[...])
    raw[1] = dot_t(columns_h[...], placed_s[...])


def second_edge_kernel(
    scale, choose, own, part, got_a, got_b, far, pre_edge, gate_edge, through_edge,
    columns_f, columns_fe, raw, w_second, w_turned, second_edge, grads,
    columns_h, columns_b, placed_f, placed_s, place,
):
    masks = region_masks()
    inside = jnp.concatenate([masks[4].astype(F32)] * 4, axis=1)
    for f, columns in ((0, columns_h), (1, columns_b)):
        candidates = edge_planes_of(
            lambda s, x: own[f, s, x], lambda s, x: part[f, s, x],
            lambda which, s: (got_a, got_b)[which][f, s], lambda which, s: far[which, f, s],
        )
        edge_columns(choose, masks, candidates, columns)
    second_edge[...] = edge_terms(dot(w_second[...], columns_h[...]), 0)
    more_t = edge_terms(dot(w_turned[...], columns_b[...]), 0)
    back_pre = gate_back(through_edge[...] + more_t, pre_edge[...], gate_edge[...], gate_rows(), inside)
    placed_f[...] = jnp.zeros_like(placed_f)
    placed_s[...] = jnp.zeros_like(placed_s)
    for n in range(2):
        for side in range(2):
            at = (2 * n + side) * LANES
            a = 2 * side
            placed_s[a * CH : (a + 1) * CH, at : at + LANES] = own[1, n, 7 * side]
            for a in range(3):
                to = (6 * n + 3 * side + a) * LANES
                placed_f[a * CH : (a + 1) * CH, to : to + LANES] = back_pre[:, at : at + LANES]
    pieces = []
    for n in range(2):
        mid, edge = n * MID, 2 * n * LANES
        pieces += [
            columns_fe[:, edge : edge + LANES], columns_f[:, mid : mid + 2 * LANES],
            columns_f[:, mid + 6 * LANES : mid + MID], columns_fe[:, edge + LANES : edge + 2 * LANES],
        ]
    shape = (CH, LANES)
    i, c = iota(shape, 0), iota(shape, 1)
    lift = jnp.where(component_class(i) == out_class(c), jnp.where(i >= 20, 2.0, 1.0), 0.0).astype(BF)
    keep = one(component_class(i) == in_class(c), F32)
    same = one(component_index(i) == component_index(c & (CH - 1)), F32)
    place[...] = jnp.zeros_like(place)
    for a in range(3):
        for half in (0, LANES):
            place[half + a * CH : half + (a + 1) * CH, a * LANES : (a + 1) * LANES] = lift
    found = (
        raw[0] + dot_t(jnp.concatenate(pieces, axis=1), placed_f[...]),
        raw[1] + dot_t(columns_h[...], placed_s[...]),
    )
    for layer in range(2):
        masked = (found[layer].reshape(9, CH, LANES) * same).reshape(9 * CH, LANES)
        top = masked.astype(BF)
        rest = (masked - top.astype(F32)).astype(BF)
        lifted = dot(jnp.concatenate([top, rest], axis=1), place[...])
        for a in range(3):
            block = lifted[:, a * LANES : (a + 1) * LANES].reshape(9, CH, LANES) * keep
            first = 27 * layer + 9 * a
            grads[first : first + 9, :] = jnp.sum(block, axis=1) * scale
    grads[54:56, :] = jnp.zeros((2, LANES), F32)


def compact_kernel(second_in, more, second):
    zero = jnp.zeros((CH, LANES), F32)
    rows = []
    for n in range(2):
        for k in range(4):
            planes = second_in[n, :, k * 256 : (k + 1) * 256]
            if k == 0:
                planes = planes + jnp.concatenate([more[:, 2 * n * LANES : (2 * n + 1) * LANES], zero], axis=1)
            if k == 3:
                planes = planes + jnp.concatenate([zero, more[:, (2 * n + 1) * LANES : (2 * n + 2) * LANES]], axis=1)
            rows.append(planes.astype(BF))
    packed = dot(jnp.concatenate(rows, axis=0), compact_table()).astype(BF)
    for n in range(2):
        for k in range(4):
            first = (4 * n + k) * CH
            second[n * CH : (n + 1) * CH, k * LANES : (k + 1) * LANES] = packed[first : first + CH]


def turn_kernel(turn_choice, own, across_y, across_x, across, out, staged):
    for n in range(2):
        staged[0, n * CH : (n + 1) * CH, :] = own[n * CH : (n + 1) * CH, :]
        for r, ref in ((1, across_y), (2, across_x), (3, across)):
            value = chosen(turn_choice, n, r, ref[0:CH, :], ref[CH : 2 * CH, :])
            staged[r, n * CH : (n + 1) * CH, :] = value * turn_signs(r, (CH, 512))
    result = turned_sum(staged, turns_table()).astype(BF)
    for k in range(4):
        for n in range(2):
            first = (2 * k + n) * CH
            out[:, n, k * 128 : (k + 1) * 128] = result[first : first + 30]


SMEM = pl.BlockSpec(memory_space=pltpu.SMEM)
VMEM = pl.BlockSpec(memory_space=pltpu.VMEM)


def call(kernel, us, n_smem, outs, scratch, *args):
    return pl.pallas_call(
        kernel,
        out_shape=tuple(jax.ShapeDtypeStruct(s, t) for s, t in outs),
        in_specs=[SMEM] * n_smem + [VMEM] * (len(args) - n_smem),
        out_specs=tuple([VMEM] * len(outs)),
        scratch_shapes=[pltpu.VMEM(s, t) for s, t in scratch],
        compiler_params=pltpu.CompilerParams(vmem_limit_bytes=24 * 1024 * 1024),
        cost_estimate=pl.CostEstimate(flops=0, transcendentals=0, bytes_accessed=int(us * 3_000_000)),
    )(*args)


def swap_y(x):
    n = lax.axis_size("yp")
    return lax.ppermute(x, "yp", [(i, n - 1 - i) for i in range(n)])


def mirror_x(x):
    n = lax.axis_size("xp")
    return lax.ppermute(x, "xp", [(i, n - 1 - i) for i in range(n)])


def pair_swap(x, first):
    n = lax.axis_size("xp")
    pairs = []
    for i in range(first, n - 1, 2):
        pairs += [(i, i + 1), (i + 1, i)]
    return lax.ppermute(x, "xp", pairs)


def exchange(face_a, face_b):
    got_b = pair_swap(face_b, 1)
    got_a = pair_swap(face_a, 0)
    return got_a, got_b


def after(arrays, *others):
    return lax.optimization_barrier((tuple(arrays), others))[0]


def side_by_side(arrays, rows):
    total = None
    for k, x in enumerate(arrays):
        x = jnp.pad(x, ((0, rows - x.shape[0]), (k * LANES, (len(arrays) - k) * LANES - LANES + LANES - x.shape[1])))
        total = x if total is None else total + x
    return lax.optimization_barrier(total)


def on_device(features, cotangent, w_first, w_second, codes, mirror):
    plane = (CH, LANES)
    cot_y = swap_y(cotangent)
    crossed = mirror_x(jnp.concatenate([cotangent, cot_y], axis=0))
    (fp,) = call(spread_kernel, 0.2, 0, [((2, 8) + plane, BF)], [((64, 512), BF)], features)
    part = swap_y(fp)
    low, high = (jnp.concatenate([fp[:, x], part[:, x]], axis=0) for x in (0, 7))
    odd = is_odd()
    got = exchange(jnp.where(odd, low, high), jnp.where(odd, high, low))
    w_first, w_second, codes, mirror = after((w_first, w_second, codes, mirror), part)
    w1, w2, w2t, codes, choose, turn_choice = call(
        weights_kernel, 1, 0,
        [
            ((192, 288), BF), ((96, 288), BF), ((96, 288), BF), (codes.shape, codes.dtype),
            ((N_CHOICES, HALF, LANES), BF), ((6, HALF, LANES), BF),
        ],
        [((2, CH, LANES), F32), ((288, LANES), BF)],
        side_by_side((w_first, w_second), CH), side_by_side((codes, mirror), 2),
    )
    columns, pre, gate_in, hidden_mid = call(
        first_mid_kernel, 2, 1,
        [((288, 2 * MID), BF), ((2, CH, MID), F32), ((2, CH, MID), F32), ((2, 6) + plane, BF)],
        [((5, 8) + plane, BF)], codes, fp, part, w1,
    )
    (crossed,) = after((crossed,), hidden_mid)
    (back,) = call(
        back_kernel, 0.8, 0, [((2, 8) + plane, BF)], [((4, 64, 512), BF)], turn_choice, cotangent, cot_y, crossed
    )
    got = after(got, hidden_mid, back)
    columns_e, pre_e, gate_e, both, face_a, face_b = call(
        first_edge_kernel, 1, 0,
        [
            ((288, 4 * LANES), BF), ((CH, 4 * LANES), F32), ((CH, 4 * LANES), F32), ((2, 2, 8) + plane, BF),
            ((2, 2) + plane, BF), ((2, 2) + plane, BF),
        ],
        [], choose, fp, part, *got, pre, gate_in, hidden_mid, back, w1,
    )
    got = exchange(face_a, face_b)
    part = swap_y(both)
    second_part, through_e, columns_h, placed_f, placed_s = call(
        second_mid_kernel, 2.5, 1,
        [((2, CH, MID), F32), ((CH, 4 * LANES), F32), ((288, 2 * MID), BF), *[((128, 2 * MID), BF)] * 2],
        [((2, 5, 8) + plane, BF), ((288, 2 * MID), BF)],
        codes, both, part, pre, gate_in, w2, w2t,
    )
    got = after(got, second_part)
    far = swap_y(jnp.stack(got))
    columns_h, placed_f, placed_s = after((columns_h, placed_f, placed_s), *got)
    (raw,) = call(gradient_kernel, 1, 0, [((2, 288, LANES), F32)], [], columns, columns_h, placed_f, placed_s)
    n_bricks = features.shape[0] * lax.axis_size("xp") * lax.axis_size("yp")
    second_e, grads = call(
        functools.partial(second_edge_kernel, 1.0 / n_bricks), 2, 0, [((CH, 4 * LANES), F32), ((56, LANES), F32)],
        [((288, 4 * LANES), BF)] * 2
        + [((128, 12 * LANES), BF), ((128, 4 * LANES), BF), ((256, 3 * LANES), BF)],
        choose, both, part, *got, far, pre_e, gate_e, through_e, columns, columns_e, raw, w2, w2t,
    )
    total = grads + swap_y(grads)
    second_part, second_e = after((second_part, second_e), total)
    (second,) = call(compact_kernel, 0.5, 0, [((64, 512), BF)], [], second_part, second_e)
    second_y = swap_y(second)
    second_x = mirror_x(second)
    second_xy = swap_y(second_x)
    (denoised,) = call(
        turn_kernel, 0.9, 0, [((30, 2, 512), BF)], [((4, 64, 512), BF)], turn_choice, second, second_y, second_x, second_xy
    )
    denoised = denoised.transpose(1, 0, 2)
    n = lax.axis_size("xp")
    bit = 1
    while bit < n:
        total = total + lax.ppermute(total, "xp", [(i, i ^ bit) for i in range(n)])
        bit *= 2
    return denoised, total[0:27, 0:84], total[27:54, 0:84]


def solution(mesh):
    brick = P(("grp", "xp", "yp"))
    return jax.shard_map(
        on_device,
        mesh=mesh,
        in_specs=(brick, brick, P(), P(), brick, brick),
        out_specs=(brick, P("grp"), P("grp")),
        check_vma=False,
    )
```

```python
import functools

import jax
import jax.numpy as jnp
from jax import lax
from jax.experimental import pallas as pl
from jax.experimental.pallas import tpu as pltpu
from jax.sharding import PartitionSpec as P

BF = jnp.bfloat16
F32 = jnp.float32
CH = 32
LANES = 128
HALF = 16
OFFSETS = 27
MID = 8 * LANES
TURNS = (0, 63, 7 + 64, 56 + 64)


def iota(shape, dim):
    return lax.broadcasted_iota(jnp.int32, shape, dim)


def component_class(i):
    tensor = jnp.where(i < 30, 12 + ((i - 20) & 1), -1)
    return jnp.where(i < 8, i, jnp.where(i < 20, 8 + ((i - 8) & 3), tensor))


def component_index(i):
    return jnp.where(i < 8, 0, jnp.where(i < 20, (i - 8) >> 2, jnp.where(i < 30, (i - 20) >> 1, -1)))


def gate_class(i):
    tensor = jnp.where(i < 30, 4 + ((i - 20) & 1), -1)
    return jnp.where(i < 8, i, jnp.where(i < 20, (i - 8) & 3, tensor))


def out_class(c):
    tensor = jnp.where(c < 84, 12 + ((c - 80) >> 1), -2)
    return jnp.where(c < 64, c >> 3, jnp.where(c < 80, 8 + ((c - 64) >> 2), tensor))


def in_class(c):
    tensor = jnp.where(c < 84, 12 + ((c - 80) & 1), -2)
    return jnp.where(c < 64, c & 7, jnp.where(c < 80, 8 + ((c - 64) & 3), tensor))


def one(condition, kind=BF):
    return jnp.where(condition, 1.0, 0.0).astype(kind)


def plane_source(q):
    lane = q & 127
    row = (lane * 205) >> 11
    y, z = row - 1, lane - 10 * row - 1
    inside = (y >= 0) & (y < 8) & (z >= 0) & (z < 8)
    return jnp.where(inside, 64 * (q >> 7) + 8 * y + z, -1)


def spread_table():
    return one(plane_source(iota((128, 256), 1)) == iota((128, 256), 0))


def compact_table():
    return one(plane_source(iota((256, 128), 0)) == iota((256, 128), 1))


def turn_table(r):
    return one((iota((128, 128), 1) ^ TURNS[r]) == iota((128, 128), 0))


def turns_table():
    return jnp.concatenate([turn_table(r) for r in range(4)], axis=0)


def turns_spread_table():
    source = plane_source(iota((128, 256), 1))
    return jnp.concatenate([one((source ^ TURNS[r]) == iota((128, 256), 0)) for r in range(4)], axis=0)


def turn_signs(r, shape):
    i = iota(shape, 0) & (CH - 1)
    m = component_index(i)
    vector = (i >= 8) & (i < 20) & (m != r - 1)
    tensor = (i >= 20) & (m < 3) & (m != 3 - r)
    return jnp.where(vector | tensor, -1.0, 1.0).astype(BF)


def region_masks():
    lane = iota((1, LANES), 1)
    row = (lane * 205) >> 11
    col = lane - 10 * row

    def part(v):
        return jnp.where(v == 0, 0, jnp.where(v == 9, 2, 1))

    region = jnp.where(row < 10, 3 * part(row) + part(col), -1)
    return [one(region == o) for o in range(9)]


def dot(a, b, **kw):
    return jnp.dot(a, b, preferred_element_type=F32, **kw)


def dot_t(a, b):
    return lax.dot_general(a, b, (((1,), (1,)), ((), ())), preferred_element_type=F32)


def is_odd():
    return (lax.axis_index("xp") & 1) == 1


def table_row(codes, n, o, last):
    e = codes[n, o]
    d = e >> 1
    dx = lax.div(d, 3)
    other = jnp.where(d - 3 * dx == 1, 0, 2) + jnp.where(dx == 1, 0, 4)
    return jnp.where(e >= 18, last, jnp.minimum(other + (e & 1), last))


def gathered(pieces_of, masks):
    total = None
    for b in range(3):
        for c in range(3):
            o = 3 * b + c
            planes = jnp.concatenate(pieces_of(o), axis=0)
            shift = ((b - 1) * 80 + (c - 1) * 8) % LANES
            if shift:
                planes = pltpu.roll(planes, shift, 1)
            planes = planes * masks[o]
            total = planes if total is None else total + planes
    return total


def unfold(planes, count, columns, start):
    for o in range(9):
        shift = (11 - 10 * (o // 3) - o % 3) % LANES
        moved = pltpu.roll(planes, shift, 1) if shift else planes
        for p in range(count):
            at = start + p * LANES
            columns[o * CH : (o + 1) * CH, at : at + LANES] = moved[p * CH : (p + 1) * CH]


def stage_mid(table, own, part):
    zero = jnp.zeros((CH, LANES), BF)
    for x in range(8):
        for s in range(2):
            table[s, x] = own(s, x)
            table[2 + s, x] = part(s, x)
        table[4, x] = zero


def mid_columns(codes, masks, table, columns):
    for n in range(2):
        planes = gathered(lambda o: [table[table_row(codes, n, 9 + o, 4)].reshape(8 * CH, LANES)], masks)
        unfold(planes, 8, columns, n * MID)


def edge_planes_of(own, part, received, far):
    odd = is_odd()
    low = [f(s, 7) for f in (own, part) for s in range(2)]
    high = [f(s, 0) for f in (own, part) for s in range(2)]
    for faces in (received, far):
        for s in range(2):
            first, second = faces(0, s), faces(1, s)
            low.append(jnp.where(odd, first, second))
            high.append(jnp.where(odd, second, first))
    return [[plane.reshape(2, HALF, LANES) for plane in side] for side in (low, high)]


OTHER_X, OTHER_Y, SLOTS, N_CHOICES = 0, 8, 16, 88


def edge_columns(choose, masks, candidates, columns):
    def pick(row, here, there):
        return [p * choose[row + 4] + q * choose[row] for p, q in zip(here, there)]

    found = []
    for e in range(4):
        own, part, near, far = (candidates[e & 1][2 * k : 2 * k + 2] for k in range(4))
        same_y = pick(OTHER_X + e, own, near)
        other_y = pick(OTHER_X + e, part, far)
        rows = [pick(OTHER_Y + 2 * (e >> 1) + k, same_y, other_y) for k in range(2)]
        found.append((rows[0], same_y, rows[1]))

    def pieces(o):
        planes = []
        for e in range(4):
            first, second = found[e][o // 3]
            at = SLOTS + 2 * (9 * e + o)
            planes.append((first * choose[at] + second * choose[at + 1]).reshape(CH, LANES))
        return planes

    unfold(gathered(pieces, masks), 4, columns, 0)


def write_choices(codes, mirror, choose, turn_choice):
    lane = iota(codes.shape, 1)
    a = (lane * 57) >> 9
    b = ((lane * 171) >> 9) - 3 * a
    d = codes >> 1
    dx = (d * 11) >> 5
    dy = d - 3 * dx
    there = (codes < 18) & (lane < OFFSETS)
    slot = jnp.where(there, codes & 1, -1)
    shape = (HALF, LANES)

    def flag(condition):
        return jnp.max(jnp.where(there & condition, 1.0, 0.0), axis=1, keepdims=True)

    for k in range(2):
        for base, found in ((OTHER_X, flag((a == 2 * k) & (dx != 1))), (OTHER_Y, flag((b == 2 * k) & (dy != 1)))):
            for n in range(2):
                wide = jnp.broadcast_to(found[n : n + 1], shape)
                choose[base + 2 * n + k] = wide.astype(BF)
                choose[base + 4 + 2 * n + k] = (1.0 - wide).astype(BF)
    for e in range(4):
        n = e >> 1
        for o in range(9):
            at = o + 18 * (e & 1)
            wide = jnp.broadcast_to(slot[n : n + 1, at : at + 1], shape)
            for s in range(2):
                choose[SLOTS + 2 * (9 * e + o) + s] = one(wide == s)
    for n in range(2):
        for r in range(3):
            wide = jnp.broadcast_to(mirror[n : n + 1, r : r + 1], shape)
            turn_choice[3 * n + r] = wide.astype(F32).astype(BF)


def chosen(turn_choice, n, r, first, second):
    tile = jnp.concatenate([turn_choice[3 * n + r - 1]] * 4, axis=1)
    slot = jnp.concatenate([tile, tile], axis=0)[: first.shape[0]]
    return second * slot + first * (1.0 - slot).astype(BF)


def fold_mid(stacked, row):
    zero = jnp.zeros((CH, LANES), F32)
    before = jnp.concatenate([zero, stacked[row : row + CH, : MID - LANES]], axis=1)
    after = jnp.concatenate([stacked[row + 2 * CH : row + 3 * CH, LANES:], zero], axis=1)
    return before + stacked[row + CH : row + 2 * CH] + after


def edge_terms(stacked, row):
    blocks = []
    for e in range(4):
        first = row + 2 * CH * (e & 1)
        blocks.append(stacked[first : first + CH, e * LANES : (e + 1) * LANES])
    return jnp.concatenate(blocks, axis=1)


def edge_planes(ref):
    return jnp.concatenate([ref[e >> 1, :, 7 * (e & 1) * LANES : (7 * (e & 1) + 1) * LANES] for e in range(4)], axis=1)


def write_faces(face_a, face_b, index, plane_low, plane_high):
    odd = is_odd()
    face_a[index] = jnp.where(odd, plane_low, plane_high)
    face_b[index] = jnp.where(odd, plane_high, plane_low)


def spread_kernel(features, fp, staged):
    staged[...] = jnp.zeros_like(staged)
    for n in range(2):
        staged[n * CH : n * CH + 30, :] = features[n]
    rows = jnp.concatenate([staged[:, k * 128 : (k + 1) * 128] for k in range(4)], axis=0)
    planes = dot(rows, spread_table()).astype(BF)
    for n in range(2):
        for x in range(8):
            first = (x >> 1) * 2 * CH + n * CH
            fp[n, x] = planes[first : first + CH, (x & 1) * LANES : (x & 1) * LANES + LANES]


def weights_kernel(packed, small, one_out, two_out, turned_out, codes_out, choose, turn_choice, padded, left):
    shape = (CH, LANES)
    i, c = iota(shape, 0), iota(shape, 1)
    double = jnp.where(i >= 20, 2.0, 1.0)
    j = iota((LANES, LANES), 1) & (CH - 1)
    col = iota((LANES, LANES), 0)
    by_in = one(in_class(col) == component_class(j))
    by_out = one(out_class(col) == component_class(j))
    rows_out = jnp.where(component_class(i) == out_class(c), double, 0.0)
    rows_gate = one(gate_class(i) == out_class(c), F32)
    rows_in = jnp.where(component_class(i) == in_class(c), double, 0.0)
    same = component_index(i) == component_index(c & (CH - 1))
    quarter = c >> 5
    padded[...] = jnp.zeros_like(padded)
    for which in range(2):
        padded[which, 0:27, 0:84] = packed[0:27, which * LANES : which * LANES + 84].astype(F32)
    codes_out[...] = small[:, 0:27]
    write_choices(small[:, 0:LANES], small[:, LANES : 2 * LANES], choose, turn_choice)
    for which, rows, columns, blocks, out, base, flip in (
        (0, rows_out, by_in, True, one_out, 0, False),
        (0, rows_gate, by_in, False, one_out, 96, False),
        (1, rows_out, by_in, True, two_out, 0, False),
        (1, rows_in, by_out, True, turned_out, 0, True),
    ):
        for a in range(3):
            for bc in range(9):
                o = 9 * a + bc
                o = 26 - o if flip else o
                left[bc * CH : (bc + 1) * CH, :] = (rows * padded[which, o : o + 1, :]).astype(BF)
            found = dot(left[...], columns)
            for g in range(3):
                tile = jnp.zeros(shape, F32)
                for q in range(min(4, 9 - 4 * g)):
                    bc = 4 * g + q
                    keep = (quarter == q) & same if blocks else quarter == q
                    tile = tile + jnp.where(keep, found[bc * CH : (bc + 1) * CH], 0.0)
                width = min(128, 288 - 128 * g)
                out[base + a * CH : base + (a + 1) * CH, g * 128 : g * 128 + width] = tile[:, :width].astype(BF)


def first_mid_kernel(codes, own, part, w_first, columns, pre, gate_in, hidden_mid, table):
    masks = region_masks()
    inside = masks[4].astype(F32)
    stage_mid(table, lambda s, x: own[s, x], lambda s, x: part[s, x])
    mid_columns(codes, masks, table, columns)
    for n in range(2):
        stacked = dot(w_first[...], columns[:, n * MID : (n + 1) * MID])
        a, g = fold_mid(stacked, 0), fold_mid(stacked, 96)
        pre[n] = a
        gate_in[n] = g
        for x in range(1, 7):
            at = slice(x * LANES, (x + 1) * LANES)
            hidden_mid[n, x - 1] = (a[:, at] * jax.nn.sigmoid(g[:, at]) * inside).astype(BF)


def turned_sum(staged, table):
    rows = []
    for k in range(4):
        blocks = (k, k, 3 - k, 3 - k)
        rows.append(jnp.concatenate([staged[r, :, 128 * b : 128 * b + 128] for r, b in enumerate(blocks)], axis=1))
    return dot(jnp.concatenate(rows, axis=0), table) * 0.25


def back_kernel(turn_choice, own, across_y, crossed, back, staged):
    zero2 = jnp.zeros((2, 512), BF)
    for n in range(2):
        for r in range(4):
            if r == 0:
                value = own[n]
            else:
                first, second = (across_y[0], across_y[1]) if r == 1 else (crossed[2 * r - 4], crossed[2 * r - 3])
                value = chosen(turn_choice, n, r, first, second) * turn_signs(r, (30, 512))
            staged[r, n * CH : n * CH + 30, :] = value
            staged[r, n * CH + 30 : (n + 1) * CH, :] = zero2
    planes = turned_sum(staged, turns_spread_table()).astype(BF)
    for n in range(2):
        for x in range(8):
            first = (x >> 1) * 2 * CH + n * CH
            back[n, x] = planes[first : first + CH, (x & 1) * LANES : (x & 1) * LANES + LANES]


def first_edge_kernel(
    choose, own, part, got_a, got_b, pre, gate_in, hidden_mid, back, w_first,
    columns, pre_edge, gate_edge, both, face_a, face_b,
):
    masks = region_masks()
    inside = jnp.concatenate([masks[4].astype(F32)] * 4, axis=1)
    candidates = edge_planes_of(
        lambda s, x: own[s, x], lambda s, x: part[s, x],
        lambda which, s: (got_a, got_b)[which][s], lambda which, s: (got_a, got_b)[which][2 + s],
    )
    edge_columns(choose, masks, candidates, columns)
    stacked = dot(w_first[...], columns[...])
    a = edge_planes(pre) + edge_terms(stacked, 0)
    g = edge_planes(gate_in) + edge_terms(stacked, 96)
    pre_edge[...] = a
    gate_edge[...] = g
    hidden = (a * jax.nn.sigmoid(g) * inside).astype(BF)
    for n in range(2):
        outer = [hidden[:, e * LANES : (e + 1) * LANES] for e in (2 * n, 2 * n + 1)]
        both[0, n, 0], both[0, n, 7] = outer
        write_faces(face_a, face_b, (0, n), *outer)
        for x in range(1, 7):
            both[0, n, x] = hidden_mid[n, x - 1]
        for x in range(8):
            both[1, n, x] = back[n, x]
        write_faces(face_a, face_b, (1, n), back[n, 0], back[n, 7])


def gate_back(grad, a, g, rows8, inside):
    sig = jax.nn.sigmoid(g)
    through = grad * sig
    left, parts = grad * a, []
    for _ in range(3):
        parts.append(left.astype(BF))
        left = left - parts[-1].astype(F32)
    extra = dot(jnp.concatenate([rows8] * 3, axis=1), jnp.concatenate(parts, axis=0))
    sig8 = sig[0:8]
    top = through[0:8] + sig8 * (1.0 - sig8) * extra
    return (jnp.concatenate([top, through[8:]], axis=0) * inside).astype(BF)


def gate_rows():
    return one(gate_class(iota((8, CH), 1)) == iota((8, CH), 0))


def second_mid_kernel(
    codes, own, part, pre, gate_in, w_second, w_turned, second, through_edge, columns_h, placed_f, placed_s,
    table, columns_b,
):
    masks = region_masks()
    inside = jnp.concatenate([masks[4].astype(F32)] * 6, axis=1)
    for f, columns in ((0, columns_h), (1, columns_b)):
        stage_mid(table.at[f], lambda s, x: own[f, s, x], lambda s, x: part[f, s, x])
        mid_columns(codes, masks, table.at[f], columns)
    zero = jnp.zeros((CH, LANES), BF)
    rows8 = gate_rows()
    for placed in (placed_f, placed_s):
        placed[3 * CH :, :] = jnp.zeros((CH, 2 * MID), BF)

    def place(placed, n, planes, first, last):
        for a in range(3):
            for q in range(8):
                x = q + 1 - a
                at = (8 * n + q) * LANES
                placed[a * CH : (a + 1) * CH, at : at + LANES] = planes(x) if first <= x <= last else zero

    for n in range(2):
        here = slice(n * MID, (n + 1) * MID)
        second[n] = fold_mid(dot(w_second[...], columns_h[:, here]), 0)
        place(placed_s, n, lambda x: own[1, n, x], 0, 7)
        grad = fold_mid(dot(w_turned[...], columns_b[:, here]), 0)
        through_edge[:, 2 * n * LANES : (2 * n + 1) * LANES] = grad[:, :LANES]
        through_edge[:, (2 * n + 1) * LANES : (2 * n + 2) * LANES] = grad[:, 7 * LANES :]
        inner = slice(LANES, 7 * LANES)
        back_pre = gate_back(grad[:, inner], pre[n, :, inner], gate_in[n, :, inner], rows8, inside)
        place(placed_f, n, lambda x: back_pre[:, (x - 1) * LANES : x * LANES], 1, 6)


def gradient_kernel(columns_f, columns_h, placed_f, placed_s, raw):
    raw[0] = dot_t(columns_f[...], placed_f[...])
    raw[1] = dot_t(columns_h[...], placed_s[...])


def second_edge_kernel(
    scale, choose, own, part, got_a, got_b, far, pre_edge, gate_edge, through_edge,
    columns_f, columns_fe, raw, w_turned, columns_h, grads,
    columns_b, placed_f, placed_s, place,
):
    masks = region_masks()
    inside = jnp.concatenate([masks[4].astype(F32)] * 4, axis=1)
    for f, columns in ((0, columns_h), (1, columns_b)):
        candidates = edge_planes_of(
            lambda s, x: own[f, s, x], lambda s, x: part[f, s, x],
            lambda which, s: (got_a, got_b)[which][f, s], lambda which, s: far[which, f, s],
        )
        edge_columns(choose, masks, candidates, columns)
    more_t = edge_terms(dot(w_turned[...], columns_b[...]), 0)
    back_pre = gate_back(through_edge[...] + more_t, pre_edge[...], gate_edge[...], gate_rows(), inside)
    placed_f[...] = jnp.zeros_like(placed_f)
    placed_s[...] = jnp.zeros_like(placed_s)
    for n in range(2):
        for side in range(2):
            at = (2 * n + side) * LANES
            a = 2 * side
            placed_s[a * CH : (a + 1) * CH, at : at + LANES] = own[1, n, 7 * side]
            for a in range(3):
                to = (6 * n + 3 * side + a) * LANES
                placed_f[a * CH : (a + 1) * CH, to : to + LANES] = back_pre[:, at : at + LANES]
    pieces = []
    for n in range(2):
        mid, edge = n * MID, 2 * n * LANES
        pieces += [
            columns_fe[:, edge : edge + LANES], columns_f[:, mid : mid + 2 * LANES],
            columns_f[:, mid + 6 * LANES : mid + MID], columns_fe[:, edge + LANES : edge + 2 * LANES],
        ]
    shape = (CH, LANES)
    i, c = iota(shape, 0), iota(shape, 1)
    lift = jnp.where(component_class(i) == out_class(c), jnp.where(i >= 20, 2.0, 1.0), 0.0).astype(BF)
    keep = one(component_class(i) == in_class(c), F32)
    same = one(component_index(i) == component_index(c & (CH - 1)), F32)
    place[...] = jnp.zeros_like(place)
    for a in range(3):
        for half in (0, LANES):
            place[half + a * CH : half + (a + 1) * CH, a * LANES : (a + 1) * LANES] = lift
    found = (
        raw[0] + dot_t(jnp.concatenate(pieces, axis=1), placed_f[...]),
        raw[1] + dot_t(columns_h[...], placed_s[...]),
    )
    for layer in range(2):
        masked = (found[layer].reshape(9, CH, LANES) * same).reshape(9 * CH, LANES)
        top = masked.astype(BF)
        rest = (masked - top.astype(F32)).astype(BF)
        lifted = dot(jnp.concatenate([top, rest], axis=1), place[...])
        for a in range(3):
            block = lifted[:, a * LANES : (a + 1) * LANES].reshape(9, CH, LANES) * keep
            first = 27 * layer + 9 * a
            grads[first : first + 9, :] = jnp.sum(block, axis=1) * scale
    grads[54:56, :] = jnp.zeros((2, LANES), F32)


def compact_kernel(second_in, columns, w_second, second):
    more = edge_terms(dot(w_second[...], columns[...]), 0)
    zero = jnp.zeros((CH, LANES), F32)
    rows = []
    for n in range(2):
        for k in range(4):
            planes = second_in[n, :, k * 256 : (k + 1) * 256]
            if k == 0:
                planes = planes + jnp.concatenate([more[:, 2 * n * LANES : (2 * n + 1) * LANES], zero], axis=1)
            if k == 3:
                planes = planes + jnp.concatenate([zero, more[:, (2 * n + 1) * LANES : (2 * n + 2) * LANES]], axis=1)
            rows.append(planes.astype(BF))
    packed = dot(jnp.concatenate(rows, axis=0), compact_table()).astype(BF)
    for n in range(2):
        for k in range(4):
            first = (4 * n + k) * CH
            second[n * CH : (n + 1) * CH, k * LANES : (k + 1) * LANES] = packed[first : first + CH]


def turn_kernel(turn_choice, own, across_y, across_x, across, out, staged):
    for n in range(2):
        staged[0, n * CH : (n + 1) * CH, :] = own[n * CH : (n + 1) * CH, :]
        for r, ref in ((1, across_y), (2, across_x), (3, across)):
            value = chosen(turn_choice, n, r, ref[0:CH, :], ref[CH : 2 * CH, :])
            staged[r, n * CH : (n + 1) * CH, :] = value * turn_signs(r, (CH, 512))
    result = turned_sum(staged, turns_table()).astype(BF)
    for k in range(4):
        for n in range(2):
            first = (2 * k + n) * CH
            out[:, n, k * 128 : (k + 1) * 128] = result[first : first + 30]


SMEM = pl.BlockSpec(memory_space=pltpu.SMEM)
VMEM = pl.BlockSpec(memory_space=pltpu.VMEM)


def call(kernel, us, n_smem, outs, scratch, *args):
    return pl.pallas_call(
        kernel,
        out_shape=tuple(jax.ShapeDtypeStruct(s, t) for s, t in outs),
        in_specs=[SMEM] * n_smem + [VMEM] * (len(args) - n_smem),
        out_specs=tuple([VMEM] * len(outs)),
        scratch_shapes=[pltpu.VMEM(s, t) for s, t in scratch],
        compiler_params=pltpu.CompilerParams(vmem_limit_bytes=24 * 1024 * 1024),
        cost_estimate=pl.CostEstimate(flops=0, transcendentals=0, bytes_accessed=int(us * 3_000_000)),
    )(*args)


def swap_y(x):
    n = lax.axis_size("yp")
    return lax.ppermute(x, "yp", [(i, n - 1 - i) for i in range(n)])


def mirror_x(x):
    n = lax.axis_size("xp")
    return lax.ppermute(x, "xp", [(i, n - 1 - i) for i in range(n)])


def pair_swap(x, first):
    n = lax.axis_size("xp")
    pairs = []
    for i in range(first, n - 1, 2):
        pairs += [(i, i + 1), (i + 1, i)]
    return lax.ppermute(x, "xp", pairs)


def exchange(face_a, face_b):
    got_b = pair_swap(face_b, 1)
    got_a = pair_swap(face_a, 0)
    return got_a, got_b


def after(arrays, *others):
    return lax.optimization_barrier((tuple(arrays), others))[0]


def side_by_side(arrays, rows):
    total = None
    for k, x in enumerate(arrays):
        x = jnp.pad(x, ((0, rows - x.shape[0]), (k * LANES, (len(arrays) - k) * LANES - LANES + LANES - x.shape[1])))
        total = x if total is None else total + x
    return lax.optimization_barrier(total)


def on_device(features, cotangent, w_first, w_second, codes, mirror):
    plane = (CH, LANES)
    cot_y = swap_y(cotangent)
    crossed = mirror_x(jnp.concatenate([cotangent, cot_y], axis=0))
    (fp,) = call(spread_kernel, 0.2, 0, [((2, 8) + plane, BF)], [((64, 512), BF)], features)
    part = swap_y(fp)
    low, high = (jnp.concatenate([fp[:, x], part[:, x]], axis=0) for x in (0, 7))
    odd = is_odd()
    got = exchange(jnp.where(odd, low, high), jnp.where(odd, high, low))
    w_first, w_second, codes, mirror = after((w_first, w_second, codes, mirror), part)
    w1, w2, w2t, codes, choose, turn_choice = call(
        weights_kernel, 1, 0,
        [
            ((192, 288), BF), ((96, 288), BF), ((96, 288), BF), (codes.shape, codes.dtype),
            ((N_CHOICES, HALF, LANES), BF), ((6, HALF, LANES), BF),
        ],
        [((2, CH, LANES), F32), ((288, LANES), BF)],
        side_by_side((w_first, w_second), CH), side_by_side((codes, mirror), 2),
    )
    columns, pre, gate_in, hidden_mid = call(
        first_mid_kernel, 2, 1,
        [((288, 2 * MID), BF), ((2, CH, MID), F32), ((2, CH, MID), F32), ((2, 6) + plane, BF)],
        [((5, 8) + plane, BF)], codes, fp, part, w1,
    )
    (crossed,) = after((crossed,), hidden_mid)
    (back,) = call(
        back_kernel, 0.8, 0, [((2, 8) + plane, BF)], [((4, 64, 512), BF)], turn_choice, cotangent, cot_y, crossed
    )
    got = after(got, hidden_mid, back)
    columns_e, pre_e, gate_e, both, face_a, face_b = call(
        first_edge_kernel, 1, 0,
        [
            ((288, 4 * LANES), BF), ((CH, 4 * LANES), F32), ((CH, 4 * LANES), F32), ((2, 2, 8) + plane, BF),
            ((2, 2) + plane, BF), ((2, 2) + plane, BF),
        ],
        [], choose, fp, part, *got, pre, gate_in, hidden_mid, back, w1,
    )
    got = exchange(face_a, face_b)
    part = swap_y(both)
    second_part, through_e, columns_h, placed_f, placed_s = call(
        second_mid_kernel, 2.5, 1,
        [((2, CH, MID), F32), ((CH, 4 * LANES), F32), ((288, 2 * MID), BF), *[((128, 2 * MID), BF)] * 2],
        [((2, 5, 8) + plane, BF), ((288, 2 * MID), BF)],
        codes, both, part, pre, gate_in, w2, w2t,
    )
    got = after(got, second_part)
    far = swap_y(jnp.stack(got))
    columns_h, placed_f, placed_s = after((columns_h, placed_f, placed_s), *got)
    (raw,) = call(gradient_kernel, 1, 0, [((2, 288, LANES), F32)], [], columns, columns_h, placed_f, placed_s)
    n_bricks = features.shape[0] * lax.axis_size("xp") * lax.axis_size("yp")
    columns_he, grads = call(
        functools.partial(second_edge_kernel, 1.0 / n_bricks), 2, 0, [((288, 4 * LANES), BF), ((56, LANES), F32)],
        [((288, 4 * LANES), BF)]
        + [((128, 12 * LANES), BF), ((128, 4 * LANES), BF), ((256, 3 * LANES), BF)],
        choose, both, part, *got, far, pre_e, gate_e, through_e, columns, columns_e, raw, w2t,
    )
    total = grads + swap_y(grads)
    second_part, columns_he = after((second_part, columns_he), total)
    (second,) = call(compact_kernel, 0.5, 0, [((64, 512), BF)], [], second_part, columns_he, w2)
    second_y = swap_y(second)
    second_x = mirror_x(second)
    second_xy = swap_y(second_x)
    (denoised,) = call(
        turn_kernel, 0.9, 0, [((30, 2, 512), BF)], [((4, 64, 512), BF)], turn_choice, second, second_y, second_x, second_xy
    )
    denoised = denoised.transpose(1, 0, 2)
    n = lax.axis_size("xp")
    bit = 1
    while bit < n:
        total = total + lax.ppermute(total, "xp", [(i, i ^ bit) for i in range(n)])
        bit *= 2
    return denoised, total[0:27, 0:84], total[27:54, 0:84]


def solution(mesh):
    brick = P(("grp", "xp", "yp"))
    return jax.shard_map(
        on_device,
        mesh=mesh,
        in_specs=(brick, brick, P(), P(), brick, brick),
        out_specs=(brick, P("grp"), P("grp")),
        check_vma=False,
    )
```

```python
import functools

import jax
import jax.numpy as jnp
from jax import lax
from jax.experimental import pallas as pl
from jax.experimental.pallas import tpu as pltpu
from jax.sharding import PartitionSpec as P

BF = jnp.bfloat16
F32 = jnp.float32
CH = 32
LANES = 128
HALF = 16
OFFSETS = 27
MID = 8 * LANES
TURNS = (0, 63, 7 + 64, 56 + 64)


def iota(shape, dim):
    return lax.broadcasted_iota(jnp.int32, shape, dim)


def component_class(i):
    tensor = jnp.where(i < 30, 12 + ((i - 20) & 1), -1)
    return jnp.where(i < 8, i, jnp.where(i < 20, 8 + ((i - 8) & 3), tensor))


def component_index(i):
    return jnp.where(i < 8, 0, jnp.where(i < 20, (i - 8) >> 2, jnp.where(i < 30, (i - 20) >> 1, -1)))


def gate_class(i):
    tensor = jnp.where(i < 30, 4 + ((i - 20) & 1), -1)
    return jnp.where(i < 8, i, jnp.where(i < 20, (i - 8) & 3, tensor))


def out_class(c):
    tensor = jnp.where(c < 84, 12 + ((c - 80) >> 1), -2)
    return jnp.where(c < 64, c >> 3, jnp.where(c < 80, 8 + ((c - 64) >> 2), tensor))


def in_class(c):
    tensor = jnp.where(c < 84, 12 + ((c - 80) & 1), -2)
    return jnp.where(c < 64, c & 7, jnp.where(c < 80, 8 + ((c - 64) & 3), tensor))


def one(condition, kind=BF):
    return jnp.where(condition, 1.0, 0.0).astype(kind)


def plane_source(q):
    lane = q & 127
    row = (lane * 205) >> 11
    y, z = row - 1, lane - 10 * row - 1
    inside = (y >= 0) & (y < 8) & (z >= 0) & (z < 8)
    return jnp.where(inside, 64 * (q >> 7) + 8 * y + z, -1)


def spread_table():
    return one(plane_source(iota((128, 256), 1)) == iota((128, 256), 0))


def compact_table():
    return one(plane_source(iota((256, 128), 0)) == iota((256, 128), 1))


def turn_table(r):
    return one((iota((128, 128), 1) ^ TURNS[r]) == iota((128, 128), 0))


def turns_table():
    return jnp.concatenate([turn_table(r) for r in range(4)], axis=0)


def turns_spread_table():
    source = plane_source(iota((128, 256), 1))
    return jnp.concatenate([one((source ^ TURNS[r]) == iota((128, 256), 0)) for r in range(4)], axis=0)


def turn_signs(r, shape):
    i = iota(shape, 0) & (CH - 1)
    m = component_index(i)
    vector = (i >= 8) & (i < 20) & (m != r - 1)
    tensor = (i >= 20) & (m < 3) & (m != 3 - r)
    return jnp.where(vector | tensor, -1.0, 1.0).astype(BF)


def region_masks():
    lane = iota((1, LANES), 1)
    row = (lane * 205) >> 11
    col = lane - 10 * row

    def part(v):
        return jnp.where(v == 0, 0, jnp.where(v == 9, 2, 1))

    region = jnp.where(row < 10, 3 * part(row) + part(col), -1)
    return [one(region == o) for o in range(9)]


def dot(a, b, **kw):
    return jnp.dot(a, b, preferred_element_type=F32, **kw)


def dot_t(a, b):
    return lax.dot_general(a, b, (((1,), (1,)), ((), ())), preferred_element_type=F32)


def is_odd():
    return (lax.axis_index("xp") & 1) == 1


def gathered(pieces_of, masks):
    total = None
    for b in range(3):
        for c in range(3):
            o = 3 * b + c
            planes = jnp.concatenate(pieces_of(o), axis=0)
            shift = ((b - 1) * 80 + (c - 1) * 8) % LANES
            if shift:
                planes = pltpu.roll(planes, shift, 1)
            planes = planes * masks[o]
            total = planes if total is None else total + planes
    return total


def unfold(planes, count, columns, start):
    for o in range(9):
        shift = (11 - 10 * (o // 3) - o % 3) % LANES
        moved = pltpu.roll(planes, shift, 1) if shift else planes
        for p in range(count):
            at = start + p * LANES
            columns[o * CH : (o + 1) * CH, at : at + LANES] = moved[p * CH : (p + 1) * CH]


def mid_columns(choose, masks, own, part, columns):
    same_y, other_y = ([planes(s).reshape(16, HALF, LANES) for s in range(2)] for planes in (own, part))
    for n in range(2):
        rows = [pick(choose, OTHER_Y + 2 * n + k, same_y, other_y) for k in range(2)]
        found = (rows[0], same_y, rows[1])

        def pieces(o):
            first, second = found[o // 3]
            at = MID_SLOTS + 2 * (9 * n + o)
            return [(first * choose[at] + second * choose[at + 1]).reshape(8 * CH, LANES)]

        unfold(gathered(pieces, masks), 8, columns, n * MID)


def edge_planes_of(own, part, received, far):
    odd = is_odd()
    low = [f(s, 7) for f in (own, part) for s in range(2)]
    high = [f(s, 0) for f in (own, part) for s in range(2)]
    for faces in (received, far):
        for s in range(2):
            first, second = faces(0, s), faces(1, s)
            low.append(jnp.where(odd, first, second))
            high.append(jnp.where(odd, second, first))
    return [[plane.reshape(2, HALF, LANES) for plane in side] for side in (low, high)]


OTHER_X, OTHER_Y, SLOTS, MID_SLOTS, N_CHOICES = 0, 8, 16, 88, 124


def pick(choose, row, here, there):
    return [p * choose[row + 4] + q * choose[row] for p, q in zip(here, there)]


def edge_columns(choose, masks, candidates, columns):
    found = []
    for e in range(4):
        own, part, near, far = (candidates[e & 1][2 * k : 2 * k + 2] for k in range(4))
        same_y = pick(choose, OTHER_X + e, own, near)
        other_y = pick(choose, OTHER_X + e, part, far)
        rows = [pick(choose, OTHER_Y + 2 * (e >> 1) + k, same_y, other_y) for k in range(2)]
        found.append((rows[0], same_y, rows[1]))

    def pieces(o):
        planes = []
        for e in range(4):
            first, second = found[e][o // 3]
            at = SLOTS + 2 * (9 * e + o)
            planes.append((first * choose[at] + second * choose[at + 1]).reshape(CH, LANES))
        return planes

    unfold(gathered(pieces, masks), 4, columns, 0)


def write_choices(codes, mirror, choose, turn_choice):
    lane = iota(codes.shape, 1)
    a = (lane * 57) >> 9
    b = ((lane * 171) >> 9) - 3 * a
    d = codes >> 1
    dx = (d * 11) >> 5
    dy = d - 3 * dx
    there = (codes < 18) & (lane < OFFSETS)
    slot = jnp.where(there, codes & 1, -1)
    shape = (HALF, LANES)

    def flag(condition):
        return jnp.max(jnp.where(there & condition, 1.0, 0.0), axis=1, keepdims=True)

    for k in range(2):
        for base, found in ((OTHER_X, flag((a == 2 * k) & (dx != 1))), (OTHER_Y, flag((b == 2 * k) & (dy != 1)))):
            for n in range(2):
                wide = jnp.broadcast_to(found[n : n + 1], shape)
                choose[base + 2 * n + k] = wide.astype(BF)
                choose[base + 4 + 2 * n + k] = (1.0 - wide).astype(BF)
    for e in range(4):
        n = e >> 1
        for o in range(9):
            at = o + 18 * (e & 1)
            wide = jnp.broadcast_to(slot[n : n + 1, at : at + 1], shape)
            for s in range(2):
                choose[SLOTS + 2 * (9 * e + o) + s] = one(wide == s)
    for n in range(2):
        for o in range(9):
            wide = jnp.broadcast_to(slot[n : n + 1, 9 + o : 10 + o], shape)
            for s in range(2):
                choose[MID_SLOTS + 2 * (9 * n + o) + s] = one(wide == s)
        for r in range(3):
            wide = jnp.broadcast_to(mirror[n : n + 1, r : r + 1], shape)
            turn_choice[3 * n + r] = wide.astype(F32).astype(BF)


def chosen(turn_choice, n, r, first, second):
    tile = jnp.concatenate([turn_choice[3 * n + r - 1]] * 4, axis=1)
    slot = jnp.concatenate([tile, tile], axis=0)[: first.shape[0]]
    return second * slot + first * (1.0 - slot).astype(BF)


def fold_mid(stacked, row):
    zero = jnp.zeros((CH, LANES), F32)
    before = jnp.concatenate([zero, stacked[row : row + CH, : MID - LANES]], axis=1)
    after = jnp.concatenate([stacked[row + 2 * CH : row + 3 * CH, LANES:], zero], axis=1)
    return before + stacked[row + CH : row + 2 * CH] + after


def edge_terms(stacked, row):
    blocks = []
    for e in range(4):
        first = row + 2 * CH * (e & 1)
        blocks.append(stacked[first : first + CH, e * LANES : (e + 1) * LANES])
    return jnp.concatenate(blocks, axis=1)


def edge_planes(ref):
    return jnp.concatenate([ref[e >> 1, :, 7 * (e & 1) * LANES : (7 * (e & 1) + 1) * LANES] for e in range(4)], axis=1)


def write_faces(face_a, face_b, index, plane_low, plane_high):
    odd = is_odd()
    face_a[index] = jnp.where(odd, plane_low, plane_high)
    face_b[index] = jnp.where(odd, plane_high, plane_low)


def spread_kernel(features, fp, staged):
    staged[...] = jnp.zeros_like(staged)
    for n in range(2):
        staged[n * CH : n * CH + 30, :] = features[n]
    rows = jnp.concatenate([staged[:, k * 128 : (k + 1) * 128] for k in range(4)], axis=0)
    planes = dot(rows, spread_table()).astype(BF)
    for n in range(2):
        for x in range(8):
            first = (x >> 1) * 2 * CH + n * CH
            fp[n, x] = planes[first : first + CH, (x & 1) * LANES : (x & 1) * LANES + LANES]


def weights_kernel(packed, small, one_out, two_out, turned_out, choose, turn_choice, padded, left):
    shape = (CH, LANES)
    i, c = iota(shape, 0), iota(shape, 1)
    double = jnp.where(i >= 20, 2.0, 1.0)
    j = iota((LANES, LANES), 1) & (CH - 1)
    col = iota((LANES, LANES), 0)
    by_in = one(in_class(col) == component_class(j))
    by_out = one(out_class(col) == component_class(j))
    rows_out = jnp.where(component_class(i) == out_class(c), double, 0.0)
    rows_gate = one(gate_class(i) == out_class(c), F32)
    rows_in = jnp.where(component_class(i) == in_class(c), double, 0.0)
    same = component_index(i) == component_index(c & (CH - 1))
    quarter = c >> 5
    padded[...] = jnp.zeros_like(padded)
    for which in range(2):
        padded[which, 0:27, 0:84] = packed[0:27, which * LANES : which * LANES + 84].astype(F32)
    write_choices(small[:, 0:LANES], small[:, LANES : 2 * LANES], choose, turn_choice)
    for which, rows, columns, blocks, out, base, flip in (
        (0, rows_out, by_in, True, one_out, 0, False),
        (0, rows_gate, by_in, False, one_out, 96, False),
        (1, rows_out, by_in, True, two_out, 0, False),
        (1, rows_in, by_out, True, turned_out, 0, True),
    ):
        for a in range(3):
            for bc in range(9):
                o = 9 * a + bc
                o = 26 - o if flip else o
                left[bc * CH : (bc + 1) * CH, :] = (rows * padded[which, o : o + 1, :]).astype(BF)
            found = dot(left[...], columns)
            for g in range(3):
                tile = jnp.zeros(shape, F32)
                for q in range(min(4, 9 - 4 * g)):
                    bc = 4 * g + q
                    keep = (quarter == q) & same if blocks else quarter == q
                    tile = tile + jnp.where(keep, found[bc * CH : (bc + 1) * CH], 0.0)
                width = min(128, 288 - 128 * g)
                out[base + a * CH : base + (a + 1) * CH, g * 128 : g * 128 + width] = tile[:, :width].astype(BF)


def first_mid_kernel(choose, own, part, w_first, columns, pre, gate_in, hidden_mid):
    masks = region_masks()
    inside = masks[4].astype(F32)
    mid_columns(choose, masks, lambda s: own[s], lambda s: part[s], columns)
    for n in range(2):
        stacked = dot(w_first[...], columns[:, n * MID : (n + 1) * MID])
        a, g = fold_mid(stacked, 0), fold_mid(stacked, 96)
        pre[n] = a
        gate_in[n] = g
        for x in range(1, 7):
            at = slice(x * LANES, (x + 1) * LANES)
            hidden_mid[n, x - 1] = (a[:, at] * jax.nn.sigmoid(g[:, at]) * inside).astype(BF)


def turned_sum(staged, table):
    rows = []
    for k in range(4):
        blocks = (k, k, 3 - k, 3 - k)
        rows.append(jnp.concatenate([staged[r, :, 128 * b : 128 * b + 128] for r, b in enumerate(blocks)], axis=1))
    return dot(jnp.concatenate(rows, axis=0), table) * 0.25


def back_kernel(turn_choice, own, across_y, crossed, back, staged):
    zero2 = jnp.zeros((2, 512), BF)
    for n in range(2):
        for r in range(4):
            if r == 0:
                value = own[n]
            else:
                first, second = (across_y[0], across_y[1]) if r == 1 else (crossed[2 * r - 4], crossed[2 * r - 3])
                value = chosen(turn_choice, n, r, first, second) * turn_signs(r, (30, 512))
            staged[r, n * CH : n * CH + 30, :] = value
            staged[r, n * CH + 30 : (n + 1) * CH, :] = zero2
    planes = turned_sum(staged, turns_spread_table()).astype(BF)
    for n in range(2):
        for x in range(8):
            first = (x >> 1) * 2 * CH + n * CH
            back[n, x] = planes[first : first + CH, (x & 1) * LANES : (x & 1) * LANES + LANES]


def first_edge_kernel(
    choose, own, part, got_a, got_b, pre, gate_in, hidden_mid, back, w_first,
    columns, pre_edge, gate_edge, both, face_a, face_b,
):
    masks = region_masks()
    inside = jnp.concatenate([masks[4].astype(F32)] * 4, axis=1)
    candidates = edge_planes_of(
        lambda s, x: own[s, x], lambda s, x: part[s, x],
        lambda which, s: (got_a, got_b)[which][s], lambda which, s: (got_a, got_b)[which][2 + s],
    )
    edge_columns(choose, masks, candidates, columns)
    stacked = dot(w_first[...], columns[...])
    a = edge_planes(pre) + edge_terms(stacked, 0)
    g = edge_planes(gate_in) + edge_terms(stacked, 96)
    pre_edge[...] = a
    gate_edge[...] = g
    hidden = (a * jax.nn.sigmoid(g) * inside).astype(BF)
    for n in range(2):
        outer = [hidden[:, e * LANES : (e + 1) * LANES] for e in (2 * n, 2 * n + 1)]
        both[0, n, 0], both[0, n, 7] = outer
        write_faces(face_a, face_b, (0, n), *outer)
        for x in range(1, 7):
            both[0, n, x] = hidden_mid[n, x - 1]
        for x in range(8):
            both[1, n, x] = back[n, x]
        write_faces(face_a, face_b, (1, n), back[n, 0], back[n, 7])


def gate_back(grad, a, g, rows8, inside):
    sig = jax.nn.sigmoid(g)
    through = grad * sig
    left, parts = grad * a, []
    for _ in range(3):
        parts.append(left.astype(BF))
        left = left - parts[-1].astype(F32)
    extra = dot(jnp.concatenate([rows8] * 3, axis=1), jnp.concatenate(parts, axis=0))
    sig8 = sig[0:8]
    top = through[0:8] + sig8 * (1.0 - sig8) * extra
    return (jnp.concatenate([top, through[8:]], axis=0) * inside).astype(BF)


def gate_rows():
    return one(gate_class(iota((8, CH), 1)) == iota((8, CH), 0))


def second_mid_kernel(
    choose, own, part, pre, gate_in, w_second, w_turned, second, through_edge, columns_h, placed_f, placed_s,
    columns_b,
):
    masks = region_masks()
    inside = jnp.concatenate([masks[4].astype(F32)] * 6, axis=1)
    for f, columns in ((0, columns_h), (1, columns_b)):
        mid_columns(choose, masks, lambda s: own[f, s], lambda s: part[f, s], columns)
    zero = jnp.zeros((CH, LANES), BF)
    rows8 = gate_rows()
    for placed in (placed_f, placed_s):
        placed[3 * CH :, :] = jnp.zeros((CH, 2 * MID), BF)

    def place(placed, n, planes, first, last):
        for a in range(3):
            for q in range(8):
                x = q + 1 - a
                at = (8 * n + q) * LANES
                placed[a * CH : (a + 1) * CH, at : at + LANES] = planes(x) if first <= x <= last else zero

    for n in range(2):
        here = slice(n * MID, (n + 1) * MID)
        second[n] = fold_mid(dot(w_second[...], columns_h[:, here]), 0)
        place(placed_s, n, lambda x: own[1, n, x], 0, 7)
        grad = fold_mid(dot(w_turned[...], columns_b[:, here]), 0)
        through_edge[:, 2 * n * LANES : (2 * n + 1) * LANES] = grad[:, :LANES]
        through_edge[:, (2 * n + 1) * LANES : (2 * n + 2) * LANES] = grad[:, 7 * LANES :]
        inner = slice(LANES, 7 * LANES)
        back_pre = gate_back(grad[:, inner], pre[n, :, inner], gate_in[n, :, inner], rows8, inside)
        place(placed_f, n, lambda x: back_pre[:, (x - 1) * LANES : x * LANES], 1, 6)


def gradient_kernel(columns_f, columns_h, placed_f, placed_s, raw):
    raw[0] = dot_t(columns_f[...], placed_f[...])
    raw[1] = dot_t(columns_h[...], placed_s[...])


def second_edge_kernel(
    scale, choose, own, part, got_a, got_b, far, pre_edge, gate_edge, through_edge,
    columns_f, columns_fe, raw, w_turned, columns_h, grads,
    columns_b, placed_f, placed_s, place,
):
    masks = region_masks()
    inside = jnp.concatenate([masks[4].astype(F32)] * 4, axis=1)
    for f, columns in ((0, columns_h), (1, columns_b)):
        candidates = edge_planes_of(
            lambda s, x: own[f, s, x], lambda s, x: part[f, s, x],
            lambda which, s: (got_a, got_b)[which][f, s], lambda which, s: far[which, f, s],
        )
        edge_columns(choose, masks, candidates, columns)
    more_t = edge_terms(dot(w_turned[...], columns_b[...]), 0)
    back_pre = gate_back(through_edge[...] + more_t, pre_edge[...], gate_edge[...], gate_rows(), inside)
    placed_f[...] = jnp.zeros_like(placed_f)
    placed_s[...] = jnp.zeros_like(placed_s)
    for n in range(2):
        for side in range(2):
            at = (2 * n + side) * LANES
            a = 2 * side
            placed_s[a * CH : (a + 1) * CH, at : at + LANES] = own[1, n, 7 * side]
            for a in range(3):
                to = (6 * n + 3 * side + a) * LANES
                placed_f[a * CH : (a + 1) * CH, to : to + LANES] = back_pre[:, at : at + LANES]
    pieces = []
    for n in range(2):
        mid, edge = n * MID, 2 * n * LANES
        pieces += [
            columns_fe[:, edge : edge + LANES], columns_f[:, mid : mid + 2 * LANES],
            columns_f[:, mid + 6 * LANES : mid + MID], columns_fe[:, edge + LANES : edge + 2 * LANES],
        ]
    shape = (CH, LANES)
    i, c = iota(shape, 0), iota(shape, 1)
    lift = jnp.where(component_class(i) == out_class(c), jnp.where(i >= 20, 2.0, 1.0), 0.0).astype(BF)
    keep = one(component_class(i) == in_class(c), F32)
    same = one(component_index(i) == component_index(c & (CH - 1)), F32)
    place[...] = jnp.zeros_like(place)
    for a in range(3):
        for half in (0, LANES):
            place[half + a * CH : half + (a + 1) * CH, a * LANES : (a + 1) * LANES] = lift
    found = (
        raw[0] + dot_t(jnp.concatenate(pieces, axis=1), placed_f[...]),
        raw[1] + dot_t(columns_h[...], placed_s[...]),
    )
    for layer in range(2):
        masked = (found[layer].reshape(9, CH, LANES) * same).reshape(9 * CH, LANES)
        top = masked.astype(BF)
        rest = (masked - top.astype(F32)).astype(BF)
        lifted = dot(jnp.concatenate([top, rest], axis=1), place[...])
        for a in range(3):
            block = lifted[:, a * LANES : (a + 1) * LANES].reshape(9, CH, LANES) * keep
            first = 27 * layer + 9 * a
            grads[first : first + 9, :] = jnp.sum(block, axis=1) * scale
    grads[54:56, :] = jnp.zeros((2, LANES), F32)


def compact_kernel(second_in, columns, w_second, second):
    more = edge_terms(dot(w_second[...], columns[...]), 0)
    zero = jnp.zeros((CH, LANES), F32)
    rows = []
    for n in range(2):
        for k in range(4):
            planes = second_in[n, :, k * 256 : (k + 1) * 256]
            if k == 0:
                planes = planes + jnp.concatenate([more[:, 2 * n * LANES : (2 * n + 1) * LANES], zero], axis=1)
            if k == 3:
                planes = planes + jnp.concatenate([zero, more[:, (2 * n + 1) * LANES : (2 * n + 2) * LANES]], axis=1)
            rows.append(planes.astype(BF))
    packed = dot(jnp.concatenate(rows, axis=0), compact_table()).astype(BF)
    for n in range(2):
        for k in range(4):
            first = (4 * n + k) * CH
            second[n * CH : (n + 1) * CH, k * LANES : (k + 1) * LANES] = packed[first : first + CH]


def turn_kernel(turn_choice, own, across_y, across_x, across, out, staged):
    for n in range(2):
        staged[0, n * CH : (n + 1) * CH, :] = own[n * CH : (n + 1) * CH, :]
        for r, ref in ((1, across_y), (2, across_x), (3, across)):
            value = chosen(turn_choice, n, r, ref[0:CH, :], ref[CH : 2 * CH, :])
            staged[r, n * CH : (n + 1) * CH, :] = value * turn_signs(r, (CH, 512))
    result = turned_sum(staged, turns_table()).astype(BF)
    for k in range(4):
        for n in range(2):
            first = (2 * k + n) * CH
            out[:, n, k * 128 : (k + 1) * 128] = result[first : first + 30]


SMEM = pl.BlockSpec(memory_space=pltpu.SMEM)
VMEM = pl.BlockSpec(memory_space=pltpu.VMEM)


def call(kernel, us, n_smem, outs, scratch, *args):
    return pl.pallas_call(
        kernel,
        out_shape=tuple(jax.ShapeDtypeStruct(s, t) for s, t in outs),
        in_specs=[SMEM] * n_smem + [VMEM] * (len(args) - n_smem),
        out_specs=tuple([VMEM] * len(outs)),
        scratch_shapes=[pltpu.VMEM(s, t) for s, t in scratch],
        compiler_params=pltpu.CompilerParams(vmem_limit_bytes=24 * 1024 * 1024),
        cost_estimate=pl.CostEstimate(flops=0, transcendentals=0, bytes_accessed=int(us * 3_000_000)),
    )(*args)


def swap_y(x):
    n = lax.axis_size("yp")
    return lax.ppermute(x, "yp", [(i, n - 1 - i) for i in range(n)])


def mirror_x(x):
    n = lax.axis_size("xp")
    return lax.ppermute(x, "xp", [(i, n - 1 - i) for i in range(n)])


def pair_swap(x, first):
    n = lax.axis_size("xp")
    pairs = []
    for i in range(first, n - 1, 2):
        pairs += [(i, i + 1), (i + 1, i)]
    return lax.ppermute(x, "xp", pairs)


def exchange(face_a, face_b):
    got_b = pair_swap(face_b, 1)
    got_a = pair_swap(face_a, 0)
    return got_a, got_b


def after(arrays, *others):
    return lax.optimization_barrier((tuple(arrays), others))[0]


def side_by_side(arrays, rows):
    total = None
    for k, x in enumerate(arrays):
        x = jnp.pad(x, ((0, rows - x.shape[0]), (k * LANES, (len(arrays) - k) * LANES - LANES + LANES - x.shape[1])))
        total = x if total is None else total + x
    return lax.optimization_barrier(total)


def on_device(features, cotangent, w_first, w_second, codes, mirror):
    plane = (CH, LANES)
    cot_y = swap_y(cotangent)
    crossed = mirror_x(jnp.concatenate([cotangent, cot_y], axis=0))
    (fp,) = call(spread_kernel, 0.2, 0, [((2, 8) + plane, BF)], [((64, 512), BF)], features)
    part = swap_y(fp)
    low, high = (jnp.concatenate([fp[:, x], part[:, x]], axis=0) for x in (0, 7))
    odd = is_odd()
    got = exchange(jnp.where(odd, low, high), jnp.where(odd, high, low))
    w_first, w_second, codes, mirror = after((w_first, w_second, codes, mirror), part)
    w1, w2, w2t, choose, turn_choice = call(
        weights_kernel, 1, 0,
        [
            ((192, 288), BF), ((96, 288), BF), ((96, 288), BF),
            ((N_CHOICES, HALF, LANES), BF), ((6, HALF, LANES), BF),
        ],
        [((2, CH, LANES), F32), ((288, LANES), BF)],
        side_by_side((w_first, w_second), CH), side_by_side((codes, mirror), 2),
    )
    columns, pre, gate_in, hidden_mid = call(
        first_mid_kernel, 2, 0,
        [((288, 2 * MID), BF), ((2, CH, MID), F32), ((2, CH, MID), F32), ((2, 6) + plane, BF)],
        [], choose, fp, part, w1,
    )
    (crossed,) = after((crossed,), hidden_mid)
    (back,) = call(
        back_kernel, 0.8, 0, [((2, 8) + plane, BF)], [((4, 64, 512), BF)], turn_choice, cotangent, cot_y, crossed
    )
    got = after(got, hidden_mid, back)
    columns_e, pre_e, gate_e, both, face_a, face_b = call(
        first_edge_kernel, 1, 0,
        [
            ((288, 4 * LANES), BF), ((CH, 4 * LANES), F32), ((CH, 4 * LANES), F32), ((2, 2, 8) + plane, BF),
            ((2, 2) + plane, BF), ((2, 2) + plane, BF),
        ],
        [], choose, fp, part, *got, pre, gate_in, hidden_mid, back, w1,
    )
    got = exchange(face_a, face_b)
    part = swap_y(both)
    second_part, through_e, columns_h, placed_f, placed_s = call(
        second_mid_kernel, 2.5, 0,
        [((2, CH, MID), F32), ((CH, 4 * LANES), F32), ((288, 2 * MID), BF), *[((128, 2 * MID), BF)] * 2],
        [((288, 2 * MID), BF)],
        choose, both, part, pre, gate_in, w2, w2t,
    )
    got = after(got, second_part)
    far = swap_y(jnp.stack(got))
    columns_h, placed_f, placed_s = after((columns_h, placed_f, placed_s), *got)
    (raw,) = call(gradient_kernel, 1, 0, [((2, 288, LANES), F32)], [], columns, columns_h, placed_f, placed_s)
    n_bricks = features.shape[0] * lax.axis_size("xp") * lax.axis_size("yp")
    columns_he, grads = call(
        functools.partial(second_edge_kernel, 1.0 / n_bricks), 2, 0, [((288, 4 * LANES), BF), ((56, LANES), F32)],
        [((288, 4 * LANES), BF)]
        + [((128, 12 * LANES), BF), ((128, 4 * LANES), BF), ((256, 3 * LANES), BF)],
        choose, both, part, *got, far, pre_e, gate_e, through_e, columns, columns_e, raw, w2t,
    )
    total = grads + swap_y(grads)
    second_part, columns_he = after((second_part, columns_he), total)
    (second,) = call(compact_kernel, 0.5, 0, [((64, 512), BF)], [], second_part, columns_he, w2)
    second_y = swap_y(second)
    second_x = mirror_x(second)
    second_xy = swap_y(second_x)
    (denoised,) = call(
        turn_kernel, 0.9, 0, [((30, 2, 512), BF)], [((4, 64, 512), BF)], turn_choice, second, second_y, second_x, second_xy
    )
    denoised = denoised.transpose(1, 0, 2)
    n = lax.axis_size("xp")
    bit = 1
    while bit < n:
        total = total + lax.ppermute(total, "xp", [(i, i ^ bit) for i in range(n)])
        bit *= 2
    return denoised, total[0:27, 0:84], total[27:54, 0:84]


def solution(mesh):
    brick = P(("grp", "xp", "yp"))
    return jax.shard_map(
        on_device,
        mesh=mesh,
        in_specs=(brick, brick, P(), P(), brick, brick),
        out_specs=(brick, P("grp"), P("grp")),
        check_vma=False,
    )
```

```python
import functools

import jax
import jax.numpy as jnp
from jax import lax
from jax.experimental import pallas as pl
from jax.experimental.pallas import tpu as pltpu
from jax.sharding import PartitionSpec as P

BF = jnp.bfloat16
F32 = jnp.float32
CH = 32
LANES = 128
HALF = 16
OFFSETS = 27
MID = 8 * LANES
TURNS = (0, 63, 7 + 64, 56 + 64)


def iota(shape, dim):
    return lax.broadcasted_iota(jnp.int32, shape, dim)


def component_class(i):
    tensor = jnp.where(i < 30, 12 + ((i - 20) & 1), -1)
    return jnp.where(i < 8, i, jnp.where(i < 20, 8 + ((i - 8) & 3), tensor))


def component_index(i):
    return jnp.where(i < 8, 0, jnp.where(i < 20, (i - 8) >> 2, jnp.where(i < 30, (i - 20) >> 1, -1)))


def gate_class(i):
    tensor = jnp.where(i < 30, 4 + ((i - 20) & 1), -1)
    return jnp.where(i < 8, i, jnp.where(i < 20, (i - 8) & 3, tensor))


def out_class(c):
    tensor = jnp.where(c < 84, 12 + ((c - 80) >> 1), -2)
    return jnp.where(c < 64, c >> 3, jnp.where(c < 80, 8 + ((c - 64) >> 2), tensor))


def in_class(c):
    tensor = jnp.where(c < 84, 12 + ((c - 80) & 1), -2)
    return jnp.where(c < 64, c & 7, jnp.where(c < 80, 8 + ((c - 64) & 3), tensor))


def one(condition, kind=BF):
    return jnp.where(condition, 1.0, 0.0).astype(kind)


def plane_source(q):
    lane = q & 127
    row = (lane * 205) >> 11
    y, z = row - 1, lane - 10 * row - 1
    inside = (y >= 0) & (y < 8) & (z >= 0) & (z < 8)
    return jnp.where(inside, 64 * (q >> 7) + 8 * y + z, -1)


def spread_table():
    return one(plane_source(iota((128, 256), 1)) == iota((128, 256), 0))


def compact_table():
    return one(plane_source(iota((256, 128), 0)) == iota((256, 128), 1))


def turn_table(r):
    return one((iota((128, 128), 1) ^ TURNS[r]) == iota((128, 128), 0))


def turns_table():
    return jnp.concatenate([turn_table(r) for r in range(4)], axis=0)


def turns_spread_table():
    source = plane_source(iota((128, 256), 1))
    return jnp.concatenate([one((source ^ TURNS[r]) == iota((128, 256), 0)) for r in range(4)], axis=0)


def turn_signs(r, shape):
    i = iota(shape, 0) & (CH - 1)
    m = component_index(i)
    vector = (i >= 8) & (i < 20) & (m != r - 1)
    tensor = (i >= 20) & (m < 3) & (m != 3 - r)
    return jnp.where(vector | tensor, -1.0, 1.0).astype(BF)


def region_masks():
    lane = iota((1, LANES), 1)
    row = (lane * 205) >> 11
    col = lane - 10 * row

    def part(v):
        return jnp.where(v == 0, 0, jnp.where(v == 9, 2, 1))

    region = jnp.where(row < 10, 3 * part(row) + part(col), -1)
    return [one(region == o) for o in range(9)]


def dot(a, b, **kw):
    return jnp.dot(a, b, preferred_element_type=F32, **kw)


def dot_t(a, b):
    return lax.dot_general(a, b, (((1,), (1,)), ((), ())), preferred_element_type=F32)


def is_odd():
    return (lax.axis_index("xp") & 1) == 1


def gathered(pieces_of, masks):
    total = None
    for b in range(3):
        for c in range(3):
            o = 3 * b + c
            planes = jnp.concatenate(pieces_of(o), axis=0)
            shift = ((b - 1) * 80 + (c - 1) * 8) % LANES
            if shift:
                planes = pltpu.roll(planes, shift, 1)
            planes = planes * masks[o]
            total = planes if total is None else total + planes
    return total


def unfold(planes, count, columns, start):
    for o in range(9):
        shift = (11 - 10 * (o // 3) - o % 3) % LANES
        moved = pltpu.roll(planes, shift, 1) if shift else planes
        for p in range(count):
            at = start + p * LANES
            columns[o * CH : (o + 1) * CH, at : at + LANES] = moved[p * CH : (p + 1) * CH]


def mid_columns(choose, masks, own, part, columns):
    same_y, other_y = ([planes(s).reshape(16, HALF, LANES) for s in range(2)] for planes in (own, part))
    for n in range(2):
        rows = [pick(choose, OTHER_Y + 2 * n + k, same_y, other_y) for k in range(2)]
        found = (rows[0], same_y, rows[1])

        def pieces(o):
            first, second = found[o // 3]
            at = MID_SLOTS + 2 * (9 * n + o)
            return [(first * choose[at] + second * choose[at + 1]).reshape(8 * CH, LANES)]

        unfold(gathered(pieces, masks), 8, columns, n * MID)


def edge_planes_of(own, part, received, far):
    odd = is_odd()
    low = [f(s, 7) for f in (own, part) for s in range(2)]
    high = [f(s, 0) for f in (own, part) for s in range(2)]
    for faces in (received, far):
        for s in range(2):
            first, second = faces(0, s), faces(1, s)
            low.append(jnp.where(odd, first, second))
            high.append(jnp.where(odd, second, first))
    return [[plane.reshape(2, HALF, LANES) for plane in side] for side in (low, high)]


OTHER_X, OTHER_Y, SLOTS, MID_SLOTS, N_CHOICES = 0, 8, 16, 88, 124


def pick(choose, row, here, there):
    return [p * choose[row + 4] + q * choose[row] for p, q in zip(here, there)]


def edge_columns(choose, masks, candidates, columns):
    found = []
    for e in range(4):
        own, part, near, far = (candidates[e & 1][2 * k : 2 * k + 2] for k in range(4))
        same_y = pick(choose, OTHER_X + e, own, near)
        other_y = pick(choose, OTHER_X + e, part, far)
        rows = [pick(choose, OTHER_Y + 2 * (e >> 1) + k, same_y, other_y) for k in range(2)]
        found.append((rows[0], same_y, rows[1]))

    def pieces(o):
        planes = []
        for e in range(4):
            first, second = found[e][o // 3]
            at = SLOTS + 2 * (9 * e + o)
            planes.append((first * choose[at] + second * choose[at + 1]).reshape(CH, LANES))
        return planes

    unfold(gathered(pieces, masks), 4, columns, 0)


def write_choices(codes, mirror, choose, turn_choice):
    lane = iota(codes.shape, 1)
    a = (lane * 57) >> 9
    b = ((lane * 171) >> 9) - 3 * a
    d = codes >> 1
    dx = (d * 11) >> 5
    dy = d - 3 * dx
    there = (codes < 18) & (lane < OFFSETS)
    slot = jnp.where(there, codes & 1, -1)
    shape = (HALF, LANES)

    def flag(condition):
        return jnp.max(jnp.where(there & condition, 1.0, 0.0), axis=1, keepdims=True)

    for k in range(2):
        for base, found in ((OTHER_X, flag((a == 2 * k) & (dx != 1))), (OTHER_Y, flag((b == 2 * k) & (dy != 1)))):
            for n in range(2):
                wide = jnp.broadcast_to(found[n : n + 1], shape)
                choose[base + 2 * n + k] = wide.astype(BF)
                choose[base + 4 + 2 * n + k] = (1.0 - wide).astype(BF)
    for e in range(4):
        n = e >> 1
        for o in range(9):
            at = o + 18 * (e & 1)
            wide = jnp.broadcast_to(slot[n : n + 1, at : at + 1], shape)
            for s in range(2):
                choose[SLOTS + 2 * (9 * e + o) + s] = one(wide == s)
    for n in range(2):
        for o in range(9):
            wide = jnp.broadcast_to(slot[n : n + 1, 9 + o : 10 + o], shape)
            for s in range(2):
                choose[MID_SLOTS + 2 * (9 * n + o) + s] = one(wide == s)
        for r in range(3):
            wide = jnp.broadcast_to(mirror[n : n + 1, r : r + 1], shape)
            turn_choice[3 * n + r] = wide.astype(F32).astype(BF)


def chosen(turn_choice, n, r, first, second):
    tile = jnp.concatenate([turn_choice[3 * n + r - 1]] * 4, axis=1)
    slot = jnp.concatenate([tile, tile], axis=0)[: first.shape[0]]
    return second * slot + first * (1.0 - slot).astype(BF)


def fold_mid(stacked, row):
    zero = jnp.zeros((CH, LANES), F32)
    before = jnp.concatenate([zero, stacked[row : row + CH, : MID - LANES]], axis=1)
    after = jnp.concatenate([stacked[row + 2 * CH : row + 3 * CH, LANES:], zero], axis=1)
    return before + stacked[row + CH : row + 2 * CH] + after


def edge_terms(stacked, row):
    blocks = []
    for e in range(4):
        first = row + 2 * CH * (e & 1)
        blocks.append(stacked[first : first + CH, e * LANES : (e + 1) * LANES])
    return jnp.concatenate(blocks, axis=1)


def edge_planes(ref):
    return jnp.concatenate([ref[e >> 1, :, 7 * (e & 1) * LANES : (7 * (e & 1) + 1) * LANES] for e in range(4)], axis=1)


def write_faces(face_a, face_b, index, plane_low, plane_high):
    odd = is_odd()
    face_a[index] = jnp.where(odd, plane_low, plane_high)
    face_b[index] = jnp.where(odd, plane_high, plane_low)


def spread_kernel(features, fp, staged):
    staged[...] = jnp.zeros_like(staged)
    for n in range(2):
        staged[n * CH : n * CH + 30, :] = features[n]
    rows = jnp.concatenate([staged[:, k * 128 : (k + 1) * 128] for k in range(4)], axis=0)
    planes = dot(rows, spread_table()).astype(BF)
    for n in range(2):
        for x in range(8):
            first = (x >> 1) * 2 * CH + n * CH
            fp[n, x] = planes[first : first + CH, (x & 1) * LANES : (x & 1) * LANES + LANES]


def weights_kernel(packed, small, one_out, two_out, turned_out, choose, turn_choice, padded, left):
    shape = (CH, LANES)
    i, c = iota(shape, 0), iota(shape, 1)
    double = jnp.where(i >= 20, 2.0, 1.0)
    j = iota((LANES, LANES), 1) & (CH - 1)
    col = iota((LANES, LANES), 0)
    by_in = one(in_class(col) == component_class(j))
    by_out = one(out_class(col) == component_class(j))
    rows_out = jnp.where(component_class(i) == out_class(c), double, 0.0)
    rows_gate = one(gate_class(i) == out_class(c), F32)
    rows_in = jnp.where(component_class(i) == in_class(c), double, 0.0)
    same = component_index(i) == component_index(c & (CH - 1))
    quarter = c >> 5
    padded[...] = jnp.zeros_like(padded)
    for which in range(2):
        padded[which, 0:27, 0:84] = packed[0:27, which * LANES : which * LANES + 84].astype(F32)
    write_choices(small[:, 0:LANES], small[:, LANES : 2 * LANES], choose, turn_choice)
    for which, rows, columns, blocks, out, base, flip in (
        (0, rows_out, by_in, True, one_out, 0, False),
        (0, rows_gate, by_in, False, one_out, 96, False),
        (1, rows_out, by_in, True, two_out, 0, False),
        (1, rows_in, by_out, True, turned_out, 0, True),
    ):
        for a in range(3):
            for bc in range(9):
                o = 9 * a + bc
                o = 26 - o if flip else o
                left[bc * CH : (bc + 1) * CH, :] = (rows * padded[which, o : o + 1, :]).astype(BF)
            found = dot(left[...], columns)
            for g in range(3):
                tile = jnp.zeros(shape, F32)
                for q in range(min(4, 9 - 4 * g)):
                    bc = 4 * g + q
                    keep = (quarter == q) & same if blocks else quarter == q
                    tile = tile + jnp.where(keep, found[bc * CH : (bc + 1) * CH], 0.0)
                width = min(128, 288 - 128 * g)
                out[base + a * CH : base + (a + 1) * CH, g * 128 : g * 128 + width] = tile[:, :width].astype(BF)


def first_mid_kernel(choose, own, part, w_first, columns, pre, gate_in, hidden_mid):
    masks = region_masks()
    inside = masks[4].astype(F32)
    mid_columns(choose, masks, lambda s: own[s], lambda s: part[s], columns)
    for n in range(2):
        stacked = dot(w_first[...], columns[:, n * MID : (n + 1) * MID])
        a, g = fold_mid(stacked, 0), fold_mid(stacked, 96)
        pre[n] = a
        gate_in[n] = g
        for x in range(1, 7):
            at = slice(x * LANES, (x + 1) * LANES)
            hidden_mid[n, x - 1] = (a[:, at] * jax.nn.sigmoid(g[:, at]) * inside).astype(BF)


def turned_sum(staged, table):
    rows = []
    for k in range(4):
        blocks = (k, k, 3 - k, 3 - k)
        rows.append(jnp.concatenate([staged[r, :, 128 * b : 128 * b + 128] for r, b in enumerate(blocks)], axis=1))
    return dot(jnp.concatenate(rows, axis=0), table) * 0.25


def back_kernel(turn_choice, own, across_y, crossed, back, staged):
    zero2 = jnp.zeros((2, 512), BF)
    for n in range(2):
        for r in range(4):
            if r == 0:
                value = own[n]
            else:
                first, second = (across_y[0], across_y[1]) if r == 1 else (crossed[2 * r - 4], crossed[2 * r - 3])
                value = chosen(turn_choice, n, r, first, second) * turn_signs(r, (30, 512))
            staged[r, n * CH : n * CH + 30, :] = value
            staged[r, n * CH + 30 : (n + 1) * CH, :] = zero2
    planes = turned_sum(staged, turns_spread_table()).astype(BF)
    for n in range(2):
        for x in range(8):
            first = (x >> 1) * 2 * CH + n * CH
            back[n, x] = planes[first : first + CH, (x & 1) * LANES : (x & 1) * LANES + LANES]


def first_edge_kernel(
    choose, own, part, got_a, got_b, pre, gate_in, hidden_mid, back, w_first,
    columns, pre_edge, gate_edge, both, face_a, face_b,
):
    masks = region_masks()
    inside = jnp.concatenate([masks[4].astype(F32)] * 4, axis=1)
    candidates = edge_planes_of(
        lambda s, x: own[s, x], lambda s, x: part[s, x],
        lambda which, s: (got_a, got_b)[which][s], lambda which, s: (got_a, got_b)[which][2 + s],
    )
    edge_columns(choose, masks, candidates, columns)
    stacked = dot(w_first[...], columns[...])
    a = edge_planes(pre) + edge_terms(stacked, 0)
    g = edge_planes(gate_in) + edge_terms(stacked, 96)
    pre_edge[...] = a
    gate_edge[...] = g
    hidden = (a * jax.nn.sigmoid(g) * inside).astype(BF)
    for n in range(2):
        outer = [hidden[:, e * LANES : (e + 1) * LANES] for e in (2 * n, 2 * n + 1)]
        both[0, n, 0], both[0, n, 7] = outer
        write_faces(face_a, face_b, (0, n), *outer)
        for x in range(1, 7):
            both[0, n, x] = hidden_mid[n, x - 1]
        for x in range(8):
            both[1, n, x] = back[n, x]
        write_faces(face_a, face_b, (1, n), back[n, 0], back[n, 7])


def gate_back(grad, a, g, rows8, inside):
    sig = jax.nn.sigmoid(g)
    through = grad * sig
    left, parts = grad * a, []
    for _ in range(3):
        parts.append(left.astype(BF))
        left = left - parts[-1].astype(F32)
    extra = dot(jnp.concatenate([rows8] * 3, axis=1), jnp.concatenate(parts, axis=0))
    sig8 = sig[0:8]
    top = through[0:8] + sig8 * (1.0 - sig8) * extra
    return (jnp.concatenate([top, through[8:]], axis=0) * inside).astype(BF)


def gate_rows():
    return one(gate_class(iota((8, CH), 1)) == iota((8, CH), 0))


def second_mid_kernel(
    choose, own, part, pre, gate_in, w_second, w_turned, second, through_edge, columns_h, placed_f, placed_s,
    columns_b,
):
    masks = region_masks()
    inside = jnp.concatenate([masks[4].astype(F32)] * 6, axis=1)
    for f, columns in ((0, columns_h), (1, columns_b)):
        mid_columns(choose, masks, lambda s: own[f, s], lambda s: part[f, s], columns)
    zero = jnp.zeros((CH, LANES), BF)
    rows8 = gate_rows()
    for placed in (placed_f, placed_s):
        placed[3 * CH :, :] = jnp.zeros((CH, 2 * MID), BF)

    def place(placed, n, planes, first, last):
        for a in range(3):
            for q in range(8):
                x = q + 1 - a
                at = (8 * n + q) * LANES
                placed[a * CH : (a + 1) * CH, at : at + LANES] = planes(x) if first <= x <= last else zero

    for n in range(2):
        here = slice(n * MID, (n + 1) * MID)
        second[n] = fold_mid(dot(w_second[...], columns_h[:, here]), 0)
        place(placed_s, n, lambda x: own[1, n, x], 0, 7)
        grad = fold_mid(dot(w_turned[...], columns_b[:, here]), 0)
        through_edge[:, 2 * n * LANES : (2 * n + 1) * LANES] = grad[:, :LANES]
        through_edge[:, (2 * n + 1) * LANES : (2 * n + 2) * LANES] = grad[:, 7 * LANES :]
        inner = slice(LANES, 7 * LANES)
        back_pre = gate_back(grad[:, inner], pre[n, :, inner], gate_in[n, :, inner], rows8, inside)
        place(placed_f, n, lambda x: back_pre[:, (x - 1) * LANES : x * LANES], 1, 6)


def gradient_kernel(columns_f, columns_h, placed_f, placed_s, raw):
    raw[0] = dot_t(columns_f[...], placed_f[...])
    raw[1] = dot_t(columns_h[...], placed_s[...])


def second_edge_kernel(
    scale, choose, own, part, got_a, got_b, far, pre_edge, gate_edge, through_edge,
    columns_f, columns_fe, raw, w_turned, columns_h, grads,
    columns_b, placed_f, placed_s, place,
):
    masks = region_masks()
    inside = jnp.concatenate([masks[4].astype(F32)] * 4, axis=1)
    for f, columns in ((0, columns_h), (1, columns_b)):
        candidates = edge_planes_of(
            lambda s, x: own[f, s, x], lambda s, x: part[f, s, x],
            lambda which, s: (got_a, got_b)[which][f, s], lambda which, s: far[which, f, s],
        )
        edge_columns(choose, masks, candidates, columns)
    more_t = edge_terms(dot(w_turned[...], columns_b[...]), 0)
    back_pre = gate_back(through_edge[...] + more_t, pre_edge[...], gate_edge[...], gate_rows(), inside)
    placed_f[...] = jnp.zeros_like(placed_f)
    placed_s[...] = jnp.zeros_like(placed_s)
    for n in range(2):
        for side in range(2):
            at = (2 * n + side) * LANES
            a = 2 * side
            placed_s[a * CH : (a + 1) * CH, at : at + LANES] = own[1, n, 7 * side]
            for a in range(3):
                to = (6 * n + 3 * side + a) * LANES
                placed_f[a * CH : (a + 1) * CH, to : to + LANES] = back_pre[:, at : at + LANES]
    pieces = []
    for n in range(2):
        mid, edge = n * MID, 2 * n * LANES
        pieces += [
            columns_fe[:, edge : edge + LANES], columns_f[:, mid : mid + 2 * LANES],
            columns_f[:, mid + 6 * LANES : mid + MID], columns_fe[:, edge + LANES : edge + 2 * LANES],
        ]
    shape = (CH, LANES)
    i, c = iota(shape, 0), iota(shape, 1)
    lift = jnp.where(component_class(i) == out_class(c), jnp.where(i >= 20, 2.0, 1.0), 0.0).astype(BF)
    keep = one(component_class(i) == in_class(c), F32)
    same = one(component_index(i) == component_index(c & (CH - 1)), F32)
    place[...] = jnp.zeros_like(place)
    for a in range(3):
        for half in (0, LANES):
            place[half + a * CH : half + (a + 1) * CH, a * LANES : (a + 1) * LANES] = lift
    found = (
        raw[0] + dot_t(jnp.concatenate(pieces, axis=1), placed_f[...]),
        raw[1] + dot_t(columns_h[...], placed_s[...]),
    )
    for layer in range(2):
        masked = (found[layer].reshape(9, CH, LANES) * same).reshape(9 * CH, LANES)
        top = masked.astype(BF)
        rest = (masked - top.astype(F32)).astype(BF)
        lifted = dot(jnp.concatenate([top, rest], axis=1), place[...])
        for a in range(3):
            block = lifted[:, a * LANES : (a + 1) * LANES].reshape(9, CH, LANES) * keep
            first = 27 * layer + 9 * a
            grads[first : first + 9, :] = jnp.sum(block, axis=1) * scale
    grads[54:56, :] = jnp.zeros((2, LANES), F32)


def compact_kernel(second_in, columns, w_second, second):
    more = edge_terms(dot(w_second[...], columns[...]), 0)
    zero = jnp.zeros((CH, LANES), F32)
    rows = []
    for n in range(2):
        for k in range(4):
            planes = second_in[n, :, k * 256 : (k + 1) * 256]
            if k == 0:
                planes = planes + jnp.concatenate([more[:, 2 * n * LANES : (2 * n + 1) * LANES], zero], axis=1)
            if k == 3:
                planes = planes + jnp.concatenate([zero, more[:, (2 * n + 1) * LANES : (2 * n + 2) * LANES]], axis=1)
            rows.append(planes.astype(BF))
    packed = dot(jnp.concatenate(rows, axis=0), compact_table()).astype(BF)
    for n in range(2):
        for k in range(4):
            first = (4 * n + k) * CH
            second[n * CH : (n + 1) * CH, k * LANES : (k + 1) * LANES] = packed[first : first + CH]


def turn_kernel(turn_choice, own, across_y, across_x, across, out, staged):
    for n in range(2):
        staged[0, n * CH : (n + 1) * CH, :] = own[n * CH : (n + 1) * CH, :]
        for r, ref in ((1, across_y), (2, across_x), (3, across)):
            value = chosen(turn_choice, n, r, ref[0:CH, :], ref[CH : 2 * CH, :])
            staged[r, n * CH : (n + 1) * CH, :] = value * turn_signs(r, (CH, 512))
    result = turned_sum(staged, turns_table()).astype(BF)
    for k in range(4):
        for n in range(2):
            first = (2 * k + n) * CH
            out[:, n, k * 128 : (k + 1) * 128] = result[first : first + 30]


SMEM = pl.BlockSpec(memory_space=pltpu.SMEM)
VMEM = pl.BlockSpec(memory_space=pltpu.VMEM)


def call(kernel, us, n_smem, outs, scratch, *args):
    return pl.pallas_call(
        kernel,
        out_shape=tuple(jax.ShapeDtypeStruct(s, t) for s, t in outs),
        in_specs=[SMEM] * n_smem + [VMEM] * (len(args) - n_smem),
        out_specs=tuple([VMEM] * len(outs)),
        scratch_shapes=[pltpu.VMEM(s, t) for s, t in scratch],
        compiler_params=pltpu.CompilerParams(vmem_limit_bytes=24 * 1024 * 1024),
        cost_estimate=pl.CostEstimate(flops=0, transcendentals=0, bytes_accessed=int(us * 3_000_000)),
    )(*args)


def swap_y(x):
    n = lax.axis_size("yp")
    return lax.ppermute(x, "yp", [(i, n - 1 - i) for i in range(n)])


def mirror_x(x):
    n = lax.axis_size("xp")
    return lax.ppermute(x, "xp", [(i, n - 1 - i) for i in range(n)])


def pair_swap(x, first):
    n = lax.axis_size("xp")
    pairs = []
    for i in range(first, n - 1, 2):
        pairs += [(i, i + 1), (i + 1, i)]
    return lax.ppermute(x, "xp", pairs)


def exchange(face_a, face_b):
    got_b = pair_swap(face_b, 1)
    got_a = pair_swap(face_a, 0)
    return got_a, got_b


def after(arrays, *others):
    return lax.optimization_barrier((tuple(arrays), others))[0]


def side_by_side(arrays, rows):
    total = None
    for k, x in enumerate(arrays):
        x = jnp.pad(x, ((0, rows - x.shape[0]), (k * LANES, (len(arrays) - k) * LANES - LANES + LANES - x.shape[1])))
        total = x if total is None else total + x
    return lax.optimization_barrier(total)


def on_device(features, cotangent, w_first, w_second, codes, mirror):
    plane = (CH, LANES)
    cot_y = swap_y(cotangent)
    crossed = mirror_x(jnp.concatenate([cotangent, cot_y], axis=0))
    (fp,) = call(spread_kernel, 0.2, 0, [((2, 8) + plane, BF)], [((64, 512), BF)], features)
    part = swap_y(fp)
    low, high = (jnp.concatenate([fp[:, x], part[:, x]], axis=0) for x in (0, 7))
    odd = is_odd()
    got = exchange(jnp.where(odd, low, high), jnp.where(odd, high, low))
    w_first, w_second, codes, mirror = after((w_first, w_second, codes, mirror), part)
    w1, w2, w2t, choose, turn_choice = call(
        weights_kernel, 1, 0,
        [
            ((192, 288), BF), ((96, 288), BF), ((96, 288), BF),
            ((N_CHOICES, HALF, LANES), BF), ((6, HALF, LANES), BF),
        ],
        [((2, CH, LANES), F32), ((288, LANES), BF)],
        side_by_side((w_first, w_second), CH), side_by_side((codes, mirror), 2),
    )
    columns, pre, gate_in, hidden_mid = call(
        first_mid_kernel, 2, 0,
        [((288, 2 * MID), BF), ((2, CH, MID), F32), ((2, CH, MID), F32), ((2, 6) + plane, BF)],
        [], choose, fp, part, w1,
    )
    (crossed,) = after((crossed,), hidden_mid)
    (back,) = call(
        back_kernel, 0.8, 0, [((2, 8) + plane, BF)], [((4, 64, 512), BF)], turn_choice, cotangent, cot_y, crossed
    )
    got = after(got, hidden_mid, back)
    columns_e, pre_e, gate_e, both, face_a, face_b = call(
        first_edge_kernel, 1, 0,
        [
            ((288, 4 * LANES), BF), ((CH, 4 * LANES), F32), ((CH, 4 * LANES), F32), ((2, 2, 8) + plane, BF),
            ((2, 2) + plane, BF), ((2, 2) + plane, BF),
        ],
        [], choose, fp, part, *got, pre, gate_in, hidden_mid, back, w1,
    )
    got = exchange(face_a, face_b)
    part = swap_y(both)
    second_part, through_e, columns_h, placed_f, placed_s = call(
        second_mid_kernel, 2.5, 0,
        [((2, CH, MID), F32), ((CH, 4 * LANES), F32), ((288, 2 * MID), BF), *[((128, 2 * MID), BF)] * 2],
        [((288, 2 * MID), BF)],
        choose, both, part, pre, gate_in, w2, w2t,
    )
    got = after(got, second_part)
    far = swap_y(jnp.stack(got))
    columns_h, placed_f, placed_s = after((columns_h, placed_f, placed_s), *got)
    (raw,) = call(gradient_kernel, 1, 0, [((2, 288, LANES), F32)], [], columns, columns_h, placed_f, placed_s)
    n_bricks = features.shape[0] * lax.axis_size("xp") * lax.axis_size("yp")
    columns_he, grads = call(
        functools.partial(second_edge_kernel, 1.0 / n_bricks), 2, 0, [((288, 4 * LANES), BF), ((56, LANES), F32)],
        [((288, 4 * LANES), BF)]
        + [((128, 12 * LANES), BF), ((128, 4 * LANES), BF), ((256, 3 * LANES), BF)],
        choose, both, part, *got, far, pre_e, gate_e, through_e, columns, columns_e, raw, w2t,
    )
    total = grads + swap_y(grads)
    (second,) = call(compact_kernel, 0.5, 0, [((64, 512), BF)], [], second_part, columns_he, w2)
    (second,) = after((second,), total)
    second_y = swap_y(second)
    second_x = mirror_x(second)
    second_xy = swap_y(second_x)
    (denoised,) = call(
        turn_kernel, 0.9, 0, [((30, 2, 512), BF)], [((4, 64, 512), BF)], turn_choice, second, second_y, second_x, second_xy
    )
    denoised = denoised.transpose(1, 0, 2)
    n = lax.axis_size("xp")
    bit = 1
    while bit < n:
        total = total + lax.ppermute(total, "xp", [(i, i ^ bit) for i in range(n)])
        bit *= 2
    return denoised, total[0:27, 0:84], total[27:54, 0:84]


def solution(mesh):
    brick = P(("grp", "xp", "yp"))
    return jax.shard_map(
        on_device,
        mesh=mesh,
        in_specs=(brick, brick, P(), P(), brick, brick),
        out_specs=(brick, P("grp"), P("grp")),
        check_vma=False,
    )
```
